128 devices in a mesh: slab: 16 (over y, x_lo, core), lat: 8 (over x_hi, z).
Axes of the slice: x: 4 (x_hi: 2, x_lo: 2; x = x_hi * 2 + x_lo), y: 4, z: 4, core: 2. Of those that a mesh axis runs over, the one named last changes fastest.
Arguments:
- nodes: bfloat16 [16384, 512], P('slab', 'lat')
- edges: bfloat16 [65536, 512], P(('slab', 'lat'))
- edge_tiles: int32 [2, 512], P(None, ('slab', 'lat')), may hold values from 0 to 11, as said below
- edge_offsets: int32 [2, 65536], P(None, ('slab', 'lat')), may hold values from 0 to 127
- tile_counts: int32 [16], P('slab'), may hold values from 10 to 32, as said below
- halo_blocks: int32 [16, 2, 2], P('slab'), may hold values from 0 to 7
- w_edge_in: bfloat16 [1536, 512], P(('slab', 'lat')), may hold values from -0.15625 to 0.15625
- w_edge_out: bfloat16 [512, 512], P(('slab', 'lat'))
- w_node_in: bfloat16 [1024, 512], P(('slab', 'lat')), may hold values from -0.1875 to 0.1875
- w_node_out: bfloat16 [512, 512], P(('slab', 'lat'))
- edge_gain: float32 [512], replicated, may hold values from 0.1 to 1.9
- node_gain: float32 [512], replicated, may hold values from 0.1 to 1.9
- node_cotangent: bfloat16 [16384, 512], P('slab', 'lat'), may hold values from -6 to 6
- edge_cotangent: bfloat16 [65536, 512], P(('slab', 'lat')), may hold values from -6 to 6
Outputs:
- new_nodes: bfloat16 [16384, 512], P('slab', 'lat')
- new_edges: bfloat16 [65536, 512], P(('slab', 'lat'))
- grad_nodes: bfloat16 [16384, 512], P('slab', 'lat')
- grad_edges: bfloat16 [65536, 512], P(('slab', 'lat'))
- grad_edge_in: float32 [1536, 512], P(('slab', 'lat'))
- grad_edge_out: float32 [512, 512], P(('slab', 'lat'))
- grad_node_in: float32 [1024, 512], P(('slab', 'lat'))
- grad_node_out: float32 [512, 512], P(('slab', 'lat'))
The draws below stay inside these ranges and needn't reach their ends.
Inputs may be any that keep to these rules, and one draw needn't show every extreme that they name: `edge_tiles`: row 0 names each tile's receiver block among its slab's 8 blocks; row 1 its sender block among the 12 blocks of the extended slab (2 received from below, the slab's own, 2 received from above). Tiles of the first slab never name the blocks from below, tiles of the last slab never those from above. `tile_counts`: live tiles are the first ones of the slab's 32 slots; in every draw some slab has all slots live.
All inputs are finite; a program needn't handle non-finite values.
Results may differ from the reference program's by a relative error of at most 0.03.
The reference program's roundings to bfloat16 on the way count: a program that leaves them out, or rounds other values in their place, can miss the bound.
Values may be sent and summed in bfloat16 or wider, within the bound.
No kernel may reach another device: no remote copies, remote signals or barrier semaphores. Data moves between devices by JAX's collectives and lax.ppermute only.
A program may use at most 64 MiB of HBM per device.

```python
import math
import jax
import jax.numpy as jnp
from jax import lax

L = 512
HID = 512
BLK = 128
HB = 2
NB_SLAB = 8
XB = 12
TILES_SLAB = 32
TILES = 512
EDGES = 65536
NODES = 16384
N_SLAB = 16


def row_scaled(key, row_count, col_count):
    first_key, second_key = jax.random.split(key, 2)
    row_scale = jnp.exp(jax.random.uniform(second_key, (row_count, 1), jnp.float32, math.log(0.3), math.log(3.0)))
    return jax.random.normal(first_key, (row_count, col_count), jnp.float32) * row_scale


def column_scaled(key, row_count, col_count):
    first_key, second_key = jax.random.split(key, 2)
    col_scale = jnp.exp(jax.random.uniform(second_key, (1, col_count), jnp.float32, math.log(0.3), math.log(3.0)))
    base = jax.random.normal(first_key, (row_count, col_count), jnp.float32)
    return base * col_scale / math.sqrt(row_count)


def draw_nodes(key, part):
    return row_scaled(jax.random.fold_in(key, 11), NODES, L).astype(jnp.bfloat16)


def draw_edges(key, part):
    return row_scaled(jax.random.fold_in(key, 12), EDGES, L).astype(jnp.bfloat16)


def draw_w_edge_out(key, part):
    return column_scaled(jax.random.fold_in(key, 13), HID, L).astype(jnp.bfloat16)


def draw_w_node_out(key, part):
    return column_scaled(jax.random.fold_in(key, 14), HID, L).astype(jnp.bfloat16)


def draw_edge_tiles(key, part):
    first_key, second_key = jax.random.split(jax.random.fold_in(key, 21), 2)
    slab_of = jnp.arange(TILES, dtype=jnp.int32) // TILES_SLAB
    receiver = jax.random.randint(first_key, (TILES,), 0, NB_SLAB, dtype=jnp.int32)
    lowest = jnp.where(slab_of == 0, HB, 0).astype(jnp.int32)
    highest = jnp.where(slab_of == N_SLAB - 1, HB + NB_SLAB, XB).astype(jnp.int32)
    sender = jax.random.randint(second_key, (TILES,), lowest, highest, dtype=jnp.int32)
    return jnp.stack([receiver, sender]).astype(jnp.int32)


def draw_tile_counts(key, part):
    first_key, second_key = jax.random.split(jax.random.fold_in(key, 31), 2)
    counts = jax.random.randint(first_key, (N_SLAB,), TILES_SLAB // 3, TILES_SLAB + 1, dtype=jnp.int32)
    chosen = jax.random.randint(second_key, (), 0, N_SLAB, dtype=jnp.int32)
    return counts.at[chosen].set(TILES_SLAB).astype(jnp.int32)


def with_ends(values, own_key, low, largest):
    longest = values.shape.index(max(values.shape))
    spots = []
    for shift in (0, 1):
        where = [jax.random.randint(jax.random.fold_in(own_key, axis), (), 0, length) for axis, length in enumerate(values.shape)]
        where[longest] = (where[longest] + shift) % values.shape[longest]
        spots.append(tuple(where))
    return values.at[spots[0]].set(low).at[spots[1]].set(largest)


def levels(key, shape, cuts, least, largest):
    def one(position, shards_of):
        steps = jax.random.uniform(jax.random.fold_in(jax.random.fold_in(key, 6), position), (shards_of,), jnp.float32, least / len(cuts), largest / len(cuts))
        return jnp.repeat(jnp.exp(steps), shape[position] // shards_of).reshape((-1,) + (1,) * (len(shape) - position - 1))

    loudness = one(*cuts[0])
    for cut in cuts[1:]:
        loudness = loudness * one(*cut)
    return loudness


def normal_values(stream_key, extent, scale, reach, shards=(), held_as=jnp.bfloat16):
    loudness = levels(stream_key, extent, shards, -0.22, 0.18) if shards else 1.0
    array = jax.random.normal(stream_key, extent, jnp.float32) * scale * loudness
    return jnp.minimum(jnp.maximum(array, -reach), reach).astype(held_as)


def setup_inputs(seed: int = 0) -> dict:
    splits = jax.random.split(jax.random.key(seed), 15)
    return {
        "nodes": draw_nodes(jax.random.fold_in(splits[14], 71), 0),
        "edges": draw_edges(jax.random.fold_in(splits[14], 71), 0),
        "edge_tiles": draw_edge_tiles(jax.random.fold_in(splits[14], 71), 0),
        "edge_offsets": with_ends(jax.random.randint(splits[3], (2, EDGES), 0, BLK), jax.random.fold_in(splits[3], 1), 0, BLK - 1).astype(jnp.int32),
        "tile_counts": draw_tile_counts(jax.random.fold_in(splits[14], 71), 0),
        "halo_blocks": with_ends(jax.random.randint(splits[5], (N_SLAB, 2, HB), 0, NB_SLAB), jax.random.fold_in(splits[5], 1), 0, NB_SLAB - 1).astype(jnp.int32),
        "w_edge_in": normal_values(splits[6], (3 * L, HID), (3 * L) ** -0.5, 0.15625, ((0, 128),)),
        "w_edge_out": draw_w_edge_out(jax.random.fold_in(splits[14], 71), 0),
        "w_node_in": normal_values(splits[8], (2 * L, HID), (2 * L) ** -0.5, 0.1875, ((0, 128),)),
        "w_node_out": draw_w_node_out(jax.random.fold_in(splits[14], 71), 0),
        "edge_gain": jnp.clip(1.0 + 0.18 * jax.random.normal(splits[10], (L,), jnp.float32), 0.1, 1.9),
        "node_gain": jnp.clip(1.0 + 0.18 * jax.random.normal(splits[11], (L,), jnp.float32), 0.1, 1.9),
        "node_cotangent": normal_values(splits[12], (NODES, L), 1.0, 6.0, ((0, 16), (1, 8))),
        "edge_cotangent": normal_values(splits[13], (EDGES, L), 1.0, 6.0, ((0, 128),)),
    }


EPSILON = 1e-05

def layer_norm(values, gain_vector):
    average = lax.optimization_barrier(jnp.mean(values, axis=-1, keepdims=True))
    centred = values - average
    variance = lax.optimization_barrier(jnp.mean(centred * centred, axis=-1, keepdims=True))
    inverse = lax.rsqrt(variance + EPSILON)
    normed = centred * inverse
    return (normed * gain_vector, normed, inverse)

def norm_back(upstream, normed, inverse, gain_vector):
    scaled = upstream * gain_vector
    return inverse * (scaled - lax.optimization_barrier(jnp.mean(scaled, axis=-1, keepdims=True)) - normed * lax.optimization_barrier(jnp.mean(scaled * normed, axis=-1, keepdims=True)))

def contract_rows(left, right):
    return lax.dot_general(left, right, (((0,), (0,)), ((), ())), preferred_element_type=jnp.float32)

def times_transpose(left, weight):
    return lax.dot_general(left, weight, (((1,), (1,)), ((), ())), preferred_element_type=jnp.float32)

def pick_blocks(source_table, blocks):
    width = source_table.shape[1]
    return jnp.take(source_table.reshape(-1, BLK, width), blocks, axis=0).reshape(-1, width)

def add_blocks(source_table, blocks, values):
    width = source_table.shape[1]
    shaped = source_table.reshape(-1, BLK, width).at[blocks].add(values.reshape(-1, BLK, width))
    return shaped.reshape(-1, width)

def reference(nodes, edges, edge_tiles, edge_offsets, tile_counts, halo_blocks, w_edge_in, w_edge_out, w_node_in, w_node_out, edge_gain, node_gain, node_cotangent, edge_cotangent):
    slab_rows = NB_SLAB * BLK
    halo_rows = HB * BLK
    slab_edges = TILES_SLAB * BLK
    latents = nodes.reshape(N_SLAB, slab_rows, L)
    to_upper = jax.vmap(pick_blocks)(latents, halo_blocks[:, 0])
    to_lower = jax.vmap(pick_blocks)(latents, halo_blocks[:, 1])
    blank_rows = jnp.zeros((1, halo_rows, L), nodes.dtype)
    from_lower = jnp.concatenate([blank_rows, to_upper[:-1]], axis=0)
    from_upper = jnp.concatenate([to_lower[1:], blank_rows], axis=0)
    extended_all = jnp.concatenate([from_lower, latents, from_upper], axis=1)
    slab_tiles = edge_tiles.reshape(2, N_SLAB, TILES_SLAB).transpose(1, 0, 2)
    slab_offsets = edge_offsets.reshape(2, N_SLAB, slab_edges).transpose(1, 0, 2)
    slab_edge_latents = edges.reshape(N_SLAB, slab_edges, L)
    slab_node_cot = node_cotangent.reshape(N_SLAB, slab_rows, L)
    slab_edge_cot = edge_cotangent.reshape(N_SLAB, slab_edges, L)

    def one_slab(totals, inputs):
        extended, tiles, offsets, count, edge_latents, node_cot, edge_cot = inputs
        slab_full = extended[halo_rows:halo_rows + slab_rows]
        tile_of = jnp.arange(slab_edges, dtype=jnp.int32) // BLK
        dst_row = tiles[0][tile_of] * BLK + offsets[0]
        src_row = tiles[1][tile_of] * BLK + offsets[1]
        live_mask = (tile_of < count).astype(jnp.float32)[:, None]
        joined = jnp.concatenate([edge_latents, extended[src_row], slab_full[dst_row]], axis=1)
        edge_first = jax.nn.relu(jnp.dot(joined, w_edge_in, preferred_element_type=jnp.float32)).astype(jnp.bfloat16)
        edge_second = jnp.dot(edge_first, w_edge_out, preferred_element_type=jnp.float32)
        edge_update, edge_normed, edge_inverse = layer_norm(edge_second, edge_gain)
        message = edge_update * live_mask
        new_edge_rows = (edge_latents.astype(jnp.float32) + message).astype(jnp.bfloat16)
        summed = jnp.zeros((slab_rows, L), jnp.float32).at[dst_row].add(message)
        aggregated = summed.astype(jnp.bfloat16)
        node_joined = jnp.concatenate([slab_full, aggregated], axis=1)
        node_first = jax.nn.relu(jnp.dot(node_joined, w_node_in, preferred_element_type=jnp.float32)).astype(jnp.bfloat16)
        node_second = jnp.dot(node_first, w_node_out, preferred_element_type=jnp.float32)
        node_update, node_normed, node_inverse = layer_norm(node_second, node_gain)
        new_rows = (slab_full.astype(jnp.float32) + node_update).astype(jnp.bfloat16)
        d_node_second = norm_back(node_cot.astype(jnp.float32), node_normed, node_inverse, node_gain).astype(jnp.bfloat16)
        g_node_out = contract_rows(node_first, d_node_second)
        d_node_first = (times_transpose(d_node_second, w_node_out) * (node_first > 0)).astype(jnp.bfloat16)
        g_node_in = contract_rows(node_joined, d_node_first)
        d_node_joined = times_transpose(d_node_first, w_node_in)
        d_direct = d_node_joined[:, :L]
        d_aggregated = d_node_joined[:, L:].astype(jnp.bfloat16)
        edge_upstream = edge_cot.astype(jnp.float32)
        d_message = (edge_upstream + d_aggregated[dst_row].astype(jnp.float32)) * live_mask
        d_edge_second = norm_back(d_message, edge_normed, edge_inverse, edge_gain).astype(jnp.bfloat16)
        g_edge_out = contract_rows(edge_first, d_edge_second)
        d_edge_first = (times_transpose(d_edge_second, w_edge_out) * (edge_first > 0)).astype(jnp.bfloat16)
        g_edge_in = contract_rows(joined, d_edge_first)
        d_joined = times_transpose(d_edge_first, w_edge_in)
        grad_edge_rows = (edge_upstream + d_joined[:, :L]).astype(jnp.bfloat16)
        d_extended = jnp.zeros((XB * BLK, L), jnp.float32)
        d_extended = d_extended.at[src_row].add(d_joined[:, L:2 * L])
        d_extended = d_extended.at[halo_rows + dst_row].add(d_joined[:, 2 * L:])
        d_extended = d_extended.at[halo_rows:halo_rows + slab_rows].add(d_direct)
        totals = (totals[0] + g_edge_in, totals[1] + g_edge_out, totals[2] + g_node_in, totals[3] + g_node_out)
        return (totals, (new_rows, new_edge_rows, grad_edge_rows, d_extended))
    start_totals = (jnp.zeros((3 * L, HID), jnp.float32), jnp.zeros((HID, L), jnp.float32), jnp.zeros((2 * L, HID), jnp.float32), jnp.zeros((HID, L), jnp.float32))
    totals, outputs = lax.scan(one_slab, start_totals, (extended_all, slab_tiles, slab_offsets, tile_counts, slab_edge_latents, slab_node_cot, slab_edge_cot))
    new_rows, new_edge_rows, grad_edge_rows, d_extended = outputs
    d_lower = d_extended[:, :halo_rows]
    d_middle = d_extended[:, halo_rows:halo_rows + slab_rows]
    d_upper = d_extended[:, halo_rows + slab_rows:]
    blank_grad = jnp.zeros((1, halo_rows, L), jnp.float32)
    from_above = jnp.concatenate([d_lower[1:], blank_grad], axis=0)
    from_below = jnp.concatenate([blank_grad, d_upper[:-1]], axis=0)
    grad_slabs = jax.vmap(add_blocks)(d_middle, halo_blocks[:, 0], from_above)
    grad_slabs = jax.vmap(add_blocks)(grad_slabs, halo_blocks[:, 1], from_below)
    return (new_rows.reshape(NODES, L), new_edge_rows.reshape(EDGES, L), grad_slabs.astype(jnp.bfloat16).reshape(NODES, L), grad_edge_rows.reshape(EDGES, L), totals[0], totals[1], totals[2], totals[3])
```

```python
import jax
import jax.numpy as jnp
from jax import lax
from jax.sharding import Mesh, PartitionSpec as P

L = 512
BLK = 128
HB = 2
EPSILON = 1e-05

SLAB = ("y", "xl", "c")
LAT = ("xh", "z")
CHIP = ("y", "xl", "xh", "z")
BF = jnp.bfloat16
F32 = jnp.float32


def from_behind(value, steps):
    count = lax.axis_size(SLAB)
    first, last = (max(0, -steps), min(count, count - steps))
    return lax.ppermute(value, SLAB, [(source, source + steps) for source in range(first, last)])


def layer_norm(values, gain_vector):
    average = jnp.mean(values, axis=-1, keepdims=True)
    centred = values - average
    variance = jnp.mean(centred * centred, axis=-1, keepdims=True)
    inverse = lax.rsqrt(variance + EPSILON)
    normed = centred * inverse
    return (normed * gain_vector, normed, inverse)


def norm_back(upstream, normed, inverse, gain_vector):
    scaled = upstream * gain_vector
    return inverse * (
        scaled
        - jnp.mean(scaled, axis=-1, keepdims=True)
        - normed * jnp.mean(scaled * normed, axis=-1, keepdims=True)
    )


def contract_rows(left, right):
    return lax.dot_general(left, right, (((0,), (0,)), ((), ())), preferred_element_type=F32)


def times_transpose(left, weight):
    return lax.dot_general(left, weight, (((1,), (1,)), ((), ())), preferred_element_type=F32)


def pick_blocks(source_table, blocks):
    width = source_table.shape[1]
    return jnp.take(source_table.reshape(-1, BLK, width), blocks, axis=0).reshape(-1, width)


def pair(value):
    half = value.shape[-2] // 2
    return jnp.concatenate([value[..., :half, :], value[..., half:, :]], axis=-1)


def unpair(value):
    half = value.shape[-1] // 2
    return jnp.concatenate([value[..., :half], value[..., half:]], axis=-2)


def gather_weights(pieces):
    rows = sum(piece.shape[0] for piece in pieces)
    packed = jnp.concatenate(pieces + [jnp.zeros((-rows % 8, L), BF)], axis=0)
    chips = lax.axis_size(CHIP)
    core = lax.axis_index("c")
    mine = lax.all_to_all(jnp.broadcast_to(packed, (chips,) + packed.shape), CHIP, 0, 0)
    theirs = lax.ppermute(mine, "c", [(0, 1), (1, 0)])
    lat = lax.axis_size(LAT)
    shape = (chips // lat, 1, lat) + packed.shape
    mine, theirs = mine.reshape(shape), theirs.reshape(shape)
    first = jnp.where(core == 0, mine, theirs)
    second = jnp.where(core == 0, theirs, mine)
    full = jnp.concatenate([first, second], axis=1).reshape((2 * chips,) + packed.shape)
    out, at = [], 0
    for piece in pieces:
        count = piece.shape[0]
        out.append(full[:, at : at + count].reshape(-1, L))
        at += count
    return out


def scatter_grads(grads):
    chips = lax.axis_size(CHIP)
    lat = lax.axis_size(LAT)
    core = lax.axis_index("c")
    parts = [grad.reshape(2 * chips, -1, L) for grad in grads]
    counts = [part.shape[1] for part in parts]
    packed = jnp.concatenate(parts, axis=1)
    rows = packed.shape[1]
    shaped = packed.reshape(chips // lat, 2, lat, rows, L)
    kept = jnp.where(core == 0, shaped[:, 0], shaped[:, 1])
    sent = jnp.where(core == 0, shaped[:, 1], shaped[:, 0]).astype(BF)
    arrived = lax.ppermute(sent, "c", [(0, 1), (1, 0)])
    summed = (kept + arrived.astype(F32)).astype(BF).reshape(chips, rows, L)
    summed = jnp.pad(summed, ((0, 0), (0, -rows % 8), (0, 0)))
    spread = lax.all_to_all(summed, CHIP, 0, 0)
    total = jnp.sum(spread.astype(F32), axis=0)
    out, at = [], 0
    for count in counts:
        out.append(total[at : at + count])
        at += count
    return out


def per_device(
    nodes,
    edges,
    edge_tiles,
    edge_offsets,
    tile_counts,
    halo_blocks,
    w_edge_in,
    w_edge_out,
    w_node_in,
    w_node_out,
    edge_gain,
    node_gain,
    node_cotangent,
    edge_cotangent,
):
    lat_size = lax.axis_size(LAT)
    lat_index = lax.axis_index(LAT)
    slab_rows, width = nodes.shape
    own_rows = slab_rows // lat_size
    halo_rows = HB * BLK
    ext_rows = slab_rows + 2 * halo_rows
    up_list = halo_blocks[0, 0]
    down_list = halo_blocks[0, 1]

    from_lower = unpair(from_behind(pair(pick_blocks(nodes, up_list)), 1))
    from_upper = unpair(from_behind(pair(pick_blocks(nodes, down_list)), -1))
    table = pair(jnp.concatenate([from_lower, nodes, from_upper], axis=0))
    cot = pair(node_cotangent.reshape(lat_size, own_rows, width))
    message_out = jnp.concatenate(
        [jnp.broadcast_to(table, (lat_size,) + table.shape), cot], axis=1
    )
    arrived = lax.all_to_all(message_out, LAT, 0, 0)
    extended = unpair(arrived[:, : ext_rows // 2]).transpose(1, 0, 2).reshape(ext_rows, L)
    upstream_rows = unpair(arrived[:, ext_rows // 2 :]).transpose(1, 0, 2).reshape(own_rows, L)
    slab_full = extended[halo_rows : halo_rows + slab_rows]

    edge_in, edge_out, node_in, node_out = gather_weights(
        [w_edge_in, w_edge_out, w_node_in, w_node_out]
    )

    tile_slots = edge_tiles.shape[1]
    tile_of = jnp.arange(edges.shape[0], dtype=jnp.int32) // BLK
    dst_row = edge_tiles[0][tile_of] * BLK + edge_offsets[0]
    src_row = edge_tiles[1][tile_of] * BLK + edge_offsets[1]
    live_mask = (lat_index * tile_slots + tile_of < tile_counts[0]).astype(F32)[:, None]
    joined = jnp.concatenate([edges, extended[src_row], slab_full[dst_row]], axis=1)
    edge_first = jax.nn.relu(jnp.dot(joined, edge_in, preferred_element_type=F32)).astype(BF)
    edge_second = jnp.dot(edge_first, edge_out, preferred_element_type=F32)
    edge_update, edge_normed, edge_inverse = layer_norm(edge_second, edge_gain)
    message = edge_update * live_mask
    new_edges = (edges.astype(F32) + message).astype(BF)
    partial_sums = jnp.zeros((slab_rows, L), F32).at[dst_row].add(message)
    spread = lax.all_to_all(partial_sums.reshape(lat_size, own_rows, L), LAT, 0, 0)
    aggregated = jnp.sum(spread, axis=0).astype(BF)
    row_start = lat_index * own_rows
    own_latents = lax.dynamic_slice_in_dim(slab_full, row_start, own_rows, 0)
    node_joined = jnp.concatenate([own_latents, aggregated], axis=1)
    node_first = jax.nn.relu(jnp.dot(node_joined, node_in, preferred_element_type=F32)).astype(BF)
    node_second = jnp.dot(node_first, node_out, preferred_element_type=F32)
    node_update, node_normed, node_inverse = layer_norm(node_second, node_gain)
    new_rows = (own_latents.astype(F32) + node_update).astype(BF)

    d_node_second = norm_back(
        upstream_rows.astype(F32), node_normed, node_inverse, node_gain
    ).astype(BF)
    g_node_out = contract_rows(node_first, d_node_second)
    d_node_first = (times_transpose(d_node_second, node_out) * (node_first > 0)).astype(BF)
    g_node_in = contract_rows(node_joined, d_node_first)
    d_node_joined = times_transpose(d_node_first, node_in)
    d_direct = d_node_joined[:, :L]
    d_aggregated = d_node_joined[:, L:].astype(BF)

    groups = L // width
    group_rows = own_rows // groups
    rows_out = (
        new_rows.reshape(groups, group_rows, lat_size, width)
        .transpose(2, 1, 0, 3)
        .reshape(lat_size, group_rows, L)
    )
    second_out = jnp.concatenate(
        [jnp.broadcast_to(d_aggregated, (lat_size,) + d_aggregated.shape), rows_out], axis=1
    )
    second_in = lax.all_to_all(second_out, LAT, 0, 0)
    d_agg_slab = second_in[:, :own_rows].reshape(slab_rows, L)
    new_nodes = (
        second_in[:, own_rows:]
        .reshape(lat_size, group_rows, groups, width)
        .transpose(0, 2, 1, 3)
        .reshape(slab_rows, width)
    )

    edge_upstream = edge_cotangent.astype(F32)
    d_message = (edge_upstream + d_agg_slab[dst_row].astype(F32)) * live_mask
    d_edge_second = norm_back(d_message, edge_normed, edge_inverse, edge_gain).astype(BF)
    g_edge_out = contract_rows(edge_first, d_edge_second)
    d_edge_first = (times_transpose(d_edge_second, edge_out) * (edge_first > 0)).astype(BF)
    g_edge_in = contract_rows(joined, d_edge_first)
    d_joined = times_transpose(d_edge_first, edge_in)
    grad_edges = (edge_upstream + d_joined[:, :L]).astype(BF)
    d_extended = jnp.zeros((ext_rows, L), F32)
    d_extended = d_extended.at[src_row].add(d_joined[:, L : 2 * L])
    d_extended = d_extended.at[halo_rows + dst_row].add(d_joined[:, 2 * L :])
    own_start = halo_rows + row_start
    own_grads = lax.dynamic_slice_in_dim(d_extended, own_start, own_rows, 0) + d_direct
    d_extended = lax.dynamic_update_slice_in_dim(d_extended, own_grads, own_start, 0)

    columns = pair(d_extended.astype(BF).reshape(ext_rows, lat_size, width).transpose(1, 0, 2))
    summed = unpair(jnp.sum(lax.all_to_all(columns, LAT, 0, 0).astype(F32), axis=0))
    d_lower = pair(summed[:halo_rows].astype(BF))
    d_middle = summed[halo_rows : halo_rows + slab_rows]
    d_upper = pair(summed[halo_rows + slab_rows :].astype(BF))
    from_above = unpair(from_behind(d_lower, -1)).astype(F32).reshape(HB, BLK, width)
    from_below = unpair(from_behind(d_upper, 1)).astype(F32).reshape(HB, BLK, width)
    blocks = d_middle.reshape(-1, BLK, width)
    numbers = jnp.arange(blocks.shape[0])
    for j in range(HB):
        blocks = blocks + jnp.where((numbers == up_list[j])[:, None, None], from_above[j], 0.0)
        blocks = blocks + jnp.where((numbers == down_list[j])[:, None, None], from_below[j], 0.0)
    grad_slab = blocks.reshape(slab_rows, width).astype(BF)
    reduced = scatter_grads([g_edge_in, g_edge_out, g_node_in, g_node_out])
    return (new_nodes, new_edges, grad_slab, grad_edges) + tuple(reduced)


def solution(mesh):
    fine = Mesh(mesh.devices.reshape(4, 2, 2, 2, 4), ("y", "xl", "c", "xh", "z"))
    every = SLAB + LAT
    by_rows = P(every, None)
    split = P(SLAB, LAT)
    placed = (
        split,
        by_rows,
        P(None, every),
        P(None, every),
        P(SLAB),
        P(SLAB, None, None),
        by_rows,
        by_rows,
        by_rows,
        by_rows,
        P(),
        P(),
        split,
        by_rows,
    )
    return jax.shard_map(
        per_device,
        mesh=fine,
        in_specs=placed,
        out_specs=(split, by_rows, split, by_rows, by_rows, by_rows, by_rows, by_rows),
        check_vma=False,
    )
```

```python
import jax
import jax.numpy as jnp
from jax import lax
from jax.experimental import pallas as pl
from jax.experimental.pallas import tpu as pltpu
from jax.sharding import Mesh, PartitionSpec as P

L = 512
BLK = 128
HB = 2
EPSILON = 1e-05

SLAB = ("y", "xl", "c")
LAT = ("xh", "z")
NEAR = ("xl", "xh", "z")
BF = jnp.bfloat16
F32 = jnp.float32
HALF = 64


def shape_of(shape, dtype):
    return jax.ShapeDtypeStruct(shape, dtype)


def from_behind(value, steps):
    count = lax.axis_size(SLAB)
    first, last = (max(0, -steps), min(count, count - steps))
    return lax.ppermute(value, SLAB, [(source, source + steps) for source in range(first, last)])


def pick_blocks(source_table, blocks):
    width = source_table.shape[1]
    return jnp.take(source_table.reshape(-1, BLK, width), blocks, axis=0).reshape(-1, width)


def pair(value):
    half = value.shape[-2] // 2
    return jnp.concatenate([value[..., :half, :], value[..., half:, :]], axis=-1)


def unpair(value):
    half = value.shape[-1] // 2
    return jnp.concatenate([value[..., :half], value[..., half:]], axis=-2)


def dot(left, right):
    return jnp.dot(left, right, preferred_element_type=F32)


def dot_rows(left, right):
    return lax.dot_general(left, right, (((0,), (0,)), ((), ())), preferred_element_type=F32)


def dot_transpose(left, right):
    return lax.dot_general(left, right, (((1,), (1,)), ((), ())), preferred_element_type=F32)


def left_lanes(rows):
    return lax.broadcasted_iota(jnp.int32, (rows, 2 * HALF), 1) < HALF


def join_halves(first, second):
    low = left_lanes(first.shape[0])
    first, second = first.astype(F32), second.astype(F32)
    upper = jnp.where(low, first, pltpu.roll(second, HALF, 1))
    lower = jnp.where(low, pltpu.roll(first, HALF, 1), second)
    return upper, lower


def one_hot_columns(offsets):
    cells = lax.broadcasted_iota(jnp.int32, (BLK, BLK), 0)
    return (cells == offsets).astype(F32)


def norm_parts(values):
    average = jnp.mean(values, axis=-1, keepdims=True)
    centred = values - average
    variance = jnp.mean(centred * centred, axis=-1, keepdims=True)
    inverse = lax.rsqrt(variance + EPSILON)
    return centred * inverse, inverse


def norm_back(upstream, normed, inverse, gain_vector):
    scaled = upstream * gain_vector
    return inverse * (
        scaled
        - jnp.mean(scaled, axis=-1, keepdims=True)
        - normed * jnp.mean(scaled * normed, axis=-1, keepdims=True)
    )


def split_three(value):
    high = value.astype(BF)
    rest = value - high.astype(F32)
    middle = rest.astype(BF)
    return high, middle, (rest - middle.astype(F32)).astype(BF)


def unpack_weights(core, mine, theirs, outs, counts):
    total = sum(counts)

    def place(source, parity):
        for y in range(source.shape[0]):
            for x in range(source.shape[1] // total):
                slab = (y * (source.shape[1] // total) + x) * 2 + parity
                at = x * total
                for out, count in zip(outs, counts):
                    out[pl.ds(slab * count, count), :] = source[y, pl.ds(at, count), :]
                    at += count

    for parity in range(2):

        @pl.when(core == parity)
        def _():
            place(mine, parity)
            place(theirs, 1 - parity)


def pack_grads(core, grads, keep, send, counts):
    total = sum(counts)
    per = keep.shape[1] // total
    for target, parity in ((keep, core), (send, 1 - core)):
        for y in range(keep.shape[0]):
            for x in range(per):
                at = x * total
                for grad, count in zip(grads, counts):
                    start = pl.multiple_of(((y * per + x) * 2 + parity) * count, 32)
                    target[y, pl.ds(at, count), :] = grad[pl.ds(start, count), :].astype(BF)
                    at += count


def edge_forward(
    scal, arrived, edges, offsets, mine, theirs, gain,
    joined, first, normed, inverse, new_edges, partial, own, upstream, w_in, w_out,
    ext, second,
):
    tiles = edges.shape[0] // BLK
    slab_blocks = partial.shape[0]
    half_rows = ext.shape[0] // 2
    lat_index, core, count = scal[2 * tiles], scal[2 * tiles + 1], scal[2 * tiles + 2]
    slabs = w_in.shape[0] // 3 // 32
    unpack_weights(core, mine, theirs, (w_in, w_out), (3 * L // slabs, L // slabs))
    for block in range(half_rows // BLK):
        rows = pl.ds(block * BLK, BLK)
        for k in range(slab_blocks // 2):
            upper, lower = join_halves(arrived[2 * k, rows, :], arrived[2 * k + 1, rows, :])
            ext[rows, pl.ds(k * BLK, BLK)] = upper.astype(BF)
            ext[pl.ds(half_rows + block * BLK, BLK), pl.ds(k * BLK, BLK)] = lower.astype(BF)
    for k in range(slab_blocks // 2):
        rows = pl.ds(half_rows, BLK // 2)
        upper, lower = join_halves(arrived[2 * k, rows, :], arrived[2 * k + 1, rows, :])
        upstream[pl.ds(0, BLK // 2), pl.ds(k * BLK, BLK)] = upper.astype(BF)
        upstream[pl.ds(BLK // 2, BLK // 2), pl.ds(k * BLK, BLK)] = lower.astype(BF)
    own[...] = ext[pl.ds(pl.multiple_of((HB + lat_index) * BLK, BLK), BLK), :]
    for t in range(tiles):
        rows = pl.ds(t * BLK, BLK)
        joined[rows, pl.ds(0, L)] = edges[rows, :]
        to_src = one_hot_columns(offsets[1, pl.ds(t, 1), :]).T.astype(BF)
        to_dst = one_hot_columns(offsets[0, pl.ds(t, 1), :]).T.astype(BF)
        src = pl.ds(pl.multiple_of(scal[tiles + t] * BLK, BLK), BLK)
        dst = pl.ds(pl.multiple_of((scal[t] + HB) * BLK, BLK), BLK)
        joined[rows, pl.ds(L, L)] = dot(to_src, ext[src, :]).astype(BF)
        joined[rows, pl.ds(2 * L, L)] = dot(to_dst, ext[dst, :]).astype(BF)
    for n in range(2):
        columns = pl.ds(n * 256, 256)
        first[:, columns] = jnp.maximum(dot(joined[...], w_in[:, columns]), 0.0).astype(BF)
    for n in range(2):
        columns = pl.ds(n * 256, 256)
        second[:, columns] = dot(first[...], w_out[:, columns])
    partial[...] = jnp.zeros_like(partial)
    for t in range(tiles):
        rows = pl.ds(t * BLK, BLK)
        live = (lat_index * tiles + t < count).astype(F32)
        values, inv = norm_parts(second[rows, :])
        normed[rows, :] = values
        inverse[rows, :] = jnp.broadcast_to(inv, (BLK, BLK))
        message = values * gain[...] * live
        new_edges[rows, :] = (edges[rows, :].astype(F32) + message).astype(BF)
        second[rows, :] = message
    for t in range(tiles):
        rows = pl.ds(t * BLK, BLK)
        into = one_hot_columns(offsets[0, pl.ds(t, 1), :]).astype(BF)
        high, middle, low = split_three(second[rows, :])
        block = scal[t]
        partial[block] = partial[block] + (dot(into, low) + dot(into, middle) + dot(into, high))


def node_step(
    scal, spread, own, upstream, mine, theirs, gain,
    d_agg, d_direct, new_rows, keep, send,
    w_in, w_out, joined, first, g_in, g_out,
):
    core = scal[1]
    slabs = w_in.shape[0] // 2 // 32
    counts = (2 * L // slabs, L // slabs)
    unpack_weights(core, mine, theirs, (w_in, w_out), counts)
    total = spread[0]
    for l in range(1, spread.shape[0]):
        total = total + spread[l]
    joined[:, pl.ds(0, L)] = own[...]
    joined[:, pl.ds(L, L)] = total.astype(BF)
    first[...] = jnp.maximum(dot(joined[...], w_in[...]), 0.0).astype(BF)
    normed, inverse = norm_parts(dot(first[...], w_out[...]))
    new_rows[...] = (own[...].astype(F32) + normed * gain[...]).astype(BF)
    d_second = norm_back(upstream[...].astype(F32), normed, inverse, gain[...]).astype(BF)
    g_out[...] = dot_rows(first[...], d_second)
    d_first = dot_transpose(d_second, w_out[...])
    d_first = jnp.where(first[...].astype(F32) > 0, d_first, 0.0).astype(BF)
    g_in[...] = dot_rows(joined[...], d_first)
    d_direct[...] = dot_transpose(d_first, w_in[pl.ds(0, L), :])
    d_agg[...] = dot_transpose(d_first, w_in[pl.ds(L, L), :]).astype(BF)
    pack_grads(core, (g_in, g_out), keep, send, counts)


def edge_backward(
    scal, d_agg, cot, normed, inverse, first, joined, w_in, w_out, gain, offsets, d_direct,
    grad_edges, columns, keep, send,
    d_second, d_first, d_ext, d_joined, g_in, g_out,
):
    tiles = cot.shape[0] // BLK
    lat_index, core, count = scal[2 * tiles], scal[2 * tiles + 1], scal[2 * tiles + 2]
    slabs = w_in.shape[0] // 3 // 32
    for t in range(tiles):
        rows = pl.ds(t * BLK, BLK)
        live = (lat_index * tiles + t < count).astype(F32)
        to_dst = one_hot_columns(offsets[0, pl.ds(t, 1), :]).T.astype(BF)
        picked = dot(to_dst, d_agg[scal[t], pl.ds(0, BLK), :])
        d_message = (cot[rows, :].astype(F32) + picked) * live
        back = norm_back(d_message, normed[rows, :], inverse[rows, pl.ds(0, 1)], gain[...])
        d_second[rows, :] = back.astype(BF)
    for n in range(2):
        part = pl.ds(n * 256, 256)
        back = dot_transpose(d_second[...], w_out[part, :])
        d_first[:, part] = jnp.where(first[:, part].astype(F32) > 0, back, 0.0).astype(BF)
    for n in range(6):
        part = pl.ds(n * 256, 256)
        d_joined[:, part] = dot_transpose(d_first[...], w_in[part, :])
    for n in range(2):
        part = pl.ds(n * 256, 256)
        g_out[part, :] = dot_rows(first[:, part], d_second[...])
    for n in range(6):
        part = pl.ds(n * 256, 256)
        g_in[part, :] = dot_rows(joined[:, part], d_first[...])
    pack_grads(core, (g_in, g_out), keep, send, (3 * L // slabs, L // slabs))
    d_ext[...] = jnp.zeros_like(d_ext)
    for t in range(tiles):
        rows = pl.ds(t * BLK, BLK)
        grad_edges[rows, :] = (cot[rows, :].astype(F32) + d_joined[rows, pl.ds(0, L)]).astype(BF)
        for row, place, at in ((1, scal[tiles + t], L), (0, scal[t] + HB, 2 * L)):
            into = one_hot_columns(offsets[row, pl.ds(t, 1), :]).astype(BF)
            value = d_joined[rows, pl.ds(at, L)]
            high = value.astype(BF)
            low = (value - high.astype(F32)).astype(BF)
            d_ext[place] = d_ext[place] + (dot(into, low) + dot(into, high))
    d_ext[HB + lat_index] = d_ext[HB + lat_index] + d_direct[...]
    half_blocks = d_ext.shape[0] // 2
    for block in range(half_blocks):
        rows = pl.ds(block * BLK, BLK)
        for k in range(columns.shape[0] // 2):
            lanes = pl.ds(k * BLK, BLK)
            first_out, second_out = join_halves(
                d_ext[block, :, lanes], d_ext[half_blocks + block, :, lanes]
            )
            columns[2 * k, rows, :] = first_out.astype(BF)
            columns[2 * k + 1, rows, :] = second_out.astype(BF)


def call(kernel, out_shape, scratch, flops, operands):
    moved = sum(x.size * x.dtype.itemsize for x in operands)
    moved += sum(x.size * x.dtype.itemsize for x in out_shape)
    vmem = pl.BlockSpec(memory_space=pltpu.VMEM)
    return pl.pallas_call(
        kernel,
        out_shape=out_shape,
        in_specs=[pl.BlockSpec(memory_space=pltpu.SMEM)] + [vmem] * (len(operands) - 1),
        out_specs=[vmem] * len(out_shape),
        scratch_shapes=[pltpu.VMEM(shape, dtype) for shape, dtype in scratch],
        cost_estimate=pl.CostEstimate(flops=flops, bytes_accessed=moved, transcendentals=0),
        compiler_params=pltpu.CompilerParams(vmem_limit_bytes=48 << 20),
    )(*operands)


def run_edge_forward(scal, arrived, edges, offsets, mine, theirs, gain):
    rows = edges.shape[0]
    lat_size = arrived.shape[0]
    ext_rows = 2 * arrived.shape[1] - BLK
    return call(
        edge_forward,
        [
            shape_of((rows, 3 * L), BF),
            shape_of((rows, L), BF),
            shape_of((rows, L), F32),
            shape_of((rows, BLK), F32),
            shape_of((rows, L), BF),
            shape_of((lat_size, BLK, L), F32),
            shape_of((BLK, L), BF),
            shape_of((BLK, L), BF),
            shape_of((3 * L, L), BF),
            shape_of((L, L), BF),
        ],
        [((ext_rows, L), BF), ((rows, L), F32)],
        2 * rows * 4 * L * L,
        (scal, arrived, edges, offsets, mine, theirs, gain),
    )


def run_node_step(scal, spread, own, upstream, mine, theirs, gain):
    return call(
        node_step,
        [
            shape_of((BLK, L), BF),
            shape_of((BLK, L), F32),
            shape_of((BLK, L), BF),
            shape_of(mine.shape, BF),
            shape_of(mine.shape, BF),
        ],
        [
            ((2 * L, L), BF),
            ((L, L), BF),
            ((BLK, 2 * L), BF),
            ((BLK, L), BF),
            ((2 * L, L), F32),
            ((L, L), F32),
        ],
        2 * BLK * 9 * L * L,
        (scal, spread, own, upstream, mine, theirs, gain),
    )


def run_edge_backward(
    scal, d_agg, cot, normed, inverse, first, joined, w_in, w_out, gain, offsets, d_direct, width
):
    rows = cot.shape[0]
    lat_size = d_agg.shape[0]
    blocks = lat_size + 2 * HB
    return call(
        edge_backward,
        [
            shape_of((rows, L), BF),
            shape_of((lat_size, blocks * BLK // 2, BLK), BF),
            shape_of((4, L // 2, L), BF),
            shape_of((4, L // 2, L), BF),
        ],
        [
            ((rows, L), BF),
            ((rows, L), BF),
            ((blocks, BLK, L), F32),
            ((rows, 3 * L), F32),
            ((3 * L, L), F32),
            ((L, L), F32),
        ],
        2 * rows * 8 * L * L,
        (scal, d_agg, cot, normed, inverse, first, joined, w_in, w_out, gain, offsets, d_direct),
    )


def swap_cores(value):
    return lax.ppermute(value, "c", [(0, 1), (1, 0)])


def spread_rows(value, axes):
    return lax.all_to_all(value, axes, 0, 0)


def gather_over(value, axes):
    return spread_rows(jnp.broadcast_to(value, (lax.axis_size(axes),) + value.shape), axes)


def slab_rows_of(near, pieces):
    lat = lax.axis_size(LAT)
    shaped = near.reshape((-1, lat) + near.shape[1:])
    out, at = [], 0
    for count in pieces:
        out.append(shaped[:, :, at : at + count].reshape(shaped.shape[0], lat * count, L))
        at += count
    return jnp.concatenate(out, axis=1).reshape(-1, L)


def reduce_grads(keep, send, counts):
    lat = lax.axis_size(LAT)
    arrived = swap_cores(send)
    halves = (keep.astype(F32) + arrived.astype(F32)).astype(BF)
    over_y = jnp.sum(spread_rows(halves, "y").astype(F32), axis=0)
    shaped = over_y.reshape(lax.axis_size("xl"), lat * sum(counts), L)
    parts, at = [], 0
    for count in counts:
        parts.append(shaped[:, at : at + lat * count].reshape(-1, lat, count, L))
        at += lat * count
    return jnp.concatenate(parts, axis=2).reshape(-1, sum(counts), L).astype(BF)


def per_device(
    nodes,
    edges,
    edge_tiles,
    edge_offsets,
    tile_counts,
    halo_blocks,
    w_edge_in,
    w_edge_out,
    w_node_in,
    w_node_out,
    edge_gain,
    node_gain,
    node_cotangent,
    edge_cotangent,
):
    lat_size = lax.axis_size(LAT)
    lat_index = lax.axis_index(LAT)
    core = lax.axis_index("c")
    slab_rows, width = nodes.shape
    own_rows = slab_rows // lat_size
    halo_rows = HB * BLK
    ext_rows = slab_rows + 2 * halo_rows
    up_list = halo_blocks[0, 0]
    down_list = halo_blocks[0, 1]
    edge_counts = (w_edge_in.shape[0], w_edge_out.shape[0])
    node_counts = (w_node_in.shape[0], w_node_out.shape[0])

    scal = jnp.concatenate(
        [
            edge_tiles.reshape(-1),
            jnp.stack([lat_index, core]).astype(jnp.int32),
            tile_counts,
        ]
    )
    node_scal = jnp.stack([lat_index, core]).astype(jnp.int32)
    offsets = edge_offsets.reshape(2, -1, BLK)
    edge_gain_row = edge_gain.reshape(1, L)
    node_gain_row = node_gain.reshape(1, L)

    from_lower = unpair(from_behind(pair(pick_blocks(nodes, up_list)), 1))
    from_upper = unpair(from_behind(pair(pick_blocks(nodes, down_list)), -1))

    shards = [w_edge_in, w_edge_out, w_node_in, w_node_out]
    rows = sum(shard.shape[0] for shard in shards)
    near = gather_over(jnp.concatenate(shards + [jnp.zeros((-rows % 16, L), BF)], axis=0), NEAR)
    edge_part = slab_rows_of(near[:, : sum(edge_counts)], edge_counts)
    node_part = slab_rows_of(near[:, sum(edge_counts) : rows], node_counts)

    table = pair(jnp.concatenate([from_lower, nodes, from_upper], axis=0))
    cot = pair(node_cotangent.reshape(lat_size, own_rows, width))
    message_out = jnp.concatenate(
        [jnp.broadcast_to(table, (lat_size,) + table.shape), cot], axis=1
    )
    edge_mine = gather_over(edge_part, "y")
    arrived = spread_rows(message_out, LAT)
    edge_theirs = swap_cores(edge_mine)

    joined, first, normed, inverse, new_edges, partial, own, upstream, e_in, e_out = (
        run_edge_forward(scal, arrived, edges, offsets, edge_mine, edge_theirs, edge_gain_row)
    )
    spread = spread_rows(partial, LAT)
    node_mine = gather_over(node_part, "y")
    node_theirs = swap_cores(node_mine)
    d_agg, d_direct, new_rows, node_keep, node_send = run_node_step(
        node_scal, spread, own, upstream, node_mine, node_theirs, node_gain_row
    )

    groups = L // width
    group_rows = own_rows // groups
    rows_out = (
        new_rows.reshape(groups, group_rows, lat_size, width)
        .transpose(2, 1, 0, 3)
        .reshape(lat_size, group_rows, L)
    )
    second_out = jnp.concatenate(
        [jnp.broadcast_to(d_agg, (lat_size,) + d_agg.shape), rows_out], axis=1
    )
    second_in = spread_rows(second_out, LAT)
    new_nodes = (
        second_in[:, own_rows:]
        .reshape(lat_size, group_rows, groups, width)
        .transpose(0, 2, 1, 3)
        .reshape(slab_rows, width)
    )
    node_near = reduce_grads(node_keep, node_send, node_counts)

    grad_edges, columns, edge_keep, edge_send = run_edge_backward(
        scal, second_in, edge_cotangent, normed, inverse, first, joined, e_in, e_out,
        edge_gain_row, offsets, d_direct, width,
    )
    summed = unpair(jnp.sum(spread_rows(columns, LAT).astype(F32), axis=0))
    d_lower = pair(summed[:halo_rows].astype(BF))
    d_middle = summed[halo_rows : halo_rows + slab_rows]
    d_upper = pair(summed[halo_rows + slab_rows :].astype(BF))
    from_above = unpair(from_behind(d_lower, -1)).astype(F32).reshape(HB, BLK, width)
    from_below = unpair(from_behind(d_upper, 1)).astype(F32).reshape(HB, BLK, width)
    blocks = d_middle.reshape(-1, BLK, width)
    numbers = jnp.arange(blocks.shape[0])
    for j in range(HB):
        blocks = blocks + jnp.where((numbers == up_list[j])[:, None, None], from_above[j], 0.0)
        blocks = blocks + jnp.where((numbers == down_list[j])[:, None, None], from_below[j], 0.0)
    grad_slab = blocks.reshape(slab_rows, width).astype(BF)

    edge_near = reduce_grads(edge_keep, edge_send, edge_counts)
    both = jnp.concatenate([edge_near, node_near], axis=1)
    both = jnp.pad(both, ((0, 0), (0, -both.shape[1] % 16), (0, 0)))
    total = jnp.sum(spread_rows(both, NEAR).astype(F32), axis=0)
    out, at = [], 0
    for count in edge_counts + node_counts:
        out.append(total[at : at + count])
        at += count
    return (new_nodes, new_edges, grad_slab, grad_edges) + tuple(out)


def solution(mesh):
    fine = Mesh(mesh.devices.reshape(4, 2, 2, 2, 4), ("y", "xl", "c", "xh", "z"))
    every = SLAB + LAT
    by_rows = P(every, None)
    split = P(SLAB, LAT)
    placed = (
        split,
        by_rows,
        P(None, every),
        P(None, every),
        P(SLAB),
        P(SLAB, None, None),
        by_rows,
        by_rows,
        by_rows,
        by_rows,
        P(),
        P(),
        split,
        by_rows,
    )
    return jax.shard_map(
        per_device,
        mesh=fine,
        in_specs=placed,
        out_specs=(split, by_rows, split, by_rows, by_rows, by_rows, by_rows, by_rows),
        check_vma=False,
    )
```

```python
import jax
import jax.numpy as jnp
from jax import lax
from jax.experimental import pallas as pl
from jax.experimental.pallas import tpu as pltpu
from jax.sharding import Mesh, PartitionSpec as P

L = 512
BLK = 128
HB = 2
EPSILON = 1e-05

SLAB = ("y", "xl", "c")
LAT = ("xh", "z")
NEAR = ("xl", "xh", "z")
BF = jnp.bfloat16
F32 = jnp.float32
EDGE_MIB = 20
NODE_MIB = 14
BACK_MIB = 26


def shape_of(shape, dtype):
    return jax.ShapeDtypeStruct(shape, dtype)


def from_behind(value, steps):
    count = lax.axis_size(SLAB)
    first, last = (max(0, -steps), min(count, count - steps))
    return lax.ppermute(value, SLAB, [(source, source + steps) for source in range(first, last)])


def dot(left, right):
    return jnp.dot(left, right, preferred_element_type=F32)


def dot_rows(left, right):
    return lax.dot_general(left, right, (((0,), (0,)), ((), ())), preferred_element_type=F32)


def dot_transpose(left, right):
    return lax.dot_general(left, right, (((1,), (1,)), ((), ())), preferred_element_type=F32)


def one_hot_columns(offsets):
    cells = lax.broadcasted_iota(jnp.int32, (BLK, BLK), 0)
    return (cells == offsets).astype(F32)


def norm_parts(values):
    average = jnp.mean(values, axis=-1, keepdims=True)
    centred = values - average
    variance = jnp.mean(centred * centred, axis=-1, keepdims=True)
    inverse = lax.rsqrt(variance + EPSILON)
    return centred * inverse, inverse


def norm_back(upstream, normed, inverse, gain_vector):
    scaled = upstream * gain_vector
    return inverse * (
        scaled
        - jnp.mean(scaled, axis=-1, keepdims=True)
        - normed * jnp.mean(scaled * normed, axis=-1, keepdims=True)
    )


def split_three(value):
    high = value.astype(BF)
    rest = value - high.astype(F32)
    middle = rest.astype(BF)
    return high, middle, (rest - middle.astype(F32)).astype(BF)


def unpack_weights(core, y_index, shards, outs, counts):
    total = sum(counts)
    y_count = len(shards) // 2
    for number, source in enumerate(shards):
        step = number % y_count
        parity = core if number < y_count else 1 - core
        y = lax.rem(y_index - step + y_count, y_count)
        per = source.shape[0] // total
        for x in range(per):
            slab = (y * per + x) * 2 + parity
            at = x * total
            for out, count in zip(outs, counts):
                start = pl.multiple_of(slab * count, 32)
                out[pl.ds(start, count), :] = source[pl.ds(at, count), :]
                at += count


def pack_grads(core, y_index, grads, keep, send, counts):
    total = sum(counts)
    y_count = keep.shape[0]
    per = keep.shape[1] // total
    for target, parity in ((keep, core), (send, 1 - core)):
        for step in range(y_count):
            y = lax.rem(y_index + step, y_count)
            for x in range(per):
                at = x * total
                for grad, count in zip(grads, counts):
                    start = pl.multiple_of(((y * per + x) * 2 + parity) * count, 32)
                    target[step, pl.ds(at, count), :] = grad[pl.ds(start, count), :].astype(BF)
                    at += count


def block_at(number):
    return pl.ds(pl.multiple_of(number * BLK, BLK), BLK)


def edge_forward(scal, ext, edges, offsets, *refs):
    shards, refs = refs[:8], refs[8:]
    gain, joined, first, normed, inverse, new_edges, partial, w_in, w_out, second = refs
    tiles = edges.shape[0] // BLK
    lat_index, core, y_index, count = (scal[2 * tiles + i] for i in range(4))
    slabs = w_in.shape[0] // 3 // 32
    unpack_weights(core, y_index, shards, (w_in, w_out), (3 * L // slabs, L // slabs))
    for t in range(tiles):
        rows = pl.ds(t * BLK, BLK)
        joined[rows, pl.ds(0, L)] = edges[rows, :]
        to_src = one_hot_columns(offsets[1, pl.ds(t, 1), :]).T.astype(BF)
        to_dst = one_hot_columns(offsets[0, pl.ds(t, 1), :]).T.astype(BF)
        src, dst = block_at(scal[tiles + t]), block_at(scal[t] + HB)
        joined[rows, pl.ds(L, L)] = dot_transpose(to_src, ext[:, src]).astype(BF)
        joined[rows, pl.ds(2 * L, L)] = dot_transpose(to_dst, ext[:, dst]).astype(BF)
    for n in range(2):
        columns = pl.ds(n * 256, 256)
        first[:, columns] = jnp.maximum(dot(joined[...], w_in[:, columns]), 0.0).astype(BF)
    for n in range(2):
        columns = pl.ds(n * 256, 256)
        second[:, columns] = dot(first[...], w_out[:, columns])
    partial[...] = jnp.zeros_like(partial)
    for t in range(tiles):
        rows = pl.ds(t * BLK, BLK)
        live = (lat_index * tiles + t < count).astype(F32)
        values, inv = norm_parts(second[rows, :])
        normed[rows, :] = values
        inverse[rows, :] = jnp.broadcast_to(inv, (BLK, BLK))
        message = values * gain[...] * live
        new_edges[rows, :] = (edges[rows, :].astype(F32) + message).astype(BF)
        second[rows, :] = message
    for t in range(tiles):
        rows = pl.ds(t * BLK, BLK)
        into = one_hot_columns(offsets[0, pl.ds(t, 1), :]).astype(BF)
        high, middle, low = split_three(second[rows, :])
        block = scal[t]
        partial[block] = partial[block] + (dot(into, low) + dot(into, middle) + dot(into, high))


def node_step(scal, spread, ext, *refs):
    shards, refs = refs[:8], refs[8:]
    gain, out, d_direct, keep, send, w_in, w_out, joined, first, g_in, g_out = refs
    lat_index, core, y_index = scal[0], scal[1], scal[2]
    slabs = w_in.shape[0] // 2 // 32
    counts = (2 * L // slabs, L // slabs)
    unpack_weights(core, y_index, shards, (w_in, w_out), counts)
    total = spread[0]
    for l in range(1, spread.shape[0]):
        total = total + spread[l]
    own = ext[:, block_at(HB + lat_index)].astype(F32).T
    upstream = ext[:, pl.ds(ext.shape[1] - BLK, BLK)].astype(F32).T
    joined[:, pl.ds(0, L)] = own.astype(BF)
    joined[:, pl.ds(L, L)] = total.astype(BF)
    first[...] = jnp.maximum(dot(joined[...], w_in[...]), 0.0).astype(BF)
    normed, inverse = norm_parts(dot(first[...], w_out[...]))
    new_rows = (own + normed * gain[...]).T.astype(BF)
    d_second = norm_back(upstream, normed, inverse, gain[...]).astype(BF)
    g_out[...] = dot_rows(first[...], d_second)
    d_first = dot_transpose(d_second, w_out[...])
    d_first = jnp.where(first[...].astype(F32) > 0, d_first, 0.0).astype(BF)
    g_in[...] = dot_rows(joined[...], d_first)
    d_direct[...] = dot_transpose(w_in[pl.ds(0, L), :], d_first)
    d_agg = dot_transpose(w_in[pl.ds(L, L), :], d_first).astype(BF)
    width = L // out.shape[0]
    for l in range(out.shape[0]):
        out[l, pl.ds(0, L), :] = d_agg
        out[l, pl.ds(L, width), :] = new_rows[l * width : (l + 1) * width, :]
    pack_grads(core, y_index, (g_in, g_out), keep, send, counts)


def edge_backward(
    scal, d_agg, cot, normed, inverse, first, joined, w_in, w_out, gain, offsets, d_direct,
    grad_edges, columns, keep, send,
    d_second, d_first, d_ext, d_turned, g_in, g_out,
):
    tiles = cot.shape[0] // BLK
    lat_index, core, y_index, count = (scal[2 * tiles + i] for i in range(4))
    slabs = w_in.shape[0] // 3 // 32
    for t in range(tiles):
        rows = pl.ds(t * BLK, BLK)
        live = (lat_index * tiles + t < count).astype(F32)
        to_dst = one_hot_columns(offsets[0, pl.ds(t, 1), :]).T.astype(BF)
        picked = dot_transpose(to_dst, d_agg[scal[t], pl.ds(0, L), :])
        d_message = (cot[rows, :].astype(F32) + picked) * live
        back = norm_back(d_message, normed[rows, :], inverse[rows, pl.ds(0, 1)], gain[...])
        d_second[rows, :] = back.astype(BF)
    for n in range(2):
        part = pl.ds(n * 256, 256)
        back = dot_transpose(d_second[...], w_out[part, :])
        d_first[:, part] = jnp.where(first[:, part].astype(F32) > 0, back, 0.0).astype(BF)
    for n in range(2):
        part = pl.ds(n * 256, 256)
        back = dot_transpose(d_first[...], w_in[part, :])
        grad_edges[:, part] = (cot[:, part].astype(F32) + back).astype(BF)
    for n in range(4):
        d_turned[pl.ds(n * 256, 256), :] = dot_transpose(
            w_in[pl.ds(L + n * 256, 256), :], d_first[...]
        )
    for n in range(2):
        part = pl.ds(n * 256, 256)
        g_out[part, :] = dot_rows(first[:, part], d_second[...])
    for n in range(6):
        part = pl.ds(n * 256, 256)
        g_in[part, :] = dot_rows(joined[:, part], d_first[...])
    pack_grads(core, y_index, (g_in, g_out), keep, send, (3 * L // slabs, L // slabs))
    d_ext[...] = jnp.zeros_like(d_ext)
    for t in range(tiles):
        rows = pl.ds(t * BLK, BLK)
        for row, place, at in ((1, scal[tiles + t], 0), (0, scal[t] + HB, L)):
            into = one_hot_columns(offsets[row, pl.ds(t, 1), :]).T.astype(BF)
            value = d_turned[pl.ds(at, L), rows]
            high = value.astype(BF)
            low = (value - high.astype(F32)).astype(BF)
            d_ext[place] = d_ext[place] + (dot(low, into) + dot(high, into))
    d_ext[HB + lat_index] = d_ext[HB + lat_index] + d_direct[...]
    width = columns.shape[1]
    for block in range(d_ext.shape[0]):
        for l in range(columns.shape[0]):
            columns[l, :, pl.ds(block * BLK, BLK)] = d_ext[
                block, pl.ds(l * width, width), :
            ].astype(BF)


def call(kernel, out_shape, scratch, flops, mib, operands):
    moved = sum(x.size * x.dtype.itemsize for x in operands)
    moved += sum(x.size * x.dtype.itemsize for x in out_shape)
    vmem = pl.BlockSpec(memory_space=pltpu.VMEM)
    return pl.pallas_call(
        kernel,
        out_shape=out_shape,
        in_specs=[pl.BlockSpec(memory_space=pltpu.SMEM)] + [vmem] * (len(operands) - 1),
        out_specs=[vmem] * len(out_shape),
        scratch_shapes=[pltpu.VMEM(shape, dtype) for shape, dtype in scratch],
        cost_estimate=pl.CostEstimate(flops=flops, bytes_accessed=moved, transcendentals=0),
        compiler_params=pltpu.CompilerParams(vmem_limit_bytes=mib << 20),
    )(*operands)


def run_edge_forward(scal, ext, edges, offsets, shards, gain, lat_size):
    rows = edges.shape[0]
    return call(
        edge_forward,
        [
            shape_of((rows, 3 * L), BF),
            shape_of((rows, L), BF),
            shape_of((rows, L), F32),
            shape_of((rows, BLK), F32),
            shape_of((rows, L), BF),
            shape_of((lat_size, BLK, L), F32),
            shape_of((3 * L, L), BF),
            shape_of((L, L), BF),
        ],
        [((rows, L), F32)],
        2 * rows * 4 * L * L,
        EDGE_MIB,
        (scal, ext, edges, offsets, *shards, gain),
    )


def run_node_step(scal, spread, ext, shards, gain):
    lat_size = spread.shape[0]
    chunk = (len(shards) // 2,) + shards[0].shape
    return call(
        node_step,
        [
            shape_of((lat_size, L + L // lat_size, BLK), BF),
            shape_of((L, BLK), F32),
            shape_of(chunk, BF),
            shape_of(chunk, BF),
        ],
        [
            ((2 * L, L), BF),
            ((L, L), BF),
            ((BLK, 2 * L), BF),
            ((BLK, L), BF),
            ((2 * L, L), F32),
            ((L, L), F32),
        ],
        2 * BLK * 9 * L * L,
        NODE_MIB,
        (scal, spread, ext, *shards, gain),
    )


def run_edge_backward(
    scal, d_agg, cot, normed, inverse, first, joined, w_in, w_out, gain, offsets, d_direct, chunk
):
    rows = cot.shape[0]
    lat_size = d_agg.shape[0]
    blocks = lat_size + 2 * HB
    return call(
        edge_backward,
        [
            shape_of((rows, L), BF),
            shape_of((lat_size, L // lat_size, blocks * BLK), BF),
            shape_of(chunk, BF),
            shape_of(chunk, BF),
        ],
        [
            ((rows, L), BF),
            ((rows, L), BF),
            ((blocks, L, BLK), F32),
            ((2 * L, rows), F32),
            ((3 * L, L), F32),
            ((L, L), F32),
        ],
        2 * rows * 8 * L * L,
        BACK_MIB,
        (scal, d_agg, cot, normed, inverse, first, joined, w_in, w_out, gain, offsets, d_direct),
    )


def swap_cores(value):
    return lax.ppermute(value, "c", [(0, 1), (1, 0)])


def shift_y(value, step):
    count = lax.axis_size("y")
    return lax.ppermute(value, "y", [(i, (i + step) % count) for i in range(count)])


def spread_rows(value, axes):
    return lax.all_to_all(value, axes, 0, 0)


def gather_over(value, axes):
    return spread_rows(jnp.broadcast_to(value, (lax.axis_size(axes),) + value.shape), axes)


def gather_far(value):
    mine = [value] + [shift_y(value, k) for k in range(1, lax.axis_size("y"))]
    return mine + [swap_cores(one) for one in mine]


def slab_rows_of(near, pieces):
    lat = lax.axis_size(LAT)
    shaped = near.reshape((-1, lat) + near.shape[1:])
    out, at = [], 0
    for count in pieces:
        out.append(shaped[:, :, at : at + count].reshape(shaped.shape[0], lat * count, L))
        at += count
    return jnp.concatenate(out, axis=1).reshape(-1, L)


def reduce_grads(keep, send, counts):
    lat = lax.axis_size(LAT)
    arrived = swap_cores(send)
    over_y = keep[0].astype(F32) + arrived[0].astype(F32)
    for k in range(1, keep.shape[0]):
        both = (keep[k].astype(F32) + arrived[k].astype(F32)).astype(BF)
        over_y = over_y + shift_y(both, k).astype(F32)
    shaped = over_y.astype(BF).reshape(lax.axis_size("xl"), lat * sum(counts), L)
    parts, at = [], 0
    for count in counts:
        parts.append(shaped[:, at : at + lat * count].reshape(-1, lat, count, L))
        at += lat * count
    return jnp.concatenate(parts, axis=2).reshape(-1, sum(counts), L)


def per_device(
    nodes,
    edges,
    edge_tiles,
    edge_offsets,
    tile_counts,
    halo_blocks,
    w_edge_in,
    w_edge_out,
    w_node_in,
    w_node_out,
    edge_gain,
    node_gain,
    node_cotangent,
    edge_cotangent,
):
    lat_size = lax.axis_size(LAT)
    place = [lax.axis_index(LAT), lax.axis_index("c"), lax.axis_index("y")]
    slab_rows, width = nodes.shape
    own_rows = slab_rows // lat_size
    halo_rows = HB * BLK
    ext_rows = slab_rows + 2 * halo_rows
    up_list = halo_blocks[0, 0]
    down_list = halo_blocks[0, 1]
    edge_counts = (w_edge_in.shape[0], w_edge_out.shape[0])
    node_counts = (w_node_in.shape[0], w_node_out.shape[0])

    node_scal = jnp.stack(place).astype(jnp.int32)
    scal = jnp.concatenate([edge_tiles.reshape(-1), node_scal, tile_counts])
    offsets = edge_offsets.reshape(2, -1, BLK)
    edge_gain_row = edge_gain.reshape(1, L)
    node_gain_row = node_gain.reshape(1, L)

    turned = nodes.T

    def halo_of(blocks):
        picked = [
            lax.dynamic_slice(turned, (0, blocks[j] * BLK), (width, BLK)) for j in range(HB)
        ]
        return jnp.concatenate(picked, axis=1)

    from_lower = from_behind(halo_of(up_list), 1)
    from_upper = from_behind(halo_of(down_list), -1)

    shards = [w_edge_in, w_edge_out, w_node_in, w_node_out]
    rows = sum(shard.shape[0] for shard in shards)
    near = gather_over(jnp.concatenate(shards + [jnp.zeros((-rows % 16, L), BF)], axis=0), NEAR)
    edge_part = slab_rows_of(near[:, : sum(edge_counts)], edge_counts)
    node_part = slab_rows_of(near[:, sum(edge_counts) : rows], node_counts)

    table = jnp.concatenate([from_lower, turned, from_upper], axis=1)
    cot = node_cotangent.T.reshape(width, lat_size, own_rows).transpose(1, 0, 2)
    message_out = jnp.concatenate(
        [jnp.broadcast_to(table, (lat_size,) + table.shape), cot], axis=2
    )
    edge_shards = gather_far(edge_part)
    ext = spread_rows(message_out, LAT).reshape(L, ext_rows + own_rows)

    joined, first, normed, inverse, new_edges, partial, e_in, e_out = run_edge_forward(
        scal, ext, edges, offsets, edge_shards, edge_gain_row, lat_size
    )
    node_shards = gather_far(node_part)
    spread = spread_rows(partial, LAT)
    second_out, d_direct, node_keep, node_send = run_node_step(
        node_scal, spread, ext, node_shards, node_gain_row
    )
    second_in = spread_rows(second_out, LAT)
    new_nodes = second_in[:, L:].transpose(1, 0, 2).reshape(width, slab_rows).T
    node_near = reduce_grads(node_keep, node_send, node_counts)

    grad_edges, columns, edge_keep, edge_send = run_edge_backward(
        scal, second_in, edge_cotangent, normed, inverse, first, joined, e_in, e_out,
        edge_gain_row, offsets, d_direct, (lax.axis_size("y"),) + edge_part.shape,
    )
    edge_near = reduce_grads(edge_keep, edge_send, edge_counts)
    summed = jnp.sum(spread_rows(columns, LAT).astype(F32), axis=0)
    d_lower = summed[:, :halo_rows].astype(BF)
    d_middle = summed[:, halo_rows : halo_rows + slab_rows]
    d_upper = summed[:, halo_rows + slab_rows :].astype(BF)
    from_above = from_behind(d_lower, -1).astype(F32).reshape(width, HB, BLK)
    from_below = from_behind(d_upper, 1).astype(F32).reshape(width, HB, BLK)
    blocks = d_middle.reshape(width, -1, BLK)
    numbers = jnp.arange(blocks.shape[1])[None, :, None]
    for j in range(HB):
        blocks = blocks + jnp.where(numbers == up_list[j], from_above[:, j : j + 1], 0.0)
        blocks = blocks + jnp.where(numbers == down_list[j], from_below[:, j : j + 1], 0.0)
    grad_slab = blocks.reshape(width, slab_rows).astype(BF).T

    both = jnp.concatenate([edge_near, node_near], axis=1)
    both = jnp.pad(both, ((0, 0), (0, -both.shape[1] % 16), (0, 0)))
    total = jnp.sum(spread_rows(both, NEAR).astype(F32), axis=0)
    out, at = [], 0
    for count in edge_counts + node_counts:
        out.append(total[at : at + count])
        at += count
    return (new_nodes, new_edges, grad_slab, grad_edges) + tuple(out)


def solution(mesh):
    fine = Mesh(mesh.devices.reshape(4, 2, 2, 2, 4), ("y", "xl", "c", "xh", "z"))
    every = SLAB + LAT
    by_rows = P(every, None)
    split = P(SLAB, LAT)
    placed = (
        split,
        by_rows,
        P(None, every),
        P(None, every),
        P(SLAB),
        P(SLAB, None, None),
        by_rows,
        by_rows,
        by_rows,
        by_rows,
        P(),
        P(),
        split,
        by_rows,
    )
    return jax.shard_map(
        per_device,
        mesh=fine,
        in_specs=placed,
        out_specs=(split, by_rows, split, by_rows, by_rows, by_rows, by_rows, by_rows),
        check_vma=False,
    )
```

```python
import functools

import jax
import jax.numpy as jnp
from jax import lax
from jax.experimental import pallas as pl
from jax.experimental.pallas import tpu as pltpu
from jax.sharding import Mesh, PartitionSpec as P

L = 512
BLK = 128
HB = 2
EPSILON = 1e-05

SLAB = ("y", "xl", "c")
LAT = ("xh", "z")
XS = ("xl", "xh")
BF = jnp.bfloat16
F32 = jnp.float32
EDGE_MIB = 16
NODE_MIB = 14
BACK_MIB = 28


def shape_of(shape, dtype):
    return jax.ShapeDtypeStruct(shape, dtype)


def from_behind(value, steps):
    count = lax.axis_size(SLAB)
    first, last = (max(0, -steps), min(count, count - steps))
    return lax.ppermute(value, SLAB, [(source, source + steps) for source in range(first, last)])


def dot(left, right):
    return jnp.dot(left, right, preferred_element_type=F32)


def dot_rows(left, right):
    return lax.dot_general(left, right, (((0,), (0,)), ((), ())), preferred_element_type=F32)


def dot_transpose(left, right):
    return lax.dot_general(left, right, (((1,), (1,)), ((), ())), preferred_element_type=F32)


def one_hot_columns(offsets):
    cells = lax.broadcasted_iota(jnp.int32, (BLK, BLK), 0)
    return (cells == offsets).astype(F32)


def norm_parts(values):
    average = jnp.mean(values, axis=-1, keepdims=True)
    centred = values - average
    variance = jnp.mean(centred * centred, axis=-1, keepdims=True)
    inverse = lax.rsqrt(variance + EPSILON)
    return centred * inverse, inverse


def norm_back(upstream, normed, inverse, gain_vector):
    scaled = upstream * gain_vector
    return inverse * (
        scaled
        - jnp.mean(scaled, axis=-1, keepdims=True)
        - normed * jnp.mean(scaled * normed, axis=-1, keepdims=True)
    )


def split_three(value):
    high = value.astype(BF)
    rest = value - high.astype(F32)
    middle = rest.astype(BF)
    return high, middle, (rest - middle.astype(F32)).astype(BF)


def block_at(number):
    return pl.ds(pl.multiple_of(number * BLK, BLK), BLK)


def copies(pairs, sems):
    made = [pltpu.make_async_copy(src, dst, sems.at[i]) for i, (src, dst) in enumerate(pairs)]
    for one in made:
        one.start()
    return made


def wait_all(made):
    for one in made:
        one.wait()


def weight_pairs(core, y_index, shards, outs, counts):
    total = sum(counts)
    y_count = len(shards) // 2
    pairs = []
    for number, source in enumerate(shards):
        step = number % y_count
        parity = core if number < y_count else 1 - core
        y = lax.rem(y_index - step + y_count, y_count)
        per = source.shape[0] // total
        for x in range(per):
            slab = (y * per + x) * 2 + parity
            at = x * total
            for out, count in zip(outs, counts):
                start = pl.multiple_of(slab * count, 32)
                pairs.append((source.at[pl.ds(at, count), :], out.at[pl.ds(start, count), :]))
                at += count
    return pairs


def pack_grads(core, y_index, grads, keep, send, counts):
    total = sum(counts)
    y_count = keep.shape[0]
    per = keep.shape[1] // total
    for target, parity in ((keep, core), (send, 1 - core)):
        for step in range(y_count):
            y = lax.rem(y_index + step, y_count)
            for x in range(per):
                at = x * total
                for grad, count in zip(grads, counts):
                    start = pl.multiple_of(((y * per + x) * 2 + parity) * count, 32)
                    target[step, pl.ds(at, count), :] = grad[pl.ds(start, count), :].astype(BF)
                    at += count


def prepare(halo, turned, w_edge_in, w_edge_out, w_node_in, w_node_out, up, down, packed):
    for j in range(HB):
        up[:, pl.ds(j * BLK, BLK)] = turned[:, block_at(halo[j])]
        down[:, pl.ds(j * BLK, BLK)] = turned[:, block_at(halo[HB + j])]
    parts = [ref[...].astype(F32) for ref in (w_edge_in, w_edge_out, w_node_in, w_node_out)]
    used = sum(part.shape[0] for part in parts)
    parts.append(jnp.zeros((packed.shape[0] - used, L), F32))
    packed[...] = jnp.concatenate(parts, axis=0).astype(BF)


def assemble(pieces, scal, *refs):
    blocks, (edge_part, node_part, held, edge_rows, node_rows) = refs[:4], refs[4:]
    z_index, x_index = scal[0], scal[1]
    for k, block in enumerate(blocks):
        held[k] = block[...]
    outs = (edge_rows, edge_rows, node_rows, node_rows)
    bases = []
    for number, count in enumerate(pieces):
        bases.append(0 if number % 2 == 0 else bases[-1] + 8 * pieces[number - 1])
    sizes = (8 * (pieces[0] + pieces[1]), 8 * (pieces[2] + pieces[3]))
    for x in range(4):
        x_step = lax.rem(x_index - x + 4, 4)
        for z in range(4):
            z_step = lax.rem(z_index - z + 4, 4)
            shard = held[z_step, pl.ds(pl.multiple_of(x_step * 32, 32), 32), :].astype(F32)
            row, lat = 0, (x % 2) * 4 + z
            for number, count in enumerate(pieces):
                base = (x // 2) * sizes[number // 2] + bases[number] + lat * count
                outs[number][pl.ds(base, count), :] = shard[row : row + count]
                row += count
    edge_part[...] = edge_rows[...].astype(BF)
    node_part[...] = node_rows[...].astype(BF)


def sum_far(pieces, scal, edge_own, e1, e2, e3, node_own, n1, n2, n3, keep, s1, s2, s3, er, nr, sent):
    z_index = scal[0]
    er[...] = sum((ref[...].astype(F32) for ref in (e1, e2, e3)), edge_own[...].astype(F32))
    nr[...] = sum((ref[...].astype(F32) for ref in (n1, n2, n3)), node_own[...].astype(F32))
    ins = (er, er, nr, nr)
    bases = []
    for number, count in enumerate(pieces):
        bases.append(0 if number % 2 == 0 else bases[-1] + 8 * pieces[number - 1])
    sizes = (8 * (pieces[0] + pieces[1]), 8 * (pieces[2] + pieces[3]))
    spare = 32 - sum(pieces)
    for x in range(4):
        for z in range(4):
            lat = (x % 2) * 4 + z
            parts = []
            for number, count in enumerate(pieces):
                base = (x // 2) * sizes[number // 2] + bases[number] + lat * count
                parts.append(ins[number][pl.ds(base, count), :])
            parts.append(jnp.zeros((spare, L), F32))
            sent[z, x] = jnp.concatenate(parts, axis=0)
    keep[...] = sent[z_index]
    for step, out in ((1, s1), (2, s2), (3, s3)):
        out[...] = sent[lax.rem(z_index + step, 4)].astype(BF)


def sum_z(scal, own, r1, r2, r3, keep, s1, s2, s3, held):
    x_index = scal[1]
    held[...] = own[...] + (r1[...].astype(F32) + r2[...].astype(F32) + r3[...].astype(F32))
    keep[...] = held[x_index]
    for step, out in ((1, s1), (2, s2), (3, s3)):
        out[...] = held[lax.rem(x_index + step, 4)].astype(BF)


def sum_x(own, r1, r2, r3, *outs):
    total = own[...] + (r1[...].astype(F32) + r2[...].astype(F32) + r3[...].astype(F32))
    row = 0
    for out in outs:
        count = out.shape[0]
        out[...] = total[row : row + count]
        row += count


def edge_forward(scal, ext_hbm, edges, offsets, *refs):
    shards, refs = refs[:8], refs[8:]
    gain, joined_out, first_out, normed_out, inverse_out, new_edges_out, partial_out = refs[:7]
    ext, joined, first, normed, inverse, new_edges, partial, w_in, w_out, second = refs[7:17]
    sems, out_sems = refs[17:]
    tiles = edges.shape[0] // BLK
    lat_index, core, y_index, count = (scal[2 * tiles + i] for i in range(4))
    slabs = w_in.shape[0] // 3 // 32
    counts = (3 * L // slabs, L // slabs)
    pairs = [(ext_hbm, ext)] + weight_pairs(core, y_index, shards, (w_in, w_out), counts)
    loads = copies(pairs, sems)
    stores = []

    def store(source, target):
        copy = pltpu.make_async_copy(source, target, out_sems.at[len(stores)])
        copy.start()
        stores.append(copy)

    joined[:, pl.ds(0, L)] = edges[...]
    loads[0].wait()
    for t in range(tiles):
        rows = pl.ds(t * BLK, BLK)
        to_src = one_hot_columns(offsets[1, pl.ds(t, 1), :]).T.astype(BF)
        to_dst = one_hot_columns(offsets[0, pl.ds(t, 1), :]).T.astype(BF)
        src, dst = block_at(scal[tiles + t]), block_at(scal[t] + HB)
        joined[rows, pl.ds(L, L)] = dot_transpose(to_src, ext[:, src]).astype(BF)
        joined[rows, pl.ds(2 * L, L)] = dot_transpose(to_dst, ext[:, dst]).astype(BF)
    store(joined, joined_out)
    wait_all(loads[1:])
    for n in range(2):
        columns = pl.ds(n * 256, 256)
        first[:, columns] = jnp.maximum(dot(joined[...], w_in[:, columns]), 0.0).astype(BF)
    store(first, first_out)
    for n in range(2):
        columns = pl.ds(n * 256, 256)
        second[:, columns] = dot(first[...], w_out[:, columns])
    partial[...] = jnp.zeros_like(partial)
    for t in range(tiles):
        rows = pl.ds(t * BLK, BLK)
        live = (lat_index * tiles + t < count).astype(F32)
        values, inv = norm_parts(second[rows, :])
        normed[rows, :] = values
        inverse[rows, :] = jnp.broadcast_to(inv, (BLK, BLK))
        message = values * gain[...] * live
        new_edges[rows, :] = (edges[rows, :].astype(F32) + message).astype(BF)
        second[rows, :] = message
    store(normed, normed_out)
    store(inverse, inverse_out)
    store(new_edges, new_edges_out)
    for t in range(tiles):
        rows = pl.ds(t * BLK, BLK)
        into = one_hot_columns(offsets[0, pl.ds(t, 1), :]).astype(BF)
        high, middle, low = split_three(second[rows, :])
        block = scal[t]
        partial[block] = partial[block] + (dot(into, low) + dot(into, middle) + dot(into, high))
    store(partial, partial_out)
    wait_all(stores)


def node_step(scal, spread, ext_hbm, *refs):
    shards, refs = refs[:8], refs[8:]
    gain, out, d_direct, keep, send = refs[:5]
    own_turned, up_turned, w_in, w_out, joined, first, g_in, g_out, sems = refs[5:]
    lat_index, core, y_index = scal[0], scal[1], scal[2]
    slabs = w_in.shape[0] // 2 // 32
    counts = (2 * L // slabs, L // slabs)
    pairs = [
        (ext_hbm.at[:, block_at(HB + lat_index)], own_turned),
        (ext_hbm.at[:, pl.ds(ext_hbm.shape[1] - BLK, BLK)], up_turned),
    ] + weight_pairs(core, y_index, shards, (w_in, w_out), counts)
    loads = copies(pairs, sems)
    total = spread[0]
    for l in range(1, spread.shape[0]):
        total = total + spread[l]
    joined[:, pl.ds(L, L)] = total.astype(BF)
    wait_all(loads)
    own = own_turned[...].astype(F32).T
    upstream = up_turned[...].astype(F32).T
    joined[:, pl.ds(0, L)] = own.astype(BF)
    first[...] = jnp.maximum(dot(joined[...], w_in[...]), 0.0).astype(BF)
    normed, inverse = norm_parts(dot(first[...], w_out[...]))
    new_rows = (own + normed * gain[...]).T.astype(BF)
    d_second = norm_back(upstream, normed, inverse, gain[...]).astype(BF)
    d_first = dot_transpose(d_second, w_out[...])
    d_first = jnp.where(first[...].astype(F32) > 0, d_first, 0.0).astype(BF)
    d_direct[...] = dot_transpose(w_in[pl.ds(0, L), :], d_first)
    d_agg = dot_transpose(w_in[pl.ds(L, L), :], d_first).astype(BF)
    width = L // out.shape[0]
    for l in range(out.shape[0]):
        out[l, pl.ds(0, L), :] = d_agg
        out[l, pl.ds(L, width), :] = new_rows[l * width : (l + 1) * width, :]
    g_out[...] = dot_rows(first[...], d_second)
    g_in[...] = dot_rows(joined[...], d_first)
    pack_grads(core, y_index, (g_in, g_out), keep, send, counts)


def edge_backward(scal, d_agg, cot, offsets, gain, *refs):
    saved, shards, refs = refs[:5], refs[5:13], refs[13:]
    grad_edges, middle_out, lower, upper, keep, send = refs[:6]
    joined, first, normed, inverse, d_direct, w_in, w_out = refs[6:13]
    d_second, d_first, d_ext, d_turned, g_in, g_out, sems = refs[13:]
    tiles = cot.shape[0] // BLK
    lat_index, core, y_index, count = (scal[2 * tiles + i] for i in range(4))
    slabs = w_in.shape[0] // 3 // 32
    counts = (3 * L // slabs, L // slabs)
    normed_in, inverse_in, first_in, joined_in, direct_in = saved
    pairs = [(normed_in, normed), (inverse_in, inverse)]
    pairs += weight_pairs(core, y_index, shards, (w_in, w_out), counts)
    pairs += [(first_in, first), (joined_in, joined), (direct_in, d_direct)]
    loads = copies(pairs, sems)
    wait_all(loads[:2])
    for t in range(tiles):
        rows = pl.ds(t * BLK, BLK)
        live = (lat_index * tiles + t < count).astype(F32)
        to_dst = one_hot_columns(offsets[0, pl.ds(t, 1), :]).T.astype(BF)
        picked = dot_transpose(to_dst, d_agg[scal[t], pl.ds(0, L), :])
        d_message = (cot[rows, :].astype(F32) + picked) * live
        back = norm_back(d_message, normed[rows, :], inverse[rows, pl.ds(0, 1)], gain[...])
        d_second[rows, :] = back.astype(BF)
    wait_all(loads[2:])
    for n in range(2):
        part = pl.ds(n * 256, 256)
        back = dot_transpose(d_second[...], w_out[part, :])
        d_first[:, part] = jnp.where(first[:, part].astype(F32) > 0, back, 0.0).astype(BF)
    for n in range(4):
        d_turned[pl.ds(n * 256, 256), :] = dot_transpose(
            w_in[pl.ds(L + n * 256, 256), :], d_first[...]
        )
    d_ext[...] = jnp.zeros_like(d_ext)
    for t in range(tiles):
        rows = pl.ds(t * BLK, BLK)
        for row, place, at in ((1, scal[tiles + t], 0), (0, scal[t] + HB, L)):
            into = one_hot_columns(offsets[row, pl.ds(t, 1), :]).T.astype(BF)
            value = d_turned[pl.ds(at, L), rows]
            high = value.astype(BF)
            low = (value - high.astype(F32)).astype(BF)
            d_ext[place] = d_ext[place] + (dot(low, into) + dot(high, into))
    d_ext[HB + lat_index] = d_ext[HB + lat_index] + d_direct[...]
    blocks = middle_out.shape[0]
    for j in range(HB):
        lower[:, pl.ds(j * BLK, BLK)] = d_ext[j].astype(BF)
        upper[:, pl.ds(j * BLK, BLK)] = d_ext[HB + blocks + j].astype(BF)
    middle_out[...] = d_ext[pl.ds(HB, blocks)]
    for n in range(2):
        part = pl.ds(n * 256, 256)
        back = dot_transpose(d_first[...], w_in[part, :])
        grad_edges[:, part] = (cot[:, part].astype(F32) + back).astype(BF)
    for n in range(2):
        part = pl.ds(n * 256, 256)
        g_out[part, :] = dot_rows(first[:, part], d_second[...])
    for n in range(6):
        part = pl.ds(n * 256, 256)
        g_in[part, :] = dot_rows(joined[:, part], d_first[...])
    pack_grads(core, y_index, (g_in, g_out), keep, send, counts)


def add_halo(halo, middle, above, below, columns, held):
    held[...] = middle[...]
    for j in range(HB):
        for place, value in ((halo[j], above), (halo[HB + j], below)):
            held[place] = held[place] + value[:, pl.ds(j * BLK, BLK)].astype(F32)
    width = columns.shape[1]
    for block in range(held.shape[0]):
        for l in range(columns.shape[0]):
            columns[l, :, pl.ds(block * BLK, BLK)] = held[
                block, pl.ds(l * width, width), :
            ].astype(BF)


def finish(arrived, out):
    total = arrived[0].astype(F32)
    for l in range(1, arrived.shape[0]):
        total = total + arrived[l].astype(F32)
    out[...] = total.astype(BF)


def call(kernel, out_shape, scratch, mib, spaces, operands, flops=0, out_spaces="", sems=()):
    moved = sum(x.size * x.dtype.itemsize for x in operands)
    moved += sum(x.size * x.dtype.itemsize for x in out_shape)
    named = {"s": pltpu.SMEM, "v": pltpu.VMEM, "h": pltpu.HBM}
    out_spaces = out_spaces or "v" * len(out_shape)
    return pl.pallas_call(
        kernel,
        out_shape=out_shape,
        in_specs=[pl.BlockSpec(memory_space=named[space]) for space in spaces],
        out_specs=[pl.BlockSpec(memory_space=named[space]) for space in out_spaces],
        scratch_shapes=[pltpu.VMEM(shape, dtype) for shape, dtype in scratch]
        + [pltpu.SemaphoreType.DMA((count,)) for count in sems],
        cost_estimate=pl.CostEstimate(flops=flops, bytes_accessed=moved, transcendentals=0),
        compiler_params=pltpu.CompilerParams(vmem_limit_bytes=mib << 20),
    )(*operands)


def run_edge_forward(scal, ext, edges, offsets, shards, gain, lat_size):
    rows = edges.shape[0]
    outs = [
        shape_of((rows, 3 * L), BF),
        shape_of((rows, L), BF),
        shape_of((rows, L), F32),
        shape_of((rows, BLK), F32),
        shape_of((rows, L), BF),
        shape_of((lat_size, BLK, L), F32),
    ]
    held = [(ext.shape, BF)] + [(out.shape, out.dtype) for out in outs]
    return call(
        edge_forward,
        outs,
        held + [((3 * L, L), BF), ((L, L), BF), ((rows, L), F32)],
        EDGE_MIB,
        "shvv" + "h" * len(shards) + "v",
        (scal, ext, edges, offsets, *shards, gain),
        flops=2 * rows * 4 * L * L,
        out_spaces="h" * len(outs),
        sems=(1 + 4 * len(shards), len(outs)),
    )


def run_node_step(scal, spread, ext, shards, gain):
    lat_size = spread.shape[0]
    chunk = (len(shards) // 2,) + shards[0].shape
    return call(
        node_step,
        [
            shape_of((lat_size, L + L // lat_size, BLK), BF),
            shape_of((L, BLK), F32),
            shape_of(chunk, BF),
            shape_of(chunk, BF),
        ],
        [
            ((L, BLK), BF),
            ((L, BLK), BF),
            ((2 * L, L), BF),
            ((L, L), BF),
            ((BLK, 2 * L), BF),
            ((BLK, L), BF),
            ((2 * L, L), F32),
            ((L, L), F32),
        ],
        NODE_MIB,
        "svh" + "h" * len(shards) + "v",
        (scal, spread, ext, *shards, gain),
        flops=2 * BLK * 9 * L * L,
        sems=(2 + 4 * len(shards),),
    )


def run_edge_backward(scal, d_agg, cot, offsets, gain, saved, shards):
    rows = cot.shape[0]
    lat_size = d_agg.shape[0]
    chunk = (len(shards) // 2,) + shards[0].shape
    normed, inverse, first, joined, d_direct = saved
    return call(
        edge_backward,
        [
            shape_of((rows, L), BF),
            shape_of((lat_size, L, BLK), F32),
            shape_of((L, HB * BLK), BF),
            shape_of((L, HB * BLK), BF),
            shape_of(chunk, BF),
            shape_of(chunk, BF),
        ],
        [
            (joined.shape, BF),
            (first.shape, BF),
            (normed.shape, F32),
            (inverse.shape, F32),
            (d_direct.shape, F32),
            ((3 * L, L), BF),
            ((L, L), BF),
            ((rows, L), BF),
            ((rows, L), BF),
            ((lat_size + 2 * HB, L, BLK), F32),
            ((2 * L, rows), F32),
            ((3 * L, L), F32),
            ((L, L), F32),
        ],
        BACK_MIB,
        "svvvv" + "h" * (len(saved) + len(shards)),
        (scal, d_agg, cot, offsets, gain, *saved, *shards),
        flops=2 * rows * 8 * L * L,
        sems=(5 + 4 * len(shards),),
    )


def swap_cores(value):
    return lax.ppermute(value, "c", [(0, 1), (1, 0)])


def shift(value, axes, step):
    count = lax.axis_size(axes)
    return lax.ppermute(value, axes, [(i, (i + step) % count) for i in range(count)])


def shifts(value, axes):
    return [value] + [shift(value, axes, k) for k in range(1, lax.axis_size(axes))]


def spread_rows(value, axes):
    return lax.all_to_all(value, axes, 0, 0)


def gather_far(value):
    mine = shifts(value, "y")
    return mine + [swap_cores(one) for one in mine]


def reduce_far(keep, send):
    arrived = swap_cores(send)
    both = [(keep[k].astype(F32) + arrived[k].astype(F32)).astype(BF) for k in range(keep.shape[0])]
    return [both[0]] + [shift(both[k], "y", k) for k in range(1, keep.shape[0])]


def per_device(
    nodes,
    edges,
    edge_tiles,
    edge_offsets,
    tile_counts,
    halo_blocks,
    w_edge_in,
    w_edge_out,
    w_node_in,
    w_node_out,
    edge_gain,
    node_gain,
    node_cotangent,
    edge_cotangent,
):
    lat_size = lax.axis_size(LAT)
    place = [lax.axis_index(LAT), lax.axis_index("c"), lax.axis_index("y")]
    slab_rows, width = nodes.shape
    own_rows = slab_rows // lat_size
    halo_rows = HB * BLK
    ext_rows = slab_rows + 2 * halo_rows
    weights = (w_edge_in, w_edge_out, w_node_in, w_node_out)
    pieces = tuple(weight.shape[0] for weight in weights)
    edge_rows = 2 * lat_size * (pieces[0] + pieces[1])
    node_rows = 2 * lat_size * (pieces[2] + pieces[3])

    near_scal = jnp.stack([lax.axis_index("z"), lax.axis_index(XS)]).astype(jnp.int32)
    node_scal = jnp.stack(place).astype(jnp.int32)
    scal = jnp.concatenate([edge_tiles.reshape(-1), node_scal, tile_counts])
    halo = halo_blocks.reshape(-1)
    offsets = edge_offsets.reshape(2, -1, BLK)
    edge_gain_row = edge_gain.reshape(1, L)
    node_gain_row = node_gain.reshape(1, L)

    turned = nodes.T
    up, down, packed = call(
        prepare,
        [
            shape_of((width, halo_rows), BF),
            shape_of((width, halo_rows), BF),
            shape_of((32, L), BF),
        ],
        [],
        4,
        "svvvvv",
        (halo, turned, *weights),
    )
    from_lower = from_behind(up, 1)
    from_upper = from_behind(down, -1)

    near = shifts(jnp.concatenate(shifts(packed, XS), axis=0), "z")
    edge_part, node_part = call(
        functools.partial(assemble, pieces),
        [shape_of((edge_rows, L), BF), shape_of((node_rows, L), BF)],
        [((4, 128, L), BF), ((edge_rows, L), F32), ((node_rows, L), F32)],
        6,
        "svvvv",
        (near_scal, *near),
    )

    table = jnp.concatenate([from_lower, turned, from_upper], axis=1)
    cot = node_cotangent.T.reshape(width, lat_size, own_rows).transpose(1, 0, 2)
    message_out = jnp.concatenate(
        [jnp.broadcast_to(table, (lat_size,) + table.shape), cot], axis=2
    )
    edge_shards = gather_far(edge_part)
    ext = spread_rows(message_out, LAT).reshape(L, ext_rows + own_rows)

    joined, first, normed, inverse, new_edges, partial = run_edge_forward(
        scal, ext, edges, offsets, edge_shards, edge_gain_row, lat_size
    )
    node_shards = gather_far(node_part)
    spread = spread_rows(partial, LAT)
    second_out, d_direct, node_keep, node_send = run_node_step(
        node_scal, spread, ext, node_shards, node_gain_row
    )
    second_in = spread_rows(second_out, LAT)
    new_nodes = second_in[:, L:].transpose(1, 0, 2).reshape(width, slab_rows).T
    node_far = reduce_far(node_keep, node_send)
    second_in, *node_far = lax.optimization_barrier((second_in, *node_far))

    grad_edges, middle, lower, upper, edge_keep, edge_send = run_edge_backward(
        scal, second_in, edge_cotangent, offsets, edge_gain_row,
        (normed, inverse, first, joined, d_direct), edge_shards,
    )
    from_above = from_behind(lower, -1)
    from_below = from_behind(upper, 1)
    (columns,) = call(
        add_halo,
        [shape_of((lat_size, width, slab_rows), BF)],
        [((lat_size, L, BLK), F32)],
        8,
        "svvv",
        (halo, middle, from_above, from_below),
    )
    edge_far = reduce_far(edge_keep, edge_send)
    (grad_slab,) = call(
        finish, [shape_of((width, slab_rows), BF)], [], 4, "v", (spread_rows(columns, LAT),)
    )

    shard = (32, L)
    shards = (4,) + shard
    kept, *sent = call(
        functools.partial(sum_far, pieces),
        [shape_of(shards, F32)] + [shape_of(shards, BF)] * 3,
        [((edge_rows, L), F32), ((node_rows, L), F32), ((4,) + shards, F32)],
        8,
        "s" + "v" * 8,
        (near_scal, *edge_far, *node_far),
    )
    moved = [shift(sent[k - 1], "z", k) for k in range(1, 4)]
    kept, *sent = call(
        sum_z,
        [shape_of(shard, F32)] + [shape_of(shard, BF)] * 3,
        [(shards, F32)],
        4,
        "s" + "v" * 4,
        (near_scal, kept, *moved),
    )
    moved = [shift(sent[k - 1], XS, k) for k in range(1, 4)]
    reduced = call(
        sum_x, [shape_of((count, L), F32) for count in pieces], [], 4, "v" * 4, (kept, *moved)
    )
    return (new_nodes, new_edges, grad_slab.T, grad_edges) + tuple(reduced)


def solution(mesh):
    fine = Mesh(mesh.devices.reshape(4, 2, 2, 2, 4), ("y", "xl", "c", "xh", "z"))
    every = SLAB + LAT
    by_rows = P(every, None)
    split = P(SLAB, LAT)
    placed = (
        split,
        by_rows,
        P(None, every),
        P(None, every),
        P(SLAB),
        P(SLAB, None, None),
        by_rows,
        by_rows,
        by_rows,
        by_rows,
        P(),
        P(),
        split,
        by_rows,
    )
    return jax.shard_map(
        per_device,
        mesh=fine,
        in_specs=placed,
        out_specs=(split, by_rows, split, by_rows, by_rows, by_rows, by_rows, by_rows),
        check_vma=False,
    )
```

```python
import functools

import jax
import jax.numpy as jnp
from jax import lax
from jax.experimental import pallas as pl
from jax.experimental.pallas import tpu as pltpu
from jax.sharding import Mesh, PartitionSpec as P

L = 512
BLK = 128
HB = 2
EPSILON = 1e-05

SLAB = ("y", "xl", "c")
LAT = ("xh", "z")
XS = ("xl", "xh")
BF = jnp.bfloat16
F32 = jnp.float32
EDGE_MIB = 16
NODE_MIB = 14
BACK_MIB = 28


def shape_of(shape, dtype):
    return jax.ShapeDtypeStruct(shape, dtype)


def from_behind(value, steps):
    count = lax.axis_size(SLAB)
    first, last = (max(0, -steps), min(count, count - steps))
    return lax.ppermute(value, SLAB, [(source, source + steps) for source in range(first, last)])


def dot(left, right):
    return jnp.dot(left, right, preferred_element_type=F32)


def dot_rows(left, right):
    return lax.dot_general(left, right, (((0,), (0,)), ((), ())), preferred_element_type=F32)


def dot_transpose(left, right):
    return lax.dot_general(left, right, (((1,), (1,)), ((), ())), preferred_element_type=F32)


def one_hot_columns(offsets):
    cells = lax.broadcasted_iota(jnp.int32, (BLK, BLK), 0)
    return (cells == offsets).astype(F32)


def norm_parts(values):
    average = jnp.mean(values, axis=-1, keepdims=True)
    centred = values - average
    variance = jnp.mean(centred * centred, axis=-1, keepdims=True)
    inverse = lax.rsqrt(variance + EPSILON)
    return centred * inverse, inverse


def norm_back(upstream, normed, inverse, gain_vector):
    scaled = upstream * gain_vector
    return inverse * (
        scaled
        - jnp.mean(scaled, axis=-1, keepdims=True)
        - normed * jnp.mean(scaled * normed, axis=-1, keepdims=True)
    )


def split_three(value):
    high = value.astype(BF)
    rest = value - high.astype(F32)
    middle = rest.astype(BF)
    return high, middle, (rest - middle.astype(F32)).astype(BF)


def block_at(number):
    return pl.ds(pl.multiple_of(number * BLK, BLK), BLK)


def copies(pairs, sems):
    made = [pltpu.make_async_copy(src, dst, sems.at[i]) for i, (src, dst) in enumerate(pairs)]
    for one in made:
        one.start()
    return made


def wait_all(made):
    for one in made:
        one.wait()


def weight_pairs(core, y_index, shards, outs, counts):
    total = sum(counts)
    y_count = len(shards) // 2
    pairs = []
    for number, source in enumerate(shards):
        step = number % y_count
        parity = core if number < y_count else 1 - core
        y = lax.rem(y_index - step + y_count, y_count)
        per = source.shape[0] // total
        for x in range(per):
            slab = (y * per + x) * 2 + parity
            at = x * total
            for out, count in zip(outs, counts):
                start = pl.multiple_of(slab * count, 32)
                pairs.append((source.at[pl.ds(at, count), :], out.at[pl.ds(start, count), :]))
                at += count
    return pairs


def pack_grads(core, y_index, grads, keep, send, counts):
    total = sum(counts)
    y_count = keep.shape[0]
    per = keep.shape[1] // total
    for target, parity in ((keep, core), (send, 1 - core)):
        for step in range(y_count):
            y = lax.rem(y_index + step, y_count)
            for x in range(per):
                at = x * total
                for grad, count in zip(grads, counts):
                    start = pl.multiple_of(((y * per + x) * 2 + parity) * count, 32)
                    target[step, pl.ds(at, count), :] = grad[pl.ds(start, count), :].astype(BF)
                    at += count


def prepare(halo, turned, *refs):
    weights, (up, down, packed), held, sems = refs[:4], refs[4:7], refs[7:-1], refs[-1]
    pairs = list(zip(weights, held))
    for j in range(HB):
        part = pl.ds(j * BLK, BLK)
        pairs.append((turned.at[:, block_at(halo[j])], up.at[:, part]))
        pairs.append((turned.at[:, block_at(halo[HB + j])], down.at[:, part]))
    wait_all(copies(pairs, sems))
    parts = [ref[...].astype(F32) for ref in held]
    used = sum(part.shape[0] for part in parts)
    parts.append(jnp.zeros((packed.shape[0] - used, L), F32))
    packed[...] = jnp.concatenate(parts, axis=0).astype(BF)


def assemble(pieces, scal, *refs):
    blocks, (edge_part, node_part, held, edge_rows, node_rows) = refs[:4], refs[4:]
    z_index, x_index = scal[0], scal[1]
    for k, block in enumerate(blocks):
        held[k] = block[...]
    outs = (edge_rows, edge_rows, node_rows, node_rows)
    bases = []
    for number, count in enumerate(pieces):
        bases.append(0 if number % 2 == 0 else bases[-1] + 8 * pieces[number - 1])
    sizes = (8 * (pieces[0] + pieces[1]), 8 * (pieces[2] + pieces[3]))
    for x in range(4):
        x_step = lax.rem(x_index - x + 4, 4)
        for z in range(4):
            z_step = lax.rem(z_index - z + 4, 4)
            shard = held[z_step, pl.ds(pl.multiple_of(x_step * 32, 32), 32), :].astype(F32)
            row, lat = 0, (x % 2) * 4 + z
            for number, count in enumerate(pieces):
                base = (x // 2) * sizes[number // 2] + bases[number] + lat * count
                outs[number][pl.ds(base, count), :] = shard[row : row + count]
                row += count
    edge_part[...] = edge_rows[...].astype(BF)
    node_part[...] = node_rows[...].astype(BF)


def sum_far(pieces, scal, edge_own, e1, e2, e3, node_own, n1, n2, n3, keep, s1, s2, s3, er, nr, sent):
    z_index = scal[0]
    er[...] = sum((ref[...].astype(F32) for ref in (e1, e2, e3)), edge_own[...].astype(F32))
    nr[...] = sum((ref[...].astype(F32) for ref in (n1, n2, n3)), node_own[...].astype(F32))
    ins = (er, er, nr, nr)
    bases = []
    for number, count in enumerate(pieces):
        bases.append(0 if number % 2 == 0 else bases[-1] + 8 * pieces[number - 1])
    sizes = (8 * (pieces[0] + pieces[1]), 8 * (pieces[2] + pieces[3]))
    spare = 32 - sum(pieces)
    for x in range(4):
        for z in range(4):
            lat = (x % 2) * 4 + z
            parts = []
            for number, count in enumerate(pieces):
                base = (x // 2) * sizes[number // 2] + bases[number] + lat * count
                parts.append(ins[number][pl.ds(base, count), :])
            parts.append(jnp.zeros((spare, L), F32))
            sent[z, x] = jnp.concatenate(parts, axis=0)
    keep[...] = sent[z_index]
    for step, out in ((1, s1), (2, s2), (3, s3)):
        out[...] = sent[lax.rem(z_index + step, 4)].astype(BF)


def sum_z(scal, own, r1, r2, r3, keep, s1, s2, s3, held):
    x_index = scal[1]
    held[...] = own[...] + (r1[...].astype(F32) + r2[...].astype(F32) + r3[...].astype(F32))
    keep[...] = held[x_index]
    for step, out in ((1, s1), (2, s2), (3, s3)):
        out[...] = held[lax.rem(x_index + step, 4)].astype(BF)


def sum_x(own, r1, r2, r3, *outs):
    total = own[...] + (r1[...].astype(F32) + r2[...].astype(F32) + r3[...].astype(F32))
    row = 0
    for out in outs:
        count = out.shape[0]
        out[...] = total[row : row + count]
        row += count


def edge_forward(scal, ext_hbm, edges, offsets, *refs):
    shards, refs = refs[:8], refs[8:]
    gain, joined_out, first_out, normed_out, inverse_out, new_edges_out, partial_out = refs[:7]
    ext, joined, first, normed, inverse, new_edges, partial, w_in, w_out, second = refs[7:17]
    sems, out_sems = refs[17:]
    tiles = edges.shape[0] // BLK
    lat_index, core, y_index, count = (scal[2 * tiles + i] for i in range(4))
    slabs = w_in.shape[0] // 3 // 32
    counts = (3 * L // slabs, L // slabs)
    pairs = [(ext_hbm, ext)] + weight_pairs(core, y_index, shards, (w_in, w_out), counts)
    loads = copies(pairs, sems)
    stores = []

    def store(source, target):
        copy = pltpu.make_async_copy(source, target, out_sems.at[len(stores)])
        copy.start()
        stores.append(copy)

    joined[:, pl.ds(0, L)] = edges[...]
    loads[0].wait()
    for t in range(tiles):
        rows = pl.ds(t * BLK, BLK)
        to_src = one_hot_columns(offsets[1, pl.ds(t, 1), :]).T.astype(BF)
        to_dst = one_hot_columns(offsets[0, pl.ds(t, 1), :]).T.astype(BF)
        src, dst = block_at(scal[tiles + t]), block_at(scal[t] + HB)
        joined[rows, pl.ds(L, L)] = dot_transpose(to_src, ext[:, src]).astype(BF)
        joined[rows, pl.ds(2 * L, L)] = dot_transpose(to_dst, ext[:, dst]).astype(BF)
    store(joined, joined_out)
    wait_all(loads[1:])
    for n in range(2):
        columns = pl.ds(n * 256, 256)
        first[:, columns] = jnp.maximum(dot(joined[...], w_in[:, columns]), 0.0).astype(BF)
    store(first, first_out)
    for n in range(2):
        columns = pl.ds(n * 256, 256)
        second[:, columns] = dot(first[...], w_out[:, columns])
    partial[...] = jnp.zeros_like(partial)
    for t in range(tiles):
        rows = pl.ds(t * BLK, BLK)
        live = (lat_index * tiles + t < count).astype(F32)
        values, inv = norm_parts(second[rows, :])
        normed[rows, :] = values
        inverse[rows, :] = jnp.broadcast_to(inv, (BLK, BLK))
        message = values * gain[...] * live
        new_edges[rows, :] = (edges[rows, :].astype(F32) + message).astype(BF)
        second[rows, :] = message
    store(normed, normed_out)
    store(inverse, inverse_out)
    store(new_edges, new_edges_out)
    for t in range(tiles):
        rows = pl.ds(t * BLK, BLK)
        into = one_hot_columns(offsets[0, pl.ds(t, 1), :]).astype(BF)
        high, middle, low = split_three(second[rows, :])
        block = scal[t]
        partial[block] = partial[block] + (dot(into, low) + dot(into, middle) + dot(into, high))
    store(partial, partial_out)
    wait_all(stores)


def node_step(scal, spread, ext_hbm, *refs):
    shards, refs = refs[:8], refs[8:]
    gain, out, direct_out, keep, send = refs[:5]
    own_turned, up_turned, w_in, w_out, joined, first, g_in, g_out, d_direct, sems, out_sems = refs[5:]
    lat_index, core, y_index = scal[0], scal[1], scal[2]
    slabs = w_in.shape[0] // 2 // 32
    counts = (2 * L // slabs, L // slabs)
    pairs = [
        (ext_hbm.at[:, block_at(HB + lat_index)], own_turned),
        (ext_hbm.at[:, pl.ds(ext_hbm.shape[1] - BLK, BLK)], up_turned),
    ] + weight_pairs(core, y_index, shards, (w_in, w_out), counts)
    loads = copies(pairs, sems)
    total = spread[0]
    for l in range(1, spread.shape[0]):
        total = total + spread[l]
    joined[:, pl.ds(L, L)] = total.astype(BF)
    wait_all(loads)
    own = own_turned[...].astype(F32).T
    upstream = up_turned[...].astype(F32).T
    joined[:, pl.ds(0, L)] = own.astype(BF)
    first[...] = jnp.maximum(dot(joined[...], w_in[...]), 0.0).astype(BF)
    normed, inverse = norm_parts(dot(first[...], w_out[...]))
    new_rows = (own + normed * gain[...]).T.astype(BF)
    d_second = norm_back(upstream, normed, inverse, gain[...]).astype(BF)
    d_first = dot_transpose(d_second, w_out[...])
    d_first = jnp.where(first[...].astype(F32) > 0, d_first, 0.0).astype(BF)
    d_direct[...] = dot_transpose(w_in[pl.ds(0, L), :], d_first)
    store = copies([(d_direct, direct_out)], out_sems)
    d_agg = dot_transpose(w_in[pl.ds(L, L), :], d_first).astype(BF)
    width = L // out.shape[0]
    for l in range(out.shape[0]):
        out[l, pl.ds(0, L), :] = d_agg
        out[l, pl.ds(L, width), :] = new_rows[l * width : (l + 1) * width, :]
    g_out[...] = dot_rows(first[...], d_second)
    g_in[...] = dot_rows(joined[...], d_first)
    pack_grads(core, y_index, (g_in, g_out), keep, send, counts)
    wait_all(store)


def edge_backward(scal, d_agg, cot, offsets, gain, *refs):
    saved, w_out_shards, refs = refs[:4], refs[4:12], refs[12:]
    d_first, keep, send = refs[:3]
    joined, first, normed, inverse, w_in, w_out, d_second, g_in, g_out, sems = refs[3:]
    tiles = cot.shape[0] // BLK
    lat_index, core, y_index, count = (scal[2 * tiles + i] for i in range(4))
    slabs = w_in.shape[0] // 3 // 32
    counts = (3 * L // slabs, L // slabs)
    normed_in, inverse_in, first_in, joined_in = saved
    pairs = [(normed_in, normed), (inverse_in, inverse)]
    pairs += weight_pairs(core, y_index, w_out_shards, (w_in, w_out), counts)[1::2]
    pairs += [(first_in, first), (joined_in, joined)]
    loads = copies(pairs, sems)
    wait_all(loads[:2])
    for t in range(tiles):
        rows = pl.ds(t * BLK, BLK)
        live = (lat_index * tiles + t < count).astype(F32)
        to_dst = one_hot_columns(offsets[0, pl.ds(t, 1), :]).T.astype(BF)
        picked = dot_transpose(to_dst, d_agg[scal[t], pl.ds(0, L), :])
        d_message = (cot[rows, :].astype(F32) + picked) * live
        back = norm_back(d_message, normed[rows, :], inverse[rows, pl.ds(0, 1)], gain[...])
        d_second[rows, :] = back.astype(BF)
    wait_all(loads[2:])
    for n in range(2):
        part = pl.ds(n * 256, 256)
        back = dot_transpose(d_second[...], w_out[part, :])
        d_first[:, part] = jnp.where(first[:, part].astype(F32) > 0, back, 0.0).astype(BF)
    for n in range(2):
        part = pl.ds(n * 256, 256)
        g_out[part, :] = dot_rows(first[:, part], d_second[...])
    for n in range(6):
        part = pl.ds(n * 256, 256)
        g_in[part, :] = dot_rows(joined[:, part], d_first[...])
    pack_grads(core, y_index, (g_in, g_out), keep, send, counts)


def edge_inputs(scal, d_first, cot, offsets, direct_in, *refs):
    shards, refs = refs[:8], refs[8:]
    grad_out, middle_out, lower, upper = refs[:4]
    grad_edges, d_direct, w_in, w_out, d_ext, d_turned, sems, out_sems = refs[4:]
    tiles = cot.shape[0] // BLK
    lat_index, core, y_index = (scal[2 * tiles + i] for i in range(3))
    slabs = w_in.shape[0] // 3 // 32
    counts = (3 * L // slabs, L // slabs)
    pairs = weight_pairs(core, y_index, shards, (w_in, w_out), counts)[::2]
    pairs += [(direct_in, d_direct)]
    loads = copies(pairs, sems)
    d_ext[...] = jnp.zeros_like(d_ext)
    wait_all(loads)
    for n in range(4):
        d_turned[pl.ds(n * 256, 256), :] = dot_transpose(
            w_in[pl.ds(L + n * 256, 256), :], d_first[...]
        )
    for n in range(2):
        part = pl.ds(n * 256, 256)
        back = dot_transpose(d_first[...], w_in[part, :])
        grad_edges[:, part] = (cot[:, part].astype(F32) + back).astype(BF)
    store = copies([(grad_edges, grad_out)], out_sems)
    for t in range(tiles):
        rows = pl.ds(t * BLK, BLK)
        for row, place, at in ((1, scal[tiles + t], 0), (0, scal[t] + HB, L)):
            into = one_hot_columns(offsets[row, pl.ds(t, 1), :]).T.astype(BF)
            value = d_turned[pl.ds(at, L), rows]
            high = value.astype(BF)
            low = (value - high.astype(F32)).astype(BF)
            d_ext[place] = d_ext[place] + (dot(low, into) + dot(high, into))
    d_ext[HB + lat_index] = d_ext[HB + lat_index] + d_direct[...]
    blocks = middle_out.shape[0]
    for j in range(HB):
        lower[:, pl.ds(j * BLK, BLK)] = d_ext[j].astype(BF)
        upper[:, pl.ds(j * BLK, BLK)] = d_ext[HB + blocks + j].astype(BF)
    middle_out[...] = d_ext[pl.ds(HB, blocks)]
    wait_all(store)


def add_halo(halo, middle, above, below, columns, held):
    held[...] = middle[...]
    for j in range(HB):
        for place, value in ((halo[j], above), (halo[HB + j], below)):
            held[place] = held[place] + value[:, pl.ds(j * BLK, BLK)].astype(F32)
    width = columns.shape[1]
    for block in range(held.shape[0]):
        for l in range(columns.shape[0]):
            columns[l, :, pl.ds(block * BLK, BLK)] = held[
                block, pl.ds(l * width, width), :
            ].astype(BF)


def finish(arrived, out):
    total = arrived[0].astype(F32)
    for l in range(1, arrived.shape[0]):
        total = total + arrived[l].astype(F32)
    out[...] = total.astype(BF)


def call(kernel, out_shape, scratch, mib, spaces, operands, flops=0, out_spaces="", sems=()):
    moved = sum(x.size * x.dtype.itemsize for x in operands)
    moved += sum(x.size * x.dtype.itemsize for x in out_shape)
    named = {"s": pltpu.SMEM, "v": pltpu.VMEM, "h": pltpu.HBM}
    out_spaces = out_spaces or "v" * len(out_shape)
    operands = [
        pltpu.with_memory_space_constraint(x, pltpu.HBM) if space == "h" else x
        for x, space in zip(operands, spaces)
    ]
    placed = [
        pltpu.HBM(x.shape, x.dtype) if space == "h" else x
        for x, space in zip(out_shape, out_spaces)
    ]
    return pl.pallas_call(
        kernel,
        out_shape=placed,
        in_specs=[pl.BlockSpec(memory_space=named[space]) for space in spaces],
        out_specs=[pl.BlockSpec(memory_space=named[space]) for space in out_spaces],
        scratch_shapes=[pltpu.VMEM(shape, dtype) for shape, dtype in scratch]
        + [pltpu.SemaphoreType.DMA((count,)) for count in sems],
        cost_estimate=pl.CostEstimate(flops=flops, bytes_accessed=moved, transcendentals=0),
        compiler_params=pltpu.CompilerParams(vmem_limit_bytes=mib << 20),
    )(*operands)


def run_edge_forward(scal, ext, edges, offsets, shards, gain, lat_size):
    rows = edges.shape[0]
    outs = [
        shape_of((rows, 3 * L), BF),
        shape_of((rows, L), BF),
        shape_of((rows, L), F32),
        shape_of((rows, BLK), F32),
        shape_of((rows, L), BF),
        shape_of((lat_size, BLK, L), F32),
    ]
    held = [(ext.shape, BF)] + [(out.shape, out.dtype) for out in outs]
    return call(
        edge_forward,
        outs,
        held + [((3 * L, L), BF), ((L, L), BF), ((rows, L), F32)],
        EDGE_MIB,
        "shvv" + "h" * len(shards) + "v",
        (scal, ext, edges, offsets, *shards, gain),
        flops=2 * rows * 4 * L * L,
        out_spaces="h" * len(outs),
        sems=(1 + 4 * len(shards), len(outs)),
    )


def run_node_step(scal, spread, ext, shards, gain):
    lat_size = spread.shape[0]
    chunk = (len(shards) // 2,) + shards[0].shape
    return call(
        node_step,
        [
            shape_of((lat_size, L + L // lat_size, BLK), BF),
            shape_of((L, BLK), F32),
            shape_of(chunk, BF),
            shape_of(chunk, BF),
        ],
        [
            ((L, BLK), BF),
            ((L, BLK), BF),
            ((2 * L, L), BF),
            ((L, L), BF),
            ((BLK, 2 * L), BF),
            ((BLK, L), BF),
            ((2 * L, L), F32),
            ((L, L), F32),
            ((L, BLK), F32),
        ],
        NODE_MIB,
        "svh" + "h" * len(shards) + "v",
        (scal, spread, ext, *shards, gain),
        flops=2 * BLK * 9 * L * L,
        out_spaces="vhvv",
        sems=(2 + 4 * len(shards), 1),
    )


def run_edge_backward(scal, d_agg, cot, offsets, gain, saved, shards):
    rows = cot.shape[0]
    chunk = (len(shards) // 2,) + shards[0].shape
    normed, inverse, first, joined = saved
    return call(
        edge_backward,
        [shape_of((rows, L), BF), shape_of(chunk, BF), shape_of(chunk, BF)],
        [
            (joined.shape, BF),
            (first.shape, BF),
            (normed.shape, F32),
            (inverse.shape, F32),
            ((3 * L, L), BF),
            ((L, L), BF),
            ((rows, L), BF),
            ((3 * L, L), F32),
            ((L, L), F32),
        ],
        BACK_MIB,
        "svvvv" + "h" * (len(saved) + len(shards)),
        (scal, d_agg, cot, offsets, gain, *saved, *shards),
        flops=2 * rows * 5 * L * L,
        sems=(4 + 2 * len(shards),),
    )


def run_edge_inputs(scal, d_first, cot, offsets, d_direct, shards, lat_size):
    rows = cot.shape[0]
    return call(
        edge_inputs,
        [
            shape_of((rows, L), BF),
            shape_of((lat_size, L, BLK), F32),
            shape_of((L, HB * BLK), BF),
            shape_of((L, HB * BLK), BF),
        ],
        [
            ((rows, L), BF),
            (d_direct.shape, F32),
            ((3 * L, L), BF),
            ((L, L), BF),
            ((lat_size + 2 * HB, L, BLK), F32),
            ((2 * L, rows), F32),
        ],
        EDGE_MIB,
        "svvvh" + "h" * len(shards),
        (scal, d_first, cot, offsets, d_direct, *shards),
        flops=2 * rows * 3 * L * L,
        out_spaces="hvvv",
        sems=(1 + 2 * len(shards), 1),
    )


def swap_cores(value):
    return lax.ppermute(value, "c", [(0, 1), (1, 0)])


def shift(value, axes, step):
    count = lax.axis_size(axes)
    return lax.ppermute(value, axes, [(i, (i + step) % count) for i in range(count)])


def shifts(value, axes):
    return [value] + [shift(value, axes, k) for k in range(1, lax.axis_size(axes))]


def spread_rows(value, axes):
    return lax.all_to_all(value, axes, 0, 0)


def gather_far(value):
    mine = shifts(value, "y")
    return mine + [swap_cores(one) for one in mine]


def reduce_far(keep, send):
    arrived = swap_cores(send)
    both = [(keep[k].astype(F32) + arrived[k].astype(F32)).astype(BF) for k in range(keep.shape[0])]
    return [both[0]] + [shift(both[k], "y", k) for k in range(1, keep.shape[0])]


def per_device(
    nodes,
    edges,
    edge_tiles,
    edge_offsets,
    tile_counts,
    halo_blocks,
    w_edge_in,
    w_edge_out,
    w_node_in,
    w_node_out,
    edge_gain,
    node_gain,
    node_cotangent,
    edge_cotangent,
):
    lat_size = lax.axis_size(LAT)
    place = [lax.axis_index(LAT), lax.axis_index("c"), lax.axis_index("y")]
    slab_rows, width = nodes.shape
    own_rows = slab_rows // lat_size
    halo_rows = HB * BLK
    ext_rows = slab_rows + 2 * halo_rows
    weights = (w_edge_in, w_edge_out, w_node_in, w_node_out)
    pieces = tuple(weight.shape[0] for weight in weights)
    edge_rows = 2 * lat_size * (pieces[0] + pieces[1])
    node_rows = 2 * lat_size * (pieces[2] + pieces[3])

    near_scal = jnp.stack([lax.axis_index("z"), lax.axis_index(XS)]).astype(jnp.int32)
    node_scal = jnp.stack(place).astype(jnp.int32)
    scal = jnp.concatenate([edge_tiles.reshape(-1), node_scal, tile_counts])
    halo = halo_blocks.reshape(-1)
    offsets = edge_offsets.reshape(2, -1, BLK)
    edge_gain_row = edge_gain.reshape(1, L)
    node_gain_row = node_gain.reshape(1, L)

    turned = nodes.T
    up, down, packed = call(
        prepare,
        [
            shape_of((width, halo_rows), BF),
            shape_of((width, halo_rows), BF),
            shape_of((32, L), BF),
        ],
        [(weight.shape, BF) for weight in weights],
        4,
        "shhhhh",
        (halo, turned, *weights),
        sems=(4 + 2 * HB,),
    )
    from_lower = from_behind(up, 1)
    from_upper = from_behind(down, -1)

    near = shifts(jnp.concatenate(shifts(packed, XS), axis=0), "z")
    edge_part, node_part = call(
        functools.partial(assemble, pieces),
        [shape_of((edge_rows, L), BF), shape_of((node_rows, L), BF)],
        [((4, 128, L), BF), ((edge_rows, L), F32), ((node_rows, L), F32)],
        6,
        "svvvv",
        (near_scal, *near),
    )

    table = jnp.concatenate([from_lower, turned, from_upper], axis=1)
    cot = node_cotangent.T.reshape(width, lat_size, own_rows).transpose(1, 0, 2)
    message_out = jnp.concatenate(
        [jnp.broadcast_to(table, (lat_size,) + table.shape), cot], axis=2
    )
    message_out, edge_part, node_part = lax.optimization_barrier(
        (message_out, edge_part, node_part)
    )
    edge_shards = gather_far(edge_part)
    ext = spread_rows(message_out, LAT).reshape(L, ext_rows + own_rows)

    joined, first, normed, inverse, new_edges, partial = run_edge_forward(
        scal, ext, edges, offsets, edge_shards, edge_gain_row, lat_size
    )
    node_shards = gather_far(node_part)
    spread = spread_rows(partial, LAT)
    second_out, d_direct, node_keep, node_send = run_node_step(
        node_scal, spread, ext, node_shards, node_gain_row
    )
    second_in = spread_rows(second_out, LAT)
    new_nodes = second_in[:, L:].transpose(1, 0, 2).reshape(width, slab_rows).T
    node_far = reduce_far(node_keep, node_send)
    second_in, *node_far = lax.optimization_barrier((second_in, *node_far))

    d_first, edge_keep, edge_send = run_edge_backward(
        scal, second_in, edge_cotangent, offsets, edge_gain_row,
        (normed, inverse, first, joined), edge_shards,
    )
    grad_edges, middle, lower, upper = run_edge_inputs(
        scal, d_first, edge_cotangent, offsets, d_direct, edge_shards, lat_size
    )
    from_above = from_behind(lower, -1)
    from_below = from_behind(upper, 1)
    (columns,) = call(
        add_halo,
        [shape_of((lat_size, width, slab_rows), BF)],
        [((lat_size, L, BLK), F32)],
        8,
        "svvv",
        (halo, middle, from_above, from_below),
    )
    edge_far = reduce_far(edge_keep, edge_send)
    (grad_slab,) = call(
        finish, [shape_of((width, slab_rows), BF)], [], 4, "v", (spread_rows(columns, LAT),)
    )

    shard = (32, L)
    shards = (4,) + shard
    kept, *sent = call(
        functools.partial(sum_far, pieces),
        [shape_of(shards, F32)] + [shape_of(shards, BF)] * 3,
        [((edge_rows, L), F32), ((node_rows, L), F32), ((4,) + shards, F32)],
        8,
        "s" + "v" * 8,
        (near_scal, *edge_far, *node_far),
    )
    moved = [shift(sent[k - 1], "z", k) for k in range(1, 4)]
    kept, *sent = call(
        sum_z,
        [shape_of(shard, F32)] + [shape_of(shard, BF)] * 3,
        [(shards, F32)],
        4,
        "s" + "v" * 4,
        (near_scal, kept, *moved),
    )
    moved = [shift(sent[k - 1], XS, k) for k in range(1, 4)]
    reduced = call(
        sum_x, [shape_of((count, L), F32) for count in pieces], [], 4, "v" * 4, (kept, *moved)
    )
    return (new_nodes, new_edges, grad_slab.T, grad_edges) + tuple(reduced)


def solution(mesh):
    fine = Mesh(mesh.devices.reshape(4, 2, 2, 2, 4), ("y", "xl", "c", "xh", "z"))
    every = SLAB + LAT
    by_rows = P(every, None)
    split = P(SLAB, LAT)
    placed = (
        split,
        by_rows,
        P(None, every),
        P(None, every),
        P(SLAB),
        P(SLAB, None, None),
        by_rows,
        by_rows,
        by_rows,
        by_rows,
        P(),
        P(),
        split,
        by_rows,
    )
    return jax.shard_map(
        per_device,
        mesh=fine,
        in_specs=placed,
        out_specs=(split, by_rows, split, by_rows, by_rows, by_rows, by_rows, by_rows),
        check_vma=False,
    )
```

```python
import functools

import jax
import jax.numpy as jnp
from jax import lax
from jax.experimental import pallas as pl
from jax.experimental.pallas import tpu as pltpu
from jax.sharding import Mesh, PartitionSpec as P


L = 512
BLK = 128
HB = 2
EPSILON = 1e-05

SLAB = ("y", "xl", "c")
LAT = ("xh", "z")
XS = ("xl", "xh")
BF = jnp.bfloat16
F32 = jnp.float32
EDGE_MIB = 16
NODE_MIB = 14
BACK_MIB = 28


def shape_of(shape, dtype):
    return jax.ShapeDtypeStruct(shape, dtype)


def from_behind(value, steps):
    count = lax.axis_size(SLAB)
    first, last = (max(0, -steps), min(count, count - steps))
    return lax.ppermute(value, SLAB, [(source, source + steps) for source in range(first, last)])


def dot(left, right):
    return jnp.dot(left, right, preferred_element_type=F32)


def dot_rows(left, right):
    return lax.dot_general(left, right, (((0,), (0,)), ((), ())), preferred_element_type=F32)


def dot_transpose(left, right):
    return lax.dot_general(left, right, (((1,), (1,)), ((), ())), preferred_element_type=F32)


def one_hot_columns(offsets):
    cells = lax.broadcasted_iota(jnp.int32, (BLK, BLK), 0)
    return (cells == offsets).astype(F32)


def norm_parts(values):
    average = jnp.mean(values, axis=-1, keepdims=True)
    centred = values - average
    variance = jnp.mean(centred * centred, axis=-1, keepdims=True)
    inverse = lax.rsqrt(variance + EPSILON)
    return centred * inverse, inverse


def norm_back(upstream, normed, inverse, gain_vector):
    scaled = upstream * gain_vector
    return inverse * (
        scaled
        - jnp.mean(scaled, axis=-1, keepdims=True)
        - normed * jnp.mean(scaled * normed, axis=-1, keepdims=True)
    )


def split_three(value):
    high = value.astype(BF)
    rest = value - high.astype(F32)
    middle = rest.astype(BF)
    return high, middle, (rest - middle.astype(F32)).astype(BF)


def block_at(number):
    return pl.ds(pl.multiple_of(number * BLK, BLK), BLK)


def copies(pairs, sems):
    made = [pltpu.make_async_copy(src, dst, sems.at[i]) for i, (src, dst) in enumerate(pairs)]
    for one in made:
        one.start()
    return made


def wait_all(made):
    for one in made:
        one.wait()


def weight_pairs(core, y_index, shards, outs, counts):
    total = sum(counts)
    y_count = len(shards) // 2
    pairs = []
    for number, source in enumerate(shards):
        step = number % y_count
        parity = core if number < y_count else 1 - core
        y = lax.rem(y_index - step + y_count, y_count)
        per = source.shape[0] // total
        for x in range(per):
            slab = (y * per + x) * 2 + parity
            at = x * total
            for out, count in zip(outs, counts):
                start = pl.multiple_of(slab * count, 32)
                pairs.append((source.at[pl.ds(at, count), :], out.at[pl.ds(start, count), :]))
                at += count
    return pairs


def pack_grads(core, y_index, grads, keep, send, counts):
    total = sum(counts)
    y_count = keep.shape[0]
    per = keep.shape[1] // total
    for target, parity in ((keep, core), (send, 1 - core)):
        for step in range(y_count):
            y = lax.rem(y_index + step, y_count)
            for x in range(per):
                at = x * total
                for grad, count in zip(grads, counts):
                    start = pl.multiple_of(((y * per + x) * 2 + parity) * count, 32)
                    target[step, pl.ds(at, count), :] = grad[pl.ds(start, count), :].astype(BF)
                    at += count


def prepare(halo, turned, *refs):
    weights, (up, down, packed), held, sems = refs[:4], refs[4:7], refs[7:-1], refs[-1]
    pairs = list(zip(weights, held))
    for j in range(HB):
        part = pl.ds(j * BLK, BLK)
        pairs.append((turned.at[:, block_at(halo[j])], up.at[:, part]))
        pairs.append((turned.at[:, block_at(halo[HB + j])], down.at[:, part]))
    wait_all(copies(pairs, sems))
    parts = [ref[...].astype(F32) for ref in held]
    used = sum(part.shape[0] for part in parts)
    parts.append(jnp.zeros((packed.shape[0] - used, L), F32))
    packed[...] = jnp.concatenate(parts, axis=0).astype(BF)


def assemble(pieces, scal, *refs):
    blocks, (edge_part, node_part, held, edge_rows, node_rows) = refs[:4], refs[4:]
    z_index, x_index = scal[0], scal[1]
    for k, block in enumerate(blocks):
        held[k] = block[...]
    outs = (edge_rows, edge_rows, node_rows, node_rows)
    bases = []
    for number, count in enumerate(pieces):
        bases.append(0 if number % 2 == 0 else bases[-1] + 8 * pieces[number - 1])
    sizes = (8 * (pieces[0] + pieces[1]), 8 * (pieces[2] + pieces[3]))
    for x in range(4):
        x_step = lax.rem(x_index - x + 4, 4)
        for z in range(4):
            z_step = lax.rem(z_index - z + 4, 4)
            shard = held[z_step, pl.ds(pl.multiple_of(x_step * 32, 32), 32), :].astype(F32)
            row, lat = 0, (x % 2) * 4 + z
            for number, count in enumerate(pieces):
                base = (x // 2) * sizes[number // 2] + bases[number] + lat * count
                outs[number][pl.ds(base, count), :] = shard[row : row + count]
                row += count
    edge_part[...] = edge_rows[...].astype(BF)
    node_part[...] = node_rows[...].astype(BF)


def sum_far(pieces, scal, edge_own, e1, e2, e3, node_own, n1, n2, n3, keep, s1, s2, s3, er, nr, sent):
    z_index = scal[0]
    er[...] = sum((ref[...].astype(F32) for ref in (e1, e2, e3)), edge_own[...].astype(F32))
    nr[...] = sum((ref[...].astype(F32) for ref in (n1, n2, n3)), node_own[...].astype(F32))
    ins = (er, er, nr, nr)
    bases = []
    for number, count in enumerate(pieces):
        bases.append(0 if number % 2 == 0 else bases[-1] + 8 * pieces[number - 1])
    sizes = (8 * (pieces[0] + pieces[1]), 8 * (pieces[2] + pieces[3]))
    spare = 32 - sum(pieces)
    for x in range(4):
        for z in range(4):
            lat = (x % 2) * 4 + z
            parts = []
            for number, count in enumerate(pieces):
                base = (x // 2) * sizes[number // 2] + bases[number] + lat * count
                parts.append(ins[number][pl.ds(base, count), :])
            parts.append(jnp.zeros((spare, L), F32))
            sent[z, x] = jnp.concatenate(parts, axis=0)
    keep[...] = sent[z_index]
    for step, out in ((1, s1), (2, s2), (3, s3)):
        out[...] = sent[lax.rem(z_index + step, 4)].astype(BF)


def sum_z(scal, own, r1, r2, r3, keep, s1, s2, s3, held):
    x_index = scal[1]
    held[...] = own[...] + (r1[...].astype(F32) + r2[...].astype(F32) + r3[...].astype(F32))
    keep[...] = held[x_index]
    for step, out in ((1, s1), (2, s2), (3, s3)):
        out[...] = held[lax.rem(x_index + step, 4)].astype(BF)


def sum_x(own, r1, r2, r3, *outs):
    total = own[...] + (r1[...].astype(F32) + r2[...].astype(F32) + r3[...].astype(F32))
    row = 0
    for out in outs:
        count = out.shape[0]
        out[...] = total[row : row + count]
        row += count


def edge_forward(scal, ext, edges, offsets, *refs):
    shards, refs = refs[:8], refs[8:]
    gain, joined_out, first_out, normed_out, inverse_out, new_edges_out, partial_out = refs[:7]
    own_out, up_out, refs = refs[7], refs[8], refs[9:]
    joined, first, normed, inverse, new_edges, partial, w_in, w_out, second, sems, out_sems = refs
    tiles = edges.shape[0] // BLK
    lat_index, core, y_index, count = (scal[2 * tiles + i] for i in range(4))
    slabs = w_in.shape[0] // 3 // 32
    counts = (3 * L // slabs, L // slabs)
    loads = copies(weight_pairs(core, y_index, shards, (w_in, w_out), counts), sems)
    stores = []

    def store(source, target):
        copy = pltpu.make_async_copy(source, target, out_sems.at[len(stores)])
        copy.start()
        stores.append(copy)

    store(ext.at[:, block_at(HB + lat_index)], own_out)
    store(ext.at[:, pl.ds(ext.shape[1] - BLK, BLK)], up_out)
    joined[:, pl.ds(0, L)] = edges[...]
    for t in range(tiles):
        rows = pl.ds(t * BLK, BLK)
        to_src = one_hot_columns(offsets[1, pl.ds(t, 1), :]).T.astype(BF)
        to_dst = one_hot_columns(offsets[0, pl.ds(t, 1), :]).T.astype(BF)
        src, dst = block_at(scal[tiles + t]), block_at(scal[t] + HB)
        joined[rows, pl.ds(L, L)] = dot_transpose(to_src, ext[:, src]).astype(BF)
        joined[rows, pl.ds(2 * L, L)] = dot_transpose(to_dst, ext[:, dst]).astype(BF)
    store(joined, joined_out)
    wait_all(loads)
    for n in range(2):
        columns = pl.ds(n * 256, 256)
        first[:, columns] = jnp.maximum(dot(joined[...], w_in[:, columns]), 0.0).astype(BF)
    store(first, first_out)
    for n in range(2):
        columns = pl.ds(n * 256, 256)
        second[:, columns] = dot(first[...], w_out[:, columns])
    partial[...] = jnp.zeros_like(partial)
    for t in range(tiles):
        rows = pl.ds(t * BLK, BLK)
        live = (lat_index * tiles + t < count).astype(F32)
        values, inv = norm_parts(second[rows, :])
        normed[rows, :] = values
        inverse[rows, :] = jnp.broadcast_to(inv, (BLK, BLK))
        message = values * gain[...] * live
        new_edges[rows, :] = (edges[rows, :].astype(F32) + message).astype(BF)
        second[rows, :] = message
    store(normed, normed_out)
    store(inverse, inverse_out)
    store(new_edges, new_edges_out)
    for t in range(tiles):
        rows = pl.ds(t * BLK, BLK)
        into = one_hot_columns(offsets[0, pl.ds(t, 1), :]).astype(BF)
        high, middle, low = split_three(second[rows, :])
        block = scal[t]
        partial[block] = partial[block] + (dot(into, low) + dot(into, middle) + dot(into, high))
    store(partial, partial_out)
    wait_all(stores)


def node_step(scal, spread, own_hbm, up_hbm, *refs):
    shards, refs = refs[:8], refs[8:]
    gain, out, direct_out, joined_out, first_out, d_second_out, d_first_out = refs[:7]
    own_turned, up_turned, w_in, w_out, joined, first, d_second, d_first, d_direct = refs[7:16]
    sems, out_sems = refs[16:]
    core, y_index = scal[1], scal[2]
    slabs = w_in.shape[0] // 2 // 32
    counts = (2 * L // slabs, L // slabs)
    pairs = [(own_hbm, own_turned), (up_hbm, up_turned)]
    pairs += weight_pairs(core, y_index, shards, (w_in, w_out), counts)
    loads = copies(pairs, sems)
    wait_all(loads[:2])
    own = own_turned[...].astype(F32).T
    upstream = up_turned[...].astype(F32).T
    joined[:, pl.ds(0, L)] = own.astype(BF)
    total = spread[0]
    for l in range(1, spread.shape[0]):
        total = total + spread[l]
    joined[:, pl.ds(L, L)] = total.astype(BF)
    wait_all(loads[2:])
    first[...] = jnp.maximum(dot(joined[...], w_in[...]), 0.0).astype(BF)
    normed, inverse = norm_parts(dot(first[...], w_out[...]))
    d_second[...] = norm_back(upstream, normed, inverse, gain[...]).astype(BF)
    back = dot_transpose(d_second[...], w_out[...])
    d_first[...] = jnp.where(first[...].astype(F32) > 0, back, 0.0).astype(BF)
    d_agg = dot_transpose(w_in[pl.ds(L, L), :], d_first[...]).astype(BF)
    new_rows = (own + normed * gain[...]).T.astype(BF)
    width = L // out.shape[0]
    for l in range(out.shape[0]):
        out[l, pl.ds(0, L), :] = d_agg
        out[l, pl.ds(L, width), :] = new_rows[l * width : (l + 1) * width, :]
    d_direct[...] = dot_transpose(w_in[pl.ds(0, L), :], d_first[...])
    held = (d_direct, joined, first, d_second, d_first)
    outs = (direct_out, joined_out, first_out, d_second_out, d_first_out)
    wait_all(copies(zip(held, outs), out_sems))


def node_grads(scal, *refs):
    saved, (keep, send), refs = refs[:4], refs[4:6], refs[6:]
    held, (g_in, g_out, sems) = refs[:4], refs[4:]
    wait_all(copies(zip(saved, held), sems))
    joined, first, d_second, d_first = held
    g_out[...] = dot_rows(first[...], d_second[...])
    g_in[...] = dot_rows(joined[...], d_first[...])
    slabs = g_in.shape[0] // 2 // 32
    pack_grads(scal[1], scal[2], (g_in, g_out), keep, send, (2 * L // slabs, L // slabs))


def edge_backward(scal, d_agg, cot, offsets, gain, *refs):
    saved, w_out_shards, refs = refs[:4], refs[4:12], refs[12:]
    d_first, keep, send = refs[:3]
    joined, first, normed, inverse, w_in, w_out, d_second, g_in, g_out, sems = refs[3:]
    tiles = cot.shape[0] // BLK
    lat_index, core, y_index, count = (scal[2 * tiles + i] for i in range(4))
    slabs = w_in.shape[0] // 3 // 32
    counts = (3 * L // slabs, L // slabs)
    normed_in, inverse_in, first_in, joined_in = saved
    pairs = [(normed_in, normed), (inverse_in, inverse)]
    pairs += weight_pairs(core, y_index, w_out_shards, (w_in, w_out), counts)[1::2]
    pairs += [(first_in, first), (joined_in, joined)]
    loads = copies(pairs, sems)
    wait_all(loads[:2])
    for t in range(tiles):
        rows = pl.ds(t * BLK, BLK)
        live = (lat_index * tiles + t < count).astype(F32)
        to_dst = one_hot_columns(offsets[0, pl.ds(t, 1), :]).T.astype(BF)
        picked = dot_transpose(to_dst, d_agg[scal[t], pl.ds(0, L), :])
        d_message = (cot[rows, :].astype(F32) + picked) * live
        back = norm_back(d_message, normed[rows, :], inverse[rows, pl.ds(0, 1)], gain[...])
        d_second[rows, :] = back.astype(BF)
    wait_all(loads[2:])
    for n in range(2):
        part = pl.ds(n * 256, 256)
        back = dot_transpose(d_second[...], w_out[part, :])
        d_first[:, part] = jnp.where(first[:, part].astype(F32) > 0, back, 0.0).astype(BF)
    for n in range(2):
        part = pl.ds(n * 256, 256)
        g_out[part, :] = dot_rows(first[:, part], d_second[...])
    for n in range(6):
        part = pl.ds(n * 256, 256)
        g_in[part, :] = dot_rows(joined[:, part], d_first[...])
    pack_grads(core, y_index, (g_in, g_out), keep, send, counts)


def edge_inputs(scal, d_first, cot, offsets, direct_in, *refs):
    shards, refs = refs[:8], refs[8:]
    grad_out, middle_out, lower, upper = refs[:4]
    grad_edges, d_direct, w_in, w_out, d_ext, d_turned, sems, out_sems = refs[4:]
    tiles = cot.shape[0] // BLK
    lat_index, core, y_index = (scal[2 * tiles + i] for i in range(3))
    slabs = w_in.shape[0] // 3 // 32
    counts = (3 * L // slabs, L // slabs)
    pairs = weight_pairs(core, y_index, shards, (w_in, w_out), counts)[::2]
    pairs += [(direct_in, d_direct)]
    loads = copies(pairs, sems)
    d_ext[...] = jnp.zeros_like(d_ext)
    wait_all(loads)
    for n in range(4):
        d_turned[pl.ds(n * 256, 256), :] = dot_transpose(
            w_in[pl.ds(L + n * 256, 256), :], d_first[...]
        )
    for n in range(2):
        part = pl.ds(n * 256, 256)
        back = dot_transpose(d_first[...], w_in[part, :])
        grad_edges[:, part] = (cot[:, part].astype(F32) + back).astype(BF)
    store = copies([(grad_edges, grad_out)], out_sems)
    for t in range(tiles):
        rows = pl.ds(t * BLK, BLK)
        for row, place, at in ((1, scal[tiles + t], 0), (0, scal[t] + HB, L)):
            into = one_hot_columns(offsets[row, pl.ds(t, 1), :]).T.astype(BF)
            value = d_turned[pl.ds(at, L), rows]
            high = value.astype(BF)
            low = (value - high.astype(F32)).astype(BF)
            d_ext[place] = d_ext[place] + (dot(low, into) + dot(high, into))
    d_ext[HB + lat_index] = d_ext[HB + lat_index] + d_direct[...]
    blocks = middle_out.shape[0]
    for j in range(HB):
        lower[:, pl.ds(j * BLK, BLK)] = d_ext[j].astype(BF)
        upper[:, pl.ds(j * BLK, BLK)] = d_ext[HB + blocks + j].astype(BF)
    middle_out[...] = d_ext[pl.ds(HB, blocks)]
    wait_all(store)


def add_halo(halo, middle, above, below, columns, held):
    held[...] = middle[...]
    for j in range(HB):
        for place, value in ((halo[j], above), (halo[HB + j], below)):
            held[place] = held[place] + value[:, pl.ds(j * BLK, BLK)].astype(F32)
    width = columns.shape[1]
    for block in range(held.shape[0]):
        for l in range(columns.shape[0]):
            columns[l, :, pl.ds(block * BLK, BLK)] = held[
                block, pl.ds(l * width, width), :
            ].astype(BF)


def finish(arrived, out):
    total = arrived[0].astype(F32)
    for l in range(1, arrived.shape[0]):
        total = total + arrived[l].astype(F32)
    out[...] = total.astype(BF)


def call(kernel, out_shape, scratch, mib, spaces, operands, flops=0, out_spaces="", sems=()):
    moved = sum(x.size * x.dtype.itemsize for x in operands)
    moved += sum(x.size * x.dtype.itemsize for x in out_shape)
    named = {"s": pltpu.SMEM, "v": pltpu.VMEM, "h": pltpu.HBM}
    out_spaces = out_spaces or "v" * len(out_shape)
    operands = [
        pltpu.with_memory_space_constraint(x, pltpu.HBM) if space == "h" else x
        for x, space in zip(operands, spaces)
    ]
    placed = [
        pltpu.HBM(x.shape, x.dtype) if space == "h" else x
        for x, space in zip(out_shape, out_spaces)
    ]
    return pl.pallas_call(
        kernel,
        out_shape=placed,
        in_specs=[pl.BlockSpec(memory_space=named[space]) for space in spaces],
        out_specs=[pl.BlockSpec(memory_space=named[space]) for space in out_spaces],
        scratch_shapes=[pltpu.VMEM(shape, dtype) for shape, dtype in scratch]
        + [pltpu.SemaphoreType.DMA((count,)) for count in sems],
        cost_estimate=pl.CostEstimate(flops=flops, bytes_accessed=moved, transcendentals=0),
        compiler_params=pltpu.CompilerParams(vmem_limit_bytes=mib << 20),
    )(*operands)


def run_edge_forward(scal, ext, edges, offsets, shards, gain, lat_size):
    rows = edges.shape[0]
    outs = [
        shape_of((rows, 3 * L), BF),
        shape_of((rows, L), BF),
        shape_of((rows, L), F32),
        shape_of((rows, BLK), F32),
        shape_of((rows, L), BF),
        shape_of((lat_size, BLK, L), F32),
    ]
    held = [(out.shape, out.dtype) for out in outs]
    outs += [shape_of((L, BLK), BF)] * 2
    return call(
        edge_forward,
        outs,
        held + [((3 * L, L), BF), ((L, L), BF), ((rows, L), F32)],
        EDGE_MIB,
        "svvv" + "h" * len(shards) + "v",
        (scal, ext, edges, offsets, *shards, gain),
        flops=2 * rows * 4 * L * L,
        out_spaces="h" * len(outs),
        sems=(4 * len(shards), len(outs)),
    )


def run_node_step(scal, spread, own, up, shards, gain):
    lat_size = spread.shape[0]
    rows = [((BLK, 2 * L), BF), ((BLK, L), BF), ((BLK, L), BF), ((BLK, L), BF)]
    return call(
        node_step,
        [shape_of((lat_size, L + L // lat_size, BLK), BF), shape_of((L, BLK), F32)]
        + [shape_of(*row) for row in rows],
        [((L, BLK), BF), ((L, BLK), BF), ((2 * L, L), BF), ((L, L), BF)]
        + rows
        + [((L, BLK), F32)],
        NODE_MIB,
        "svhh" + "h" * len(shards) + "v",
        (scal, spread, own, up, *shards, gain),
        flops=2 * BLK * 6 * L * L,
        out_spaces="vhhhhh",
        sems=(2 + 4 * len(shards), 5),
    )


def run_node_grads(scal, saved, shard, y_count):
    return call(
        node_grads,
        [shape_of((y_count,) + shard.shape, BF)] * 2,
        [(one.shape, BF) for one in saved] + [((2 * L, L), F32), ((L, L), F32)],
        NODE_MIB,
        "shhhh",
        (scal, *saved),
        flops=2 * BLK * 3 * L * L,
        sems=(4,),
    )


def run_edge_backward(scal, d_agg, cot, offsets, gain, saved, shards):
    rows = cot.shape[0]
    chunk = (len(shards) // 2,) + shards[0].shape
    normed, inverse, first, joined = saved
    return call(
        edge_backward,
        [shape_of((rows, L), BF), shape_of(chunk, BF), shape_of(chunk, BF)],
        [
            (joined.shape, BF),
            (first.shape, BF),
            (normed.shape, F32),
            (inverse.shape, F32),
            ((3 * L, L), BF),
            ((L, L), BF),
            ((rows, L), BF),
            ((3 * L, L), F32),
            ((L, L), F32),
        ],
        BACK_MIB,
        "svvvv" + "h" * (len(saved) + len(shards)),
        (scal, d_agg, cot, offsets, gain, *saved, *shards),
        flops=2 * rows * 5 * L * L,
        sems=(4 + 2 * len(shards),),
    )


def run_edge_inputs(scal, d_first, cot, offsets, d_direct, shards, lat_size):
    rows = cot.shape[0]
    return call(
        edge_inputs,
        [
            shape_of((rows, L), BF),
            shape_of((lat_size, L, BLK), F32),
            shape_of((L, HB * BLK), BF),
            shape_of((L, HB * BLK), BF),
        ],
        [
            ((rows, L), BF),
            (d_direct.shape, F32),
            ((3 * L, L), BF),
            ((L, L), BF),
            ((lat_size + 2 * HB, L, BLK), F32),
            ((2 * L, rows), F32),
        ],
        EDGE_MIB,
        "svvvh" + "h" * len(shards),
        (scal, d_first, cot, offsets, d_direct, *shards),
        flops=2 * rows * 3 * L * L,
        out_spaces="hvvv",
        sems=(1 + 2 * len(shards), 1),
    )


def swap_cores(value):
    return lax.ppermute(value, "c", [(0, 1), (1, 0)])


def shift(value, axes, step):
    count = lax.axis_size(axes)
    return lax.ppermute(value, axes, [(i, (i + step) % count) for i in range(count)])


def shifts(value, axes):
    return [value] + [shift(value, axes, k) for k in range(1, lax.axis_size(axes))]


def spread_rows(value, axes):
    return lax.all_to_all(value, axes, 0, 0)


def gather_far(value):
    mine = shifts(value, "y")
    return mine + [swap_cores(one) for one in mine]


def reduce_far(keep, send):
    arrived = swap_cores(send)
    both = [(keep[k].astype(F32) + arrived[k].astype(F32)).astype(BF) for k in range(keep.shape[0])]
    return [both[0]] + [shift(both[k], "y", k) for k in range(1, keep.shape[0])]


def per_device(
    nodes,
    edges,
    edge_tiles,
    edge_offsets,
    tile_counts,
    halo_blocks,
    w_edge_in,
    w_edge_out,
    w_node_in,
    w_node_out,
    edge_gain,
    node_gain,
    node_cotangent,
    edge_cotangent,
):
    lat_size = lax.axis_size(LAT)
    place = [lax.axis_index(LAT), lax.axis_index("c"), lax.axis_index("y")]
    slab_rows, width = nodes.shape
    own_rows = slab_rows // lat_size
    halo_rows = HB * BLK
    ext_rows = slab_rows + 2 * halo_rows
    weights = (w_edge_in, w_edge_out, w_node_in, w_node_out)
    pieces = tuple(weight.shape[0] for weight in weights)
    edge_rows = 2 * lat_size * (pieces[0] + pieces[1])
    node_rows = 2 * lat_size * (pieces[2] + pieces[3])

    near_scal = jnp.stack([lax.axis_index("z"), lax.axis_index(XS)]).astype(jnp.int32)
    node_scal = jnp.stack(place).astype(jnp.int32)
    scal = jnp.concatenate([edge_tiles.reshape(-1), node_scal, tile_counts])
    halo = halo_blocks.reshape(-1)
    offsets = edge_offsets.reshape(2, -1, BLK)
    edge_gain_row = edge_gain.reshape(1, L)
    node_gain_row = node_gain.reshape(1, L)

    turned = nodes.T
    up, down, packed = call(
        prepare,
        [
            shape_of((width, halo_rows), BF),
            shape_of((width, halo_rows), BF),
            shape_of((32, L), BF),
        ],
        [(weight.shape, BF) for weight in weights],
        4,
        "shhhhh",
        (halo, turned, *weights),
        sems=(4 + 2 * HB,),
    )
    from_lower = from_behind(up, 1)
    from_upper = from_behind(down, -1)

    table = jnp.concatenate([from_lower, turned, from_upper], axis=1)
    cot = node_cotangent.T.reshape(width, lat_size, own_rows).transpose(1, 0, 2)
    message_out = jnp.concatenate(
        [jnp.broadcast_to(table, (lat_size,) + table.shape), cot], axis=2
    )
    by_x = jnp.concatenate(shifts(packed, XS), axis=0)
    near = shifts(by_x, "z")
    edge_part, node_part = call(
        functools.partial(assemble, pieces),
        [shape_of((edge_rows, L), BF), shape_of((node_rows, L), BF)],
        [((4, 128, L), BF), ((edge_rows, L), F32), ((node_rows, L), F32)],
        6,
        "svvvv",
        (near_scal, *near),
    )

    edge_shards = gather_far(edge_part)
    ext = spread_rows(message_out, LAT).reshape(L, ext_rows + own_rows)

    joined, first, normed, inverse, new_edges, partial, own, node_up = run_edge_forward(
        scal, ext, edges, offsets, edge_shards, edge_gain_row, lat_size
    )
    node_shards = gather_far(node_part)
    spread = spread_rows(partial, LAT)
    second_out, d_direct, *node_saved = run_node_step(
        node_scal, spread, own, node_up, node_shards, node_gain_row
    )
    node_keep, node_send = run_node_grads(
        node_scal, node_saved, node_part, lax.axis_size("y")
    )
    second_in = spread_rows(second_out, LAT)
    new_nodes = second_in[:, L:].transpose(1, 0, 2).reshape(width, slab_rows).T
    node_far = reduce_far(node_keep, node_send)
    second_in, *node_far = lax.optimization_barrier((second_in, *node_far))

    d_first, edge_keep, edge_send = run_edge_backward(
        scal, second_in, edge_cotangent, offsets, edge_gain_row,
        (normed, inverse, first, joined), edge_shards,
    )
    grad_edges, middle, lower, upper = run_edge_inputs(
        scal, d_first, edge_cotangent, offsets, d_direct, edge_shards, lat_size
    )
    from_above = from_behind(lower, -1)
    from_below = from_behind(upper, 1)
    edge_far = reduce_far(edge_keep, edge_send)
    (columns,) = call(
        add_halo,
        [shape_of((lat_size, width, slab_rows), BF)],
        [((lat_size, L, BLK), F32)],
        8,
        "svvv",
        (halo, middle, from_above, from_below),
    )
    columns = spread_rows(columns, LAT)
    (grad_slab,) = call(finish, [shape_of((width, slab_rows), BF)], [], 4, "v", (columns,))

    shard = (32, L)
    shards = (4,) + shard
    kept, *sent = call(
        functools.partial(sum_far, pieces),
        [shape_of(shards, F32)] + [shape_of(shards, BF)] * 3,
        [((edge_rows, L), F32), ((node_rows, L), F32), ((4,) + shards, F32)],
        8,
        "s" + "v" * 8,
        (near_scal, *edge_far, *node_far),
    )
    moved = [shift(sent[k - 1], "z", k) for k in range(1, 4)]
    kept, *sent = call(
        sum_z,
        [shape_of(shard, F32)] + [shape_of(shard, BF)] * 3,
        [(shards, F32)],
        4,
        "s" + "v" * 4,
        (near_scal, kept, *moved),
    )
    moved = [shift(sent[k - 1], XS, k) for k in range(1, 4)]
    reduced = call(
        sum_x, [shape_of((count, L), F32) for count in pieces], [], 4, "v" * 4, (kept, *moved)
    )
    return (new_nodes, new_edges, grad_slab.T, grad_edges) + tuple(reduced)


def solution(mesh):
    fine = Mesh(mesh.devices.reshape(4, 2, 2, 2, 4), ("y", "xl", "c", "xh", "z"))
    every = SLAB + LAT
    by_rows = P(every, None)
    split = P(SLAB, LAT)
    placed = (
        split,
        by_rows,
        P(None, every),
        P(None, every),
        P(SLAB),
        P(SLAB, None, None),
        by_rows,
        by_rows,
        by_rows,
        by_rows,
        P(),
        P(),
        split,
        by_rows,
    )

    return jax.shard_map(
        per_device,
        mesh=fine,
        in_specs=placed,
        out_specs=(split, by_rows, split, by_rows, by_rows, by_rows, by_rows, by_rows),
        check_vma=False,
    )
```

```python
import functools

import jax
import jax.numpy as jnp
from jax import lax
from jax.experimental import pallas as pl
from jax.experimental.pallas import tpu as pltpu
from jax.sharding import Mesh, PartitionSpec as P


L = 512
BLK = 128
HB = 2
EPSILON = 1e-05

SLAB = ("y", "xl", "c")
LAT = ("xh", "z")
XS = ("xl", "xh")
BF = jnp.bfloat16
F32 = jnp.float32
EDGE_MIB = 16
NODE_MIB = 14
BACK_MIB = 28


def shape_of(shape, dtype):
    return jax.ShapeDtypeStruct(shape, dtype)


def from_behind(value, steps):
    count = lax.axis_size(SLAB)
    first, last = (max(0, -steps), min(count, count - steps))
    return lax.ppermute(value, SLAB, [(source, source + steps) for source in range(first, last)])


def dot(left, right):
    return jnp.dot(left, right, preferred_element_type=F32)


def dot_rows(left, right):
    return lax.dot_general(left, right, (((0,), (0,)), ((), ())), preferred_element_type=F32)


def dot_transpose(left, right):
    return lax.dot_general(left, right, (((1,), (1,)), ((), ())), preferred_element_type=F32)


def one_hot_columns(offsets):
    cells = lax.broadcasted_iota(jnp.int32, (BLK, BLK), 0)
    return (cells == offsets).astype(F32)


def norm_parts(values):
    average = jnp.mean(values, axis=-1, keepdims=True)
    centred = values - average
    variance = jnp.mean(centred * centred, axis=-1, keepdims=True)
    inverse = lax.rsqrt(variance + EPSILON)
    return centred * inverse, inverse


def norm_back(upstream, normed, inverse, gain_vector):
    scaled = upstream * gain_vector
    return inverse * (
        scaled
        - jnp.mean(scaled, axis=-1, keepdims=True)
        - normed * jnp.mean(scaled * normed, axis=-1, keepdims=True)
    )


def split_three(value):
    high = value.astype(BF)
    rest = value - high.astype(F32)
    middle = rest.astype(BF)
    return high, middle, (rest - middle.astype(F32)).astype(BF)


def block_at(number):
    return pl.ds(pl.multiple_of(number * BLK, BLK), BLK)


def copies(pairs, sems):
    made = [pltpu.make_async_copy(src, dst, sems.at[i]) for i, (src, dst) in enumerate(pairs)]
    for one in made:
        one.start()
    return made


def wait_all(made):
    for one in made:
        one.wait()


def weight_pairs(core, y_index, shards, outs, counts):
    total = sum(counts)
    y_count = len(shards) // 2
    pairs = []
    for number, source in enumerate(shards):
        step = number % y_count
        parity = core if number < y_count else 1 - core
        y = lax.rem(y_index - step + y_count, y_count)
        per = source.shape[0] // total
        for x in range(per):
            slab = (y * per + x) * 2 + parity
            at = x * total
            for out, count in zip(outs, counts):
                start = pl.multiple_of(slab * count, 32)
                pairs.append((source.at[pl.ds(at, count), :], out.at[pl.ds(start, count), :]))
                at += count
    return pairs


def unpack_weights(core, y_index, shards, outs, counts):
    for source, target in weight_pairs(core, y_index, shards, outs, counts):
        target[...] = source[...]


def pack_grads(core, y_index, grads, keep, send, counts):
    total = sum(counts)
    y_count = keep.shape[0]
    per = keep.shape[1] // total
    for target, parity in ((keep, core), (send, 1 - core)):
        for step in range(y_count):
            y = lax.rem(y_index + step, y_count)
            for x in range(per):
                at = x * total
                for grad, count in zip(grads, counts):
                    start = pl.multiple_of(((y * per + x) * 2 + parity) * count, 32)
                    target[step, pl.ds(at, count), :] = grad[pl.ds(start, count), :].astype(BF)
                    at += count


def prepare(halo, turned, *refs):
    weights, (up, down, packed), held, sems = refs[:4], refs[4:7], refs[7:-1], refs[-1]
    pairs = list(zip(weights, held))
    for j in range(HB):
        part = pl.ds(j * BLK, BLK)
        pairs.append((turned.at[:, block_at(halo[0, 0, j])], up.at[:, part]))
        pairs.append((turned.at[:, block_at(halo[0, 1, j])], down.at[:, part]))
    wait_all(copies(pairs, sems))
    parts = [ref[...].astype(F32) for ref in held]
    used = sum(part.shape[0] for part in parts)
    parts.append(jnp.zeros((packed.shape[0] - used, L), F32))
    packed[...] = jnp.concatenate(parts, axis=0).astype(BF)


def fill_message(lower, turned, upper, cot, out, table, held, in_sems, sems):
    rows, halo_rows = turned.shape[1], lower.shape[1]
    loads = copies([(turned, table.at[:, pl.ds(halo_rows, rows)]), (cot, held)], in_sems)
    table[:, pl.ds(0, halo_rows)] = lower[...]
    table[:, pl.ds(halo_rows + rows, halo_rows)] = upper[...]
    wait_all(loads)
    pairs = []
    for l in range(out.shape[0]):
        pairs.append((table, out.at[l, :, pl.ds(0, table.shape[1])]))
        part = out.at[l, :, pl.ds(table.shape[1], BLK)]
        pairs.append((held.at[:, pl.ds(l * BLK, BLK)], part))
    wait_all(copies(pairs, sems))


def assemble(pieces, scal, *refs):
    blocks, (edge_part, node_part, held, edge_rows, node_rows) = refs[:4], refs[4:]
    z_index, x_index = scal[0], scal[1]
    for k, block in enumerate(blocks):
        held[k] = block[...]
    outs = (edge_rows, edge_rows, node_rows, node_rows)
    bases = []
    for number, count in enumerate(pieces):
        bases.append(0 if number % 2 == 0 else bases[-1] + 8 * pieces[number - 1])
    sizes = (8 * (pieces[0] + pieces[1]), 8 * (pieces[2] + pieces[3]))
    for x in range(4):
        x_step = lax.rem(x_index - x + 4, 4)
        for z in range(4):
            z_step = lax.rem(z_index - z + 4, 4)
            shard = held[z_step, pl.ds(pl.multiple_of(x_step * 32, 32), 32), :].astype(F32)
            row, lat = 0, (x % 2) * 4 + z
            for number, count in enumerate(pieces):
                base = (x // 2) * sizes[number // 2] + bases[number] + lat * count
                outs[number][pl.ds(base, count), :] = shard[row : row + count]
                row += count
    edge_part[...] = edge_rows[...].astype(BF)
    node_part[...] = node_rows[...].astype(BF)


def sum_far(pieces, scal, edge_own, e1, e2, e3, node_own, n1, n2, n3, keep, s1, s2, s3, er, nr, sent):
    z_index = scal[0]
    er[...] = sum((ref[...].astype(F32) for ref in (e1, e2, e3)), edge_own[...].astype(F32))
    nr[...] = sum((ref[...].astype(F32) for ref in (n1, n2, n3)), node_own[...].astype(F32))
    ins = (er, er, nr, nr)
    bases = []
    for number, count in enumerate(pieces):
        bases.append(0 if number % 2 == 0 else bases[-1] + 8 * pieces[number - 1])
    sizes = (8 * (pieces[0] + pieces[1]), 8 * (pieces[2] + pieces[3]))
    spare = 32 - sum(pieces)
    for x in range(4):
        for z in range(4):
            lat = (x % 2) * 4 + z
            parts = []
            for number, count in enumerate(pieces):
                base = (x // 2) * sizes[number // 2] + bases[number] + lat * count
                parts.append(ins[number][pl.ds(base, count), :])
            parts.append(jnp.zeros((spare, L), F32))
            sent[z, x] = jnp.concatenate(parts, axis=0)
    keep[...] = sent[z_index]
    for step, out in ((1, s1), (2, s2), (3, s3)):
        out[...] = sent[lax.rem(z_index + step, 4)].astype(BF)


def sum_z(scal, own, r1, r2, r3, keep, s1, s2, s3, held):
    x_index = scal[1]
    held[...] = own[...] + (r1[...].astype(F32) + r2[...].astype(F32) + r3[...].astype(F32))
    keep[...] = held[x_index]
    for step, out in ((1, s1), (2, s2), (3, s3)):
        out[...] = held[lax.rem(x_index + step, 4)].astype(BF)


def sum_x(own, r1, r2, r3, *outs):
    total = own[...] + (r1[...].astype(F32) + r2[...].astype(F32) + r3[...].astype(F32))
    row = 0
    for out in outs:
        count = out.shape[0]
        out[...] = total[row : row + count]
        row += count


def edge_forward(scal, ext, edges, offsets, *refs):
    shards, refs = refs[:8], refs[8:]
    gain, joined_out, first_out, normed_out, inverse_out, new_edges_out, partial_out = refs[:7]
    own_out, up_out, refs = refs[7], refs[8], refs[9:]
    joined, first, normed, inverse, new_edges, partial, w_in, w_out, second, sems, out_sems = refs
    tiles = edges.shape[0] // BLK
    lat_index, core, y_index, count = (scal[2 * tiles + i] for i in range(4))
    slabs = w_in.shape[0] // 3 // 32
    counts = (3 * L // slabs, L // slabs)
    stores = []

    def store(source, target):
        copy = pltpu.make_async_copy(source, target, out_sems.at[len(stores)])
        copy.start()
        stores.append(copy)

    store(ext.at[:, block_at(HB + lat_index)], own_out)
    store(ext.at[:, pl.ds(ext.shape[1] - BLK, BLK)], up_out)
    loads = copies([(edges, joined.at[:, pl.ds(0, L)])], sems)
    for t in range(tiles):
        rows = pl.ds(t * BLK, BLK)
        to_src = one_hot_columns(offsets[1, pl.ds(t, 1), :]).T.astype(BF)
        to_dst = one_hot_columns(offsets[0, pl.ds(t, 1), :]).T.astype(BF)
        src, dst = block_at(scal[tiles + t]), block_at(scal[t] + HB)
        joined[rows, pl.ds(L, L)] = dot_transpose(to_src, ext[:, src]).astype(BF)
        joined[rows, pl.ds(2 * L, L)] = dot_transpose(to_dst, ext[:, dst]).astype(BF)
    wait_all(loads)
    store(joined, joined_out)
    unpack_weights(core, y_index, shards, (w_in, w_out), counts)
    for n in range(2):
        columns = pl.ds(n * 256, 256)
        first[:, columns] = jnp.maximum(dot(joined[...], w_in[:, columns]), 0.0).astype(BF)
    store(first, first_out)
    for n in range(2):
        columns = pl.ds(n * 256, 256)
        second[:, columns] = dot(first[...], w_out[:, columns])
    partial[...] = jnp.zeros_like(partial)
    for t in range(tiles):
        rows = pl.ds(t * BLK, BLK)
        live = (lat_index * tiles + t < count).astype(F32)
        values, inv = norm_parts(second[rows, :])
        normed[rows, :] = values
        inverse[rows, :] = jnp.broadcast_to(inv, (BLK, BLK))
        message = values * gain[...] * live
        new_edges[rows, :] = (joined[rows, pl.ds(0, L)].astype(F32) + message).astype(BF)
        second[rows, :] = message
    store(normed, normed_out)
    store(inverse, inverse_out)
    store(new_edges, new_edges_out)
    for t in range(tiles):
        rows = pl.ds(t * BLK, BLK)
        into = one_hot_columns(offsets[0, pl.ds(t, 1), :]).astype(BF)
        high, middle, low = split_three(second[rows, :])
        block = scal[t]
        partial[block] = partial[block] + (dot(into, low) + dot(into, middle) + dot(into, high))
    store(partial, partial_out)
    wait_all(stores)


def node_step(scal, spread, own_hbm, up_hbm, *refs):
    shards, refs = refs[:8], refs[8:]
    gain, out, direct_out, joined_out, first_out, d_second_out, d_first_out = refs[:7]
    own_turned, up_turned, w_in, w_out, joined, first, d_second, d_first, d_direct = refs[7:16]
    sems, out_sems = refs[16:]
    core, y_index = scal[1], scal[2]
    slabs = w_in.shape[0] // 2 // 32
    counts = (2 * L // slabs, L // slabs)
    loads = copies([(own_hbm, own_turned), (up_hbm, up_turned)], sems)
    unpack_weights(core, y_index, shards, (w_in, w_out), counts)
    wait_all(loads)
    own = own_turned[...].astype(F32).T
    upstream = up_turned[...].astype(F32).T
    joined[:, pl.ds(0, L)] = own.astype(BF)
    total = spread[0]
    for l in range(1, spread.shape[0]):
        total = total + spread[l]
    joined[:, pl.ds(L, L)] = total.astype(BF)
    first[...] = jnp.maximum(dot(joined[...], w_in[...]), 0.0).astype(BF)
    normed, inverse = norm_parts(dot(first[...], w_out[...]))
    d_second[...] = norm_back(upstream, normed, inverse, gain[...]).astype(BF)
    back = dot_transpose(d_second[...], w_out[...])
    d_first[...] = jnp.where(first[...].astype(F32) > 0, back, 0.0).astype(BF)
    d_agg = dot_transpose(w_in[pl.ds(L, L), :], d_first[...]).astype(BF)
    new_rows = (own + normed * gain[...]).T.astype(BF)
    width = L // out.shape[0]
    for l in range(out.shape[0]):
        out[l, pl.ds(0, L), :] = d_agg
        out[l, pl.ds(L, width), :] = new_rows[l * width : (l + 1) * width, :]
    d_direct[...] = dot_transpose(w_in[pl.ds(0, L), :], d_first[...])
    held = (d_direct, joined, first, d_second, d_first)
    outs = (direct_out, joined_out, first_out, d_second_out, d_first_out)
    wait_all(copies(zip(held, outs), out_sems))


def node_grads(scal, *refs):
    saved, (keep, send), refs = refs[:4], refs[4:6], refs[6:]
    held, (g_in, g_out, sems) = refs[:4], refs[4:]
    wait_all(copies(zip(saved, held), sems))
    joined, first, d_second, d_first = held
    g_out[...] = dot_rows(first[...], d_second[...])
    g_in[...] = dot_rows(joined[...], d_first[...])
    slabs = g_in.shape[0] // 2 // 32
    pack_grads(scal[1], scal[2], (g_in, g_out), keep, send, (2 * L // slabs, L // slabs))


def edge_backward(scal, d_agg, cot, offsets, gain, *refs):
    saved, w_out_shards, refs = refs[:4], refs[4:12], refs[12:]
    d_first, keep, send = refs[:3]
    joined, first, normed, inverse, w_in, w_out, d_second, g_in, g_out, sems = refs[3:]
    tiles = cot.shape[0] // BLK
    lat_index, core, y_index, count = (scal[2 * tiles + i] for i in range(4))
    slabs = w_in.shape[0] // 3 // 32
    counts = (3 * L // slabs, L // slabs)
    normed_in, inverse_in, first_in, joined_in = saved
    pairs = [(normed_in, normed), (inverse_in, inverse)]
    pairs += weight_pairs(core, y_index, w_out_shards, (w_in, w_out), counts)[1::2]
    pairs += [(first_in, first), (joined_in, joined)]
    loads = copies(pairs, sems)
    wait_all(loads[:2])
    for t in range(tiles):
        rows = pl.ds(t * BLK, BLK)
        live = (lat_index * tiles + t < count).astype(F32)
        to_dst = one_hot_columns(offsets[0, pl.ds(t, 1), :]).T.astype(BF)
        picked = dot_transpose(to_dst, d_agg[scal[t], pl.ds(0, L), :])
        d_message = (cot[rows, :].astype(F32) + picked) * live
        back = norm_back(d_message, normed[rows, :], inverse[rows, pl.ds(0, 1)], gain[...])
        d_second[rows, :] = back.astype(BF)
    wait_all(loads[2:])
    for n in range(2):
        part = pl.ds(n * 256, 256)
        back = dot_transpose(d_second[...], w_out[part, :])
        d_first[:, part] = jnp.where(first[:, part].astype(F32) > 0, back, 0.0).astype(BF)
    for n in range(2):
        part = pl.ds(n * 256, 256)
        g_out[part, :] = dot_rows(first[:, part], d_second[...])
    for n in range(6):
        part = pl.ds(n * 256, 256)
        g_in[part, :] = dot_rows(joined[:, part], d_first[...])
    pack_grads(core, y_index, (g_in, g_out), keep, send, counts)


def edge_inputs(scal, d_first, cot, offsets, direct_in, *refs):
    shards, refs = refs[:8], refs[8:]
    grad_out, middle_out, lower, upper = refs[:4]
    grad_edges, d_direct, w_in, w_out, d_ext, d_turned, sems, out_sems = refs[4:]
    tiles = cot.shape[0] // BLK
    lat_index, core, y_index = (scal[2 * tiles + i] for i in range(3))
    slabs = w_in.shape[0] // 3 // 32
    counts = (3 * L // slabs, L // slabs)
    pairs = weight_pairs(core, y_index, shards, (w_in, w_out), counts)[::2]
    pairs += [(direct_in, d_direct)]
    loads = copies(pairs, sems)
    d_ext[...] = jnp.zeros_like(d_ext)
    wait_all(loads)
    for n in range(4):
        d_turned[pl.ds(n * 256, 256), :] = dot_transpose(
            w_in[pl.ds(L + n * 256, 256), :], d_first[...]
        )
    for n in range(2):
        part = pl.ds(n * 256, 256)
        back = dot_transpose(d_first[...], w_in[part, :])
        grad_edges[:, part] = (cot[:, part].astype(F32) + back).astype(BF)
    store = copies([(grad_edges, grad_out)], out_sems)
    for t in range(tiles):
        rows = pl.ds(t * BLK, BLK)
        for row, place, at in ((1, scal[tiles + t], 0), (0, scal[t] + HB, L)):
            into = one_hot_columns(offsets[row, pl.ds(t, 1), :]).T.astype(BF)
            value = d_turned[pl.ds(at, L), rows]
            high = value.astype(BF)
            low = (value - high.astype(F32)).astype(BF)
            d_ext[place] = d_ext[place] + (dot(low, into) + dot(high, into))
    d_ext[HB + lat_index] = d_ext[HB + lat_index] + d_direct[...]
    blocks = middle_out.shape[0]
    for j in range(HB):
        lower[:, pl.ds(j * BLK, BLK)] = d_ext[j].astype(BF)
        upper[:, pl.ds(j * BLK, BLK)] = d_ext[HB + blocks + j].astype(BF)
    middle_out[...] = d_ext[pl.ds(HB, blocks)]
    wait_all(store)


def add_halo(halo, middle, above, below, columns, held):
    held[...] = middle[...]
    for j in range(HB):
        for place, value in ((halo[0, 0, j], above), (halo[0, 1, j], below)):
            held[place] = held[place] + value[:, pl.ds(j * BLK, BLK)].astype(F32)
    width = columns.shape[1]
    for block in range(held.shape[0]):
        for l in range(columns.shape[0]):
            columns[l, :, pl.ds(block * BLK, BLK)] = held[
                block, pl.ds(l * width, width), :
            ].astype(BF)


def finish(arrived, out):
    total = arrived[0].astype(F32)
    for l in range(1, arrived.shape[0]):
        total = total + arrived[l].astype(F32)
    out[...] = total.astype(BF)


def call(kernel, out_shape, scratch, mib, spaces, operands, flops=0, out_spaces="", sems=()):
    moved = sum(x.size * x.dtype.itemsize for x in operands)
    moved += sum(x.size * x.dtype.itemsize for x in out_shape)
    named = {"s": pltpu.SMEM, "v": pltpu.VMEM, "h": pltpu.HBM}
    out_spaces = out_spaces or "v" * len(out_shape)
    operands = [
        pltpu.with_memory_space_constraint(x, pltpu.HBM) if space == "h" else x
        for x, space in zip(operands, spaces)
    ]
    placed = [
        pltpu.HBM(x.shape, x.dtype) if space == "h" else x
        for x, space in zip(out_shape, out_spaces)
    ]
    return pl.pallas_call(
        kernel,
        out_shape=placed,
        in_specs=[pl.BlockSpec(memory_space=named[space]) for space in spaces],
        out_specs=[pl.BlockSpec(memory_space=named[space]) for space in out_spaces],
        scratch_shapes=[pltpu.VMEM(shape, dtype) for shape, dtype in scratch]
        + [pltpu.SemaphoreType.DMA((count,)) for count in sems],
        cost_estimate=pl.CostEstimate(flops=flops, bytes_accessed=moved, transcendentals=0),
        compiler_params=pltpu.CompilerParams(vmem_limit_bytes=mib << 20),
    )(*operands)


def run_edge_forward(scal, ext, edges, offsets, shards, gain, lat_size):
    rows = edges.shape[0]
    outs = [
        shape_of((rows, 3 * L), BF),
        shape_of((rows, L), BF),
        shape_of((rows, L), F32),
        shape_of((rows, BLK), F32),
        shape_of((rows, L), BF),
        shape_of((lat_size, BLK, L), F32),
    ]
    held = [(out.shape, out.dtype) for out in outs]
    outs += [shape_of((L, BLK), BF)] * 2
    return call(
        edge_forward,
        outs,
        held + [((3 * L, L), BF), ((L, L), BF), ((rows, L), F32)],
        EDGE_MIB,
        "svhv" + "v" * len(shards) + "v",
        (scal, ext, edges, offsets, *shards, gain),
        flops=2 * rows * 4 * L * L,
        out_spaces="h" * len(outs),
        sems=(1, len(outs)),
    )


def run_node_step(scal, spread, own, up, shards, gain):
    lat_size = spread.shape[0]
    rows = [((BLK, 2 * L), BF), ((BLK, L), BF), ((BLK, L), BF), ((BLK, L), BF)]
    return call(
        node_step,
        [shape_of((lat_size, L + L // lat_size, BLK), BF), shape_of((L, BLK), F32)]
        + [shape_of(*row) for row in rows],
        [((L, BLK), BF), ((L, BLK), BF), ((2 * L, L), BF), ((L, L), BF)]
        + rows
        + [((L, BLK), F32)],
        NODE_MIB,
        "svhh" + "v" * len(shards) + "v",
        (scal, spread, own, up, *shards, gain),
        flops=2 * BLK * 6 * L * L,
        out_spaces="vhhhhh",
        sems=(2, 5),
    )


def run_node_grads(scal, saved, shard, y_count):
    return call(
        node_grads,
        [shape_of((y_count,) + shard.shape, BF)] * 2,
        [(one.shape, BF) for one in saved] + [((2 * L, L), F32), ((L, L), F32)],
        NODE_MIB,
        "shhhh",
        (scal, *saved),
        flops=2 * BLK * 3 * L * L,
        sems=(4,),
    )


def run_edge_backward(scal, d_agg, cot, offsets, gain, saved, shards):
    rows = cot.shape[0]
    chunk = (len(shards) // 2,) + shards[0].shape
    normed, inverse, first, joined = saved
    return call(
        edge_backward,
        [shape_of((rows, L), BF), shape_of(chunk, BF), shape_of(chunk, BF)],
        [
            (joined.shape, BF),
            (first.shape, BF),
            (normed.shape, F32),
            (inverse.shape, F32),
            ((3 * L, L), BF),
            ((L, L), BF),
            ((rows, L), BF),
            ((3 * L, L), F32),
            ((L, L), F32),
        ],
        BACK_MIB,
        "svvvv" + "h" * (len(saved) + len(shards)),
        (scal, d_agg, cot, offsets, gain, *saved, *shards),
        flops=2 * rows * 5 * L * L,
        sems=(4 + 2 * len(shards),),
    )


def run_edge_inputs(scal, d_first, cot, offsets, d_direct, shards, lat_size):
    rows = cot.shape[0]
    return call(
        edge_inputs,
        [
            shape_of((rows, L), BF),
            shape_of((lat_size, L, BLK), F32),
            shape_of((L, HB * BLK), BF),
            shape_of((L, HB * BLK), BF),
        ],
        [
            ((rows, L), BF),
            (d_direct.shape, F32),
            ((3 * L, L), BF),
            ((L, L), BF),
            ((lat_size + 2 * HB, L, BLK), F32),
            ((2 * L, rows), F32),
        ],
        EDGE_MIB,
        "svvvh" + "h" * len(shards),
        (scal, d_first, cot, offsets, d_direct, *shards),
        flops=2 * rows * 3 * L * L,
        out_spaces="hvvv",
        sems=(1 + 2 * len(shards), 1),
    )


def swap_cores(value):
    return lax.ppermute(value, "c", [(0, 1), (1, 0)])


def shift(value, axes, step):
    count = lax.axis_size(axes)
    return lax.ppermute(value, axes, [(i, (i + step) % count) for i in range(count)])


def shifts(value, axes):
    return [value] + [shift(value, axes, k) for k in range(1, lax.axis_size(axes))]


def spread_rows(value, axes):
    return lax.all_to_all(value, axes, 0, 0)


def gather_far(value):
    mine = shifts(value, "y")
    return mine + [swap_cores(one) for one in mine]


def reduce_far(keep, send):
    arrived = swap_cores(send)
    both = [(keep[k].astype(F32) + arrived[k].astype(F32)).astype(BF) for k in range(keep.shape[0])]
    return [both[0]] + [shift(both[k], "y", k) for k in range(1, keep.shape[0])]


def per_device(
    nodes,
    edges,
    edge_tiles,
    edge_offsets,
    tile_counts,
    halo_blocks,
    w_edge_in,
    w_edge_out,
    w_node_in,
    w_node_out,
    edge_gain,
    node_gain,
    node_cotangent,
    edge_cotangent,
):
    lat_size = lax.axis_size(LAT)
    place = [lax.axis_index(LAT), lax.axis_index("c"), lax.axis_index("y")]
    slab_rows, width = nodes.shape
    own_rows = slab_rows // lat_size
    halo_rows = HB * BLK
    ext_rows = slab_rows + 2 * halo_rows
    weights = (w_edge_in, w_edge_out, w_node_in, w_node_out)
    pieces = tuple(weight.shape[0] for weight in weights)
    edge_rows = 2 * lat_size * (pieces[0] + pieces[1])
    node_rows = 2 * lat_size * (pieces[2] + pieces[3])

    near_scal = jnp.stack([lax.axis_index("z"), lax.axis_index(XS)]).astype(jnp.int32)
    node_scal = jnp.stack(place).astype(jnp.int32)
    scal = jnp.concatenate([edge_tiles.reshape(-1), node_scal, tile_counts])
    halo = halo_blocks
    offsets = edge_offsets.reshape(2, -1, BLK)
    edge_gain_row = edge_gain.reshape(1, L)
    node_gain_row = node_gain.reshape(1, L)

    turned = nodes.T
    up, down, packed = call(
        prepare,
        [
            shape_of((width, halo_rows), BF),
            shape_of((width, halo_rows), BF),
            shape_of((32, L), BF),
        ],
        [(weight.shape, BF) for weight in weights],
        4,
        "shhhhh",
        (halo, turned, *weights),
        sems=(4 + 2 * HB,),
    )
    from_lower = from_behind(up, 1)
    from_upper = from_behind(down, -1)

    (message_out,) = call(
        fill_message,
        [shape_of((lat_size, width, ext_rows + own_rows), BF)],
        [((width, ext_rows), BF), ((width, slab_rows), BF)],
        4,
        "vhvh",
        (from_lower, turned, from_upper, node_cotangent.T),
        out_spaces="h",
        sems=(2, 2 * lat_size),
    )
    by_x = jnp.concatenate(shifts(packed, XS), axis=0)
    near = shifts(by_x, "z")
    edge_part, node_part = call(
        functools.partial(assemble, pieces),
        [shape_of((edge_rows, L), BF), shape_of((node_rows, L), BF)],
        [((4, 128, L), BF), ((edge_rows, L), F32), ((node_rows, L), F32)],
        6,
        "svvvv",
        (near_scal, *near),
    )

    edge_shards = gather_far(edge_part)
    ext = spread_rows(message_out, LAT).reshape(L, ext_rows + own_rows)

    joined, first, normed, inverse, new_edges, partial, own, node_up = run_edge_forward(
        scal, ext, edges, offsets, edge_shards, edge_gain_row, lat_size
    )
    node_shards = gather_far(node_part)
    spread = spread_rows(partial, LAT)
    second_out, d_direct, *node_saved = run_node_step(
        node_scal, spread, own, node_up, node_shards, node_gain_row
    )
    node_keep, node_send = run_node_grads(
        node_scal, node_saved, node_part, lax.axis_size("y")
    )
    second_in = spread_rows(second_out, LAT)
    new_nodes = second_in[:, L:].transpose(1, 0, 2).reshape(width, slab_rows).T
    node_far = reduce_far(node_keep, node_send)

    d_first, edge_keep, edge_send = run_edge_backward(
        scal, second_in, edge_cotangent, offsets, edge_gain_row,
        (normed, inverse, first, joined), edge_shards,
    )
    grad_edges, middle, lower, upper = run_edge_inputs(
        scal, d_first, edge_cotangent, offsets, d_direct, edge_shards, lat_size
    )
    from_above = from_behind(lower, -1)
    from_below = from_behind(upper, 1)
    edge_far = reduce_far(edge_keep, edge_send)
    (columns,) = call(
        add_halo,
        [shape_of((lat_size, width, slab_rows), BF)],
        [((lat_size, L, BLK), F32)],
        8,
        "svvv",
        (halo, middle, from_above, from_below),
    )
    columns = spread_rows(columns, LAT)
    (grad_slab,) = call(finish, [shape_of((width, slab_rows), BF)], [], 4, "v", (columns,))

    shard = (32, L)
    shards = (4,) + shard
    kept, *sent = call(
        functools.partial(sum_far, pieces),
        [shape_of(shards, F32)] + [shape_of(shards, BF)] * 3,
        [((edge_rows, L), F32), ((node_rows, L), F32), ((4,) + shards, F32)],
        8,
        "s" + "v" * 8,
        (near_scal, *edge_far, *node_far),
    )
    moved = [shift(sent[k - 1], "z", k) for k in range(1, 4)]
    kept, *sent = call(
        sum_z,
        [shape_of(shard, F32)] + [shape_of(shard, BF)] * 3,
        [(shards, F32)],
        4,
        "s" + "v" * 4,
        (near_scal, kept, *moved),
    )
    moved = [shift(sent[k - 1], XS, k) for k in range(1, 4)]
    reduced = call(
        sum_x, [shape_of((count, L), F32) for count in pieces], [], 4, "v" * 4, (kept, *moved)
    )
    return (new_nodes, new_edges, grad_slab.T, grad_edges) + tuple(reduced)


def solution(mesh):
    fine = Mesh(mesh.devices.reshape(4, 2, 2, 2, 4), ("y", "xl", "c", "xh", "z"))
    every = SLAB + LAT
    by_rows = P(every, None)
    split = P(SLAB, LAT)
    placed = (
        split,
        by_rows,
        P(None, every),
        P(None, every),
        P(SLAB),
        P(SLAB, None, None),
        by_rows,
        by_rows,
        by_rows,
        by_rows,
        P(),
        P(),
        split,
        by_rows,
    )

    return jax.shard_map(
        per_device,
        mesh=fine,
        in_specs=placed,
        out_specs=(split, by_rows, split, by_rows, by_rows, by_rows, by_rows, by_rows),
        check_vma=False,
    )
```

```python
import functools

import jax
import jax.numpy as jnp
from jax import lax
from jax.experimental import pallas as pl
from jax.experimental.pallas import tpu as pltpu
from jax.sharding import Mesh, PartitionSpec as P


L = 512
BLK = 128
HB = 2
EPSILON = 1e-05

SLAB = ("y", "xl", "c")
LAT = ("xh", "z")
XS = ("xl", "xh")
BF = jnp.bfloat16
F32 = jnp.float32
EDGE_MIB = 16
NODE_MIB = 14
BACK_MIB = 28


def shape_of(shape, dtype):
    return jax.ShapeDtypeStruct(shape, dtype)


def from_behind(value, steps):
    count = lax.axis_size(SLAB)
    first, last = (max(0, -steps), min(count, count - steps))
    return lax.ppermute(value, SLAB, [(source, source + steps) for source in range(first, last)])


def dot(left, right):
    return jnp.dot(left, right, preferred_element_type=F32)


def dot_rows(left, right):
    return lax.dot_general(left, right, (((0,), (0,)), ((), ())), preferred_element_type=F32)


def dot_transpose(left, right):
    return lax.dot_general(left, right, (((1,), (1,)), ((), ())), preferred_element_type=F32)


def one_hot_columns(offsets):
    cells = lax.broadcasted_iota(jnp.int32, (BLK, BLK), 0)
    return (cells == offsets).astype(F32)


def norm_parts(values):
    average = jnp.mean(values, axis=-1, keepdims=True)
    centred = values - average
    variance = jnp.mean(centred * centred, axis=-1, keepdims=True)
    inverse = lax.rsqrt(variance + EPSILON)
    return centred * inverse, inverse


def norm_back(upstream, normed, inverse, gain_vector):
    scaled = upstream * gain_vector
    return inverse * (
        scaled
        - jnp.mean(scaled, axis=-1, keepdims=True)
        - normed * jnp.mean(scaled * normed, axis=-1, keepdims=True)
    )


def split_three(value):
    high = value.astype(BF)
    rest = value - high.astype(F32)
    middle = rest.astype(BF)
    return high, middle, (rest - middle.astype(F32)).astype(BF)


def block_at(number):
    return pl.ds(pl.multiple_of(number * BLK, BLK), BLK)


def copies(pairs, sems):
    made = [pltpu.make_async_copy(src, dst, sems.at[i]) for i, (src, dst) in enumerate(pairs)]
    for one in made:
        one.start()
    return made


def wait_all(made):
    for one in made:
        one.wait()


def weight_pairs(core, y_index, shards, outs, counts):
    total = sum(counts)
    y_count = len(shards) // 2
    pairs = []
    for number, source in enumerate(shards):
        step = number % y_count
        parity = core if number < y_count else 1 - core
        y = lax.rem(y_index - step + y_count, y_count)
        per = source.shape[0] // total
        for x in range(per):
            slab = (y * per + x) * 2 + parity
            at = x * total
            for out, count in zip(outs, counts):
                start = pl.multiple_of(slab * count, 32)
                pairs.append((source.at[pl.ds(at, count), :], out.at[pl.ds(start, count), :]))
                at += count
    return pairs


def unpack_weights(core, y_index, shards, outs, counts):
    for source, target in weight_pairs(core, y_index, shards, outs, counts):
        target[...] = source[...]


def pack_grads(core, y_index, grads, keep, send, counts):
    total = sum(counts)
    y_count = keep.shape[0]
    per = keep.shape[1] // total
    for target, parity in ((keep, core), (send, 1 - core)):
        for step in range(y_count):
            y = lax.rem(y_index + step, y_count)
            for x in range(per):
                at = x * total
                for grad, count in zip(grads, counts):
                    start = pl.multiple_of(((y * per + x) * 2 + parity) * count, 32)
                    target[step, pl.ds(at, count), :] = grad[pl.ds(start, count), :].astype(BF)
                    at += count


def prepare(halo, turned, *refs):
    weights, (up, down, packed), held, sems = refs[:4], refs[4:7], refs[7:-1], refs[-1]
    pairs = list(zip(weights, held))
    for j in range(HB):
        part = pl.ds(j * BLK, BLK)
        pairs.append((turned.at[:, block_at(halo[0, 0, j])], up.at[:, part]))
        pairs.append((turned.at[:, block_at(halo[0, 1, j])], down.at[:, part]))
    wait_all(copies(pairs, sems))
    parts = [ref[...].astype(F32) for ref in held]
    used = sum(part.shape[0] for part in parts)
    parts.append(jnp.zeros((packed.shape[0] - used, L), F32))
    packed[...] = jnp.concatenate(parts, axis=0).astype(BF)


def fill_message(lower, turned, upper, cot, out, table, held, in_sems, sems):
    rows, halo_rows = turned.shape[1], lower.shape[1]
    loads = copies([(turned, table.at[:, pl.ds(halo_rows, rows)]), (cot, held)], in_sems)
    table[:, pl.ds(0, halo_rows)] = lower[...]
    table[:, pl.ds(halo_rows + rows, halo_rows)] = upper[...]
    wait_all(loads)
    pairs = []
    for l in range(out.shape[0]):
        pairs.append((table, out.at[l, :, pl.ds(0, table.shape[1])]))
        part = out.at[l, :, pl.ds(table.shape[1], BLK)]
        pairs.append((held.at[:, pl.ds(l * BLK, BLK)], part))
    wait_all(copies(pairs, sems))


def assemble(pieces, scal, *refs):
    blocks, (edge_part, node_part, held, edge_rows, node_rows) = refs[:4], refs[4:]
    z_index, x_index = scal[0], scal[1]
    for k, block in enumerate(blocks):
        held[k] = block[...]
    outs = (edge_rows, edge_rows, node_rows, node_rows)
    bases = []
    for number, count in enumerate(pieces):
        bases.append(0 if number % 2 == 0 else bases[-1] + 8 * pieces[number - 1])
    sizes = (8 * (pieces[0] + pieces[1]), 8 * (pieces[2] + pieces[3]))
    for x in range(4):
        x_step = lax.rem(x_index - x + 4, 4)
        for z in range(4):
            z_step = lax.rem(z_index - z + 4, 4)
            shard = held[z_step, pl.ds(pl.multiple_of(x_step * 32, 32), 32), :].astype(F32)
            row, lat = 0, (x % 2) * 4 + z
            for number, count in enumerate(pieces):
                base = (x // 2) * sizes[number // 2] + bases[number] + lat * count
                outs[number][pl.ds(base, count), :] = shard[row : row + count]
                row += count
    edge_part[...] = edge_rows[...].astype(BF)
    node_part[...] = node_rows[...].astype(BF)


def sum_far(pieces, scal, edge_own, e1, e2, e3, node_own, n1, n2, n3, keep, s1, s2, s3, er, nr, sent):
    z_index = scal[0]
    er[...] = sum((ref[...].astype(F32) for ref in (e1, e2, e3)), edge_own[...].astype(F32))
    nr[...] = sum((ref[...].astype(F32) for ref in (n1, n2, n3)), node_own[...].astype(F32))
    ins = (er, er, nr, nr)
    bases = []
    for number, count in enumerate(pieces):
        bases.append(0 if number % 2 == 0 else bases[-1] + 8 * pieces[number - 1])
    sizes = (8 * (pieces[0] + pieces[1]), 8 * (pieces[2] + pieces[3]))
    spare = 32 - sum(pieces)
    for x in range(4):
        for z in range(4):
            lat = (x % 2) * 4 + z
            parts = []
            for number, count in enumerate(pieces):
                base = (x // 2) * sizes[number // 2] + bases[number] + lat * count
                parts.append(ins[number][pl.ds(base, count), :])
            parts.append(jnp.zeros((spare, L), F32))
            sent[z, x] = jnp.concatenate(parts, axis=0)
    keep[...] = sent[z_index]
    for step, out in ((1, s1), (2, s2), (3, s3)):
        out[...] = sent[lax.rem(z_index + step, 4)].astype(BF)


def sum_z(scal, own, r1, r2, r3, keep, s1, s2, s3, held):
    x_index = scal[1]
    held[...] = own[...] + (r1[...].astype(F32) + r2[...].astype(F32) + r3[...].astype(F32))
    keep[...] = held[x_index]
    for step, out in ((1, s1), (2, s2), (3, s3)):
        out[...] = held[lax.rem(x_index + step, 4)].astype(BF)


def sum_x(own, r1, r2, r3, *outs):
    total = own[...] + (r1[...].astype(F32) + r2[...].astype(F32) + r3[...].astype(F32))
    row = 0
    for out in outs:
        count = out.shape[0]
        out[...] = total[row : row + count]
        row += count


def edge_forward(scal, ext, edges, offsets, *refs):
    shards, refs = refs[:8], refs[8:]
    gain, joined_out, first_out, normed_out, inverse_out, new_edges_out, partial_out = refs[:7]
    own_out, up_out, refs = refs[7], refs[8], refs[9:]
    joined, first, normed, inverse, new_edges, partial, w_in, w_out, second, sems, out_sems = refs
    tiles = edges.shape[0] // BLK
    lat_index, core, y_index, count = (scal[2 * tiles + i] for i in range(4))
    slabs = w_in.shape[0] // 3 // 32
    counts = (3 * L // slabs, L // slabs)
    stores = []

    def store(source, target):
        copy = pltpu.make_async_copy(source, target, out_sems.at[len(stores)])
        copy.start()
        stores.append(copy)

    store(ext.at[:, block_at(HB + lat_index)], own_out)
    store(ext.at[:, pl.ds(ext.shape[1] - BLK, BLK)], up_out)
    loads = copies([(edges, joined.at[:, pl.ds(0, L)])], sems)
    for t in range(tiles):
        rows = pl.ds(t * BLK, BLK)
        to_src = one_hot_columns(offsets[1, pl.ds(t, 1), :]).T.astype(BF)
        to_dst = one_hot_columns(offsets[0, pl.ds(t, 1), :]).T.astype(BF)
        src, dst = block_at(scal[tiles + t]), block_at(scal[t] + HB)
        joined[rows, pl.ds(L, L)] = dot_transpose(to_src, ext[:, src]).astype(BF)
        joined[rows, pl.ds(2 * L, L)] = dot_transpose(to_dst, ext[:, dst]).astype(BF)
    wait_all(loads)
    store(joined, joined_out)
    unpack_weights(core, y_index, shards, (w_in, w_out), counts)
    for n in range(2):
        columns = pl.ds(n * 256, 256)
        first[:, columns] = jnp.maximum(dot(joined[...], w_in[:, columns]), 0.0).astype(BF)
    store(first, first_out)
    for n in range(2):
        columns = pl.ds(n * 256, 256)
        second[:, columns] = dot(first[...], w_out[:, columns])
    partial[...] = jnp.zeros_like(partial)
    for t in range(tiles):
        rows = pl.ds(t * BLK, BLK)
        live = (lat_index * tiles + t < count).astype(F32)
        values, inv = norm_parts(second[rows, :])
        normed[rows, :] = values
        inverse[rows, :] = jnp.broadcast_to(inv, (BLK, BLK))
        message = values * gain[...] * live
        new_edges[rows, :] = (joined[rows, pl.ds(0, L)].astype(F32) + message).astype(BF)
        second[rows, :] = message
    store(normed, normed_out)
    store(inverse, inverse_out)
    store(new_edges, new_edges_out)
    for t in range(tiles):
        rows = pl.ds(t * BLK, BLK)
        into = one_hot_columns(offsets[0, pl.ds(t, 1), :]).astype(BF)
        high, middle, low = split_three(second[rows, :])
        block = scal[t]
        partial[block] = partial[block] + (dot(into, low) + dot(into, middle) + dot(into, high))
    store(partial, partial_out)
    wait_all(stores)


def node_step(scal, spread, own_hbm, up_hbm, *refs):
    shards, refs = refs[:8], refs[8:]
    gain, out, direct_out, joined_out, first_out, d_second_out, d_first_out = refs[:7]
    own_turned, up_turned, w_in, w_out, joined, first, d_second, d_first, d_direct = refs[7:16]
    sems, out_sems = refs[16:]
    core, y_index = scal[1], scal[2]
    slabs = w_in.shape[0] // 2 // 32
    counts = (2 * L // slabs, L // slabs)
    loads = copies([(own_hbm, own_turned), (up_hbm, up_turned)], sems)
    unpack_weights(core, y_index, shards, (w_in, w_out), counts)
    wait_all(loads)
    own = own_turned[...].astype(F32).T
    upstream = up_turned[...].astype(F32).T
    joined[:, pl.ds(0, L)] = own.astype(BF)
    total = spread[0]
    for l in range(1, spread.shape[0]):
        total = total + spread[l]
    joined[:, pl.ds(L, L)] = total.astype(BF)
    first[...] = jnp.maximum(dot(joined[...], w_in[...]), 0.0).astype(BF)
    normed, inverse = norm_parts(dot(first[...], w_out[...]))
    d_second[...] = norm_back(upstream, normed, inverse, gain[...]).astype(BF)
    back = dot_transpose(d_second[...], w_out[...])
    d_first[...] = jnp.where(first[...].astype(F32) > 0, back, 0.0).astype(BF)
    d_agg = dot_transpose(w_in[pl.ds(L, L), :], d_first[...]).astype(BF)
    new_rows = (own + normed * gain[...]).T.astype(BF)
    width = L // out.shape[0]
    for l in range(out.shape[0]):
        out[l, pl.ds(0, L), :] = d_agg
        out[l, pl.ds(L, width), :] = new_rows[l * width : (l + 1) * width, :]
    d_direct[...] = dot_transpose(w_in[pl.ds(0, L), :], d_first[...])
    held = (d_direct, joined, first, d_second, d_first)
    outs = (direct_out, joined_out, first_out, d_second_out, d_first_out)
    wait_all(copies(zip(held, outs), out_sems))


def node_grads(scal, *refs):
    saved, (keep, send), refs = refs[:4], refs[4:6], refs[6:]
    held, (g_in, g_out, sems) = refs[:4], refs[4:]
    wait_all(copies(zip(saved, held), sems))
    joined, first, d_second, d_first = held
    g_out[...] = dot_rows(first[...], d_second[...])
    g_in[...] = dot_rows(joined[...], d_first[...])
    slabs = g_in.shape[0] // 2 // 32
    pack_grads(scal[1], scal[2], (g_in, g_out), keep, send, (2 * L // slabs, L // slabs))


def edge_backward(scal, d_agg, cot, offsets, gain, *refs):
    saved, shards, refs = refs[:4], refs[4:12], refs[12:]
    d_first, d_second, middle_out, lower, upper = refs[:5]
    first, normed, inverse, d_direct, w_in, w_out, d_ext, d_turned, sems = refs[5:]
    tiles = cot.shape[0] // BLK
    lat_index, core, y_index, count = (scal[2 * tiles + i] for i in range(4))
    slabs = w_in.shape[0] // 3 // 32
    counts = (3 * L // slabs, L // slabs)
    normed_in, inverse_in, first_in, direct_in = saved
    weights = weight_pairs(core, y_index, shards, (w_in, w_out), counts)
    pairs = [(normed_in, normed), (inverse_in, inverse)] + weights[1::2] + [(first_in, first)]
    early = len(pairs)
    loads = copies(pairs + weights[::2] + [(direct_in, d_direct)], sems)
    d_ext[...] = jnp.zeros_like(d_ext)
    wait_all(loads[:2])
    for t in range(tiles):
        rows = pl.ds(t * BLK, BLK)
        live = (lat_index * tiles + t < count).astype(F32)
        to_dst = one_hot_columns(offsets[0, pl.ds(t, 1), :]).T.astype(BF)
        picked = dot_transpose(to_dst, d_agg[scal[t], pl.ds(0, L), :])
        d_message = (cot[rows, :].astype(F32) + picked) * live
        back = norm_back(d_message, normed[rows, :], inverse[rows, pl.ds(0, 1)], gain[...])
        d_second[rows, :] = back.astype(BF)
    wait_all(loads[2:early])
    for n in range(2):
        part = pl.ds(n * 256, 256)
        back = dot_transpose(d_second[...], w_out[part, :])
        d_first[:, part] = jnp.where(first[:, part].astype(F32) > 0, back, 0.0).astype(BF)
    wait_all(loads[early:])
    for n in range(4):
        d_turned[pl.ds(n * 256, 256), :] = dot_transpose(
            w_in[pl.ds(L + n * 256, 256), :], d_first[...]
        )
    for t in range(tiles):
        rows = pl.ds(t * BLK, BLK)
        for row, place, at in ((1, scal[tiles + t], 0), (0, scal[t] + HB, L)):
            into = one_hot_columns(offsets[row, pl.ds(t, 1), :]).T.astype(BF)
            value = d_turned[pl.ds(at, L), rows]
            high = value.astype(BF)
            low = (value - high.astype(F32)).astype(BF)
            d_ext[place] = d_ext[place] + (dot(low, into) + dot(high, into))
    d_ext[HB + lat_index] = d_ext[HB + lat_index] + d_direct[...]
    blocks = middle_out.shape[0]
    for j in range(HB):
        lower[:, pl.ds(j * BLK, BLK)] = d_ext[j].astype(BF)
        upper[:, pl.ds(j * BLK, BLK)] = d_ext[HB + blocks + j].astype(BF)
    middle_out[...] = d_ext[pl.ds(HB, blocks)]


def edge_grads(scal, d_first, d_second, cot, *refs):
    saved, shards, refs = refs[:2], refs[2:10], refs[10:]
    grad_out, keep, send, first, joined, grad_edges, w_in, w_out, g_in, g_out = refs[:10]
    sems, out_sems = refs[10:]
    tiles = cot.shape[0] // BLK
    core, y_index = scal[2 * tiles + 1], scal[2 * tiles + 2]
    slabs = w_in.shape[0] // 3 // 32
    counts = (3 * L // slabs, L // slabs)
    first_in, joined_in = saved
    pairs = [(first_in, first), (joined_in, joined)]
    pairs += weight_pairs(core, y_index, shards, (w_in, w_out), counts)[::2]
    loads = copies(pairs, sems)
    loads[0].wait()
    for n in range(2):
        part = pl.ds(n * 256, 256)
        g_out[part, :] = dot_rows(first[:, part], d_second[...])
    loads[1].wait()
    for n in range(6):
        part = pl.ds(n * 256, 256)
        g_in[part, :] = dot_rows(joined[:, part], d_first[...])
    pack_grads(core, y_index, (g_in, g_out), keep, send, counts)
    wait_all(loads[2:])
    for n in range(2):
        part = pl.ds(n * 256, 256)
        back = dot_transpose(d_first[...], w_in[part, :])
        grad_edges[:, part] = (cot[:, part].astype(F32) + back).astype(BF)
    wait_all(copies([(grad_edges, grad_out)], out_sems))


def add_halo(halo, middle, above, below, columns, held):
    held[...] = middle[...]
    for j in range(HB):
        for place, value in ((halo[0, 0, j], above), (halo[0, 1, j], below)):
            held[place] = held[place] + value[:, pl.ds(j * BLK, BLK)].astype(F32)
    width = columns.shape[1]
    for block in range(held.shape[0]):
        for l in range(columns.shape[0]):
            columns[l, :, pl.ds(block * BLK, BLK)] = held[
                block, pl.ds(l * width, width), :
            ].astype(BF)


def finish(arrived, out):
    total = arrived[0].astype(F32)
    for l in range(1, arrived.shape[0]):
        total = total + arrived[l].astype(F32)
    out[...] = total.astype(BF)


def call(kernel, out_shape, scratch, mib, spaces, operands, flops=0, out_spaces="", sems=()):
    moved = sum(x.size * x.dtype.itemsize for x in operands)
    moved += sum(x.size * x.dtype.itemsize for x in out_shape)
    named = {"s": pltpu.SMEM, "v": pltpu.VMEM, "h": pltpu.HBM}
    out_spaces = out_spaces or "v" * len(out_shape)
    operands = [
        pltpu.with_memory_space_constraint(x, pltpu.HBM) if space == "h" else x
        for x, space in zip(operands, spaces)
    ]
    placed = [
        pltpu.HBM(x.shape, x.dtype) if space == "h" else x
        for x, space in zip(out_shape, out_spaces)
    ]
    return pl.pallas_call(
        kernel,
        out_shape=placed,
        in_specs=[pl.BlockSpec(memory_space=named[space]) for space in spaces],
        out_specs=[pl.BlockSpec(memory_space=named[space]) for space in out_spaces],
        scratch_shapes=[pltpu.VMEM(shape, dtype) for shape, dtype in scratch]
        + [pltpu.SemaphoreType.DMA((count,)) for count in sems],
        cost_estimate=pl.CostEstimate(flops=flops, bytes_accessed=moved, transcendentals=0),
        compiler_params=pltpu.CompilerParams(vmem_limit_bytes=mib << 20),
    )(*operands)


def run_edge_forward(scal, ext, edges, offsets, shards, gain, lat_size):
    rows = edges.shape[0]
    outs = [
        shape_of((rows, 3 * L), BF),
        shape_of((rows, L), BF),
        shape_of((rows, L), F32),
        shape_of((rows, BLK), F32),
        shape_of((rows, L), BF),
        shape_of((lat_size, BLK, L), F32),
    ]
    held = [(out.shape, out.dtype) for out in outs]
    outs += [shape_of((L, BLK), BF)] * 2
    return call(
        edge_forward,
        outs,
        held + [((3 * L, L), BF), ((L, L), BF), ((rows, L), F32)],
        EDGE_MIB,
        "svhv" + "v" * len(shards) + "v",
        (scal, ext, edges, offsets, *shards, gain),
        flops=2 * rows * 4 * L * L,
        out_spaces="h" * len(outs),
        sems=(1, len(outs)),
    )


def run_node_step(scal, spread, own, up, shards, gain):
    lat_size = spread.shape[0]
    rows = [((BLK, 2 * L), BF), ((BLK, L), BF), ((BLK, L), BF), ((BLK, L), BF)]
    return call(
        node_step,
        [shape_of((lat_size, L + L // lat_size, BLK), BF), shape_of((L, BLK), F32)]
        + [shape_of(*row) for row in rows],
        [((L, BLK), BF), ((L, BLK), BF), ((2 * L, L), BF), ((L, L), BF)]
        + rows
        + [((L, BLK), F32)],
        NODE_MIB,
        "svhh" + "v" * len(shards) + "v",
        (scal, spread, own, up, *shards, gain),
        flops=2 * BLK * 6 * L * L,
        out_spaces="vhhhhh",
        sems=(2, 5),
    )


def run_node_grads(scal, saved, shard, y_count):
    return call(
        node_grads,
        [shape_of((y_count,) + shard.shape, BF)] * 2,
        [(one.shape, BF) for one in saved] + [((2 * L, L), F32), ((L, L), F32)],
        NODE_MIB,
        "shhhh",
        (scal, *saved),
        flops=2 * BLK * 3 * L * L,
        sems=(4,),
    )


def run_edge_backward(scal, d_agg, cot, offsets, gain, saved, shards):
    rows = cot.shape[0]
    lat_size = d_agg.shape[0]
    return call(
        edge_backward,
        [
            shape_of((rows, L), BF),
            shape_of((rows, L), BF),
            shape_of((lat_size, L, BLK), F32),
            shape_of((L, HB * BLK), BF),
            shape_of((L, HB * BLK), BF),
        ],
        [
            ((rows, L), BF),
            ((rows, L), F32),
            ((rows, BLK), F32),
            ((L, BLK), F32),
            ((3 * L, L), BF),
            ((L, L), BF),
            ((lat_size + 2 * HB, L, BLK), F32),
            ((2 * L, rows), F32),
        ],
        BACK_MIB,
        "svvvv" + "h" * (len(saved) + len(shards)),
        (scal, d_agg, cot, offsets, gain, *saved, *shards),
        flops=2 * rows * 4 * L * L,
        sems=(4 + 4 * len(shards),),
    )


def run_edge_grads(scal, d_first, d_second, cot, saved, shards):
    rows = cot.shape[0]
    chunk = (len(shards) // 2,) + shards[0].shape
    return call(
        edge_grads,
        [shape_of((rows, L), BF), shape_of(chunk, BF), shape_of(chunk, BF)],
        [(one.shape, BF) for one in saved]
        + [((rows, L), BF), ((3 * L, L), BF), ((L, L), BF), ((3 * L, L), F32), ((L, L), F32)],
        BACK_MIB,
        "svvv" + "h" * (len(saved) + len(shards)),
        (scal, d_first, d_second, cot, *saved, *shards),
        flops=2 * rows * 5 * L * L,
        out_spaces="hvv",
        sems=(2 + 2 * len(shards), 1),
    )


def swap_cores(value):
    return lax.ppermute(value, "c", [(0, 1), (1, 0)])


def shift(value, axes, step):
    count = lax.axis_size(axes)
    return lax.ppermute(value, axes, [(i, (i + step) % count) for i in range(count)])


def shifts(value, axes):
    return [value] + [shift(value, axes, k) for k in range(1, lax.axis_size(axes))]


def spread_rows(value, axes):
    return lax.all_to_all(value, axes, 0, 0)


def gather_far(value):
    mine = shifts(value, "y")
    return mine + [swap_cores(one) for one in mine]


def reduce_far(keep, arrived):
    both = [(keep[k].astype(F32) + arrived[k].astype(F32)).astype(BF) for k in range(keep.shape[0])]
    return [both[0]] + [shift(both[k], "y", k) for k in range(1, keep.shape[0])]


def per_device(
    nodes,
    edges,
    edge_tiles,
    edge_offsets,
    tile_counts,
    halo_blocks,
    w_edge_in,
    w_edge_out,
    w_node_in,
    w_node_out,
    edge_gain,
    node_gain,
    node_cotangent,
    edge_cotangent,
):
    lat_size = lax.axis_size(LAT)
    place = [lax.axis_index(LAT), lax.axis_index("c"), lax.axis_index("y")]
    slab_rows, width = nodes.shape
    own_rows = slab_rows // lat_size
    halo_rows = HB * BLK
    ext_rows = slab_rows + 2 * halo_rows
    weights = (w_edge_in, w_edge_out, w_node_in, w_node_out)
    pieces = tuple(weight.shape[0] for weight in weights)
    edge_rows = 2 * lat_size * (pieces[0] + pieces[1])
    node_rows = 2 * lat_size * (pieces[2] + pieces[3])

    near_scal = jnp.stack([lax.axis_index("z"), lax.axis_index(XS)]).astype(jnp.int32)
    node_scal = jnp.stack(place).astype(jnp.int32)
    scal = jnp.concatenate([edge_tiles.reshape(-1), node_scal, tile_counts])
    halo = halo_blocks
    offsets = edge_offsets.reshape(2, -1, BLK)
    edge_gain_row = edge_gain.reshape(1, L)
    node_gain_row = node_gain.reshape(1, L)

    turned = nodes.T
    up, down, packed = call(
        prepare,
        [
            shape_of((width, halo_rows), BF),
            shape_of((width, halo_rows), BF),
            shape_of((32, L), BF),
        ],
        [(weight.shape, BF) for weight in weights],
        4,
        "shhhhh",
        (halo, turned, *weights),
        sems=(4 + 2 * HB,),
    )
    from_lower = from_behind(up, 1)
    from_upper = from_behind(down, -1)

    (message_out,) = call(
        fill_message,
        [shape_of((lat_size, width, ext_rows + own_rows), BF)],
        [((width, ext_rows), BF), ((width, slab_rows), BF)],
        4,
        "vhvh",
        (from_lower, turned, from_upper, node_cotangent.T),
        out_spaces="h",
        sems=(2, 2 * lat_size),
    )
    by_x = jnp.concatenate(shifts(packed, XS), axis=0)
    near = shifts(by_x, "z")
    edge_part, node_part = call(
        functools.partial(assemble, pieces),
        [shape_of((edge_rows, L), BF), shape_of((node_rows, L), BF)],
        [((4, 128, L), BF), ((edge_rows, L), F32), ((node_rows, L), F32)],
        6,
        "svvvv",
        (near_scal, *near),
    )

    edge_shards = gather_far(edge_part)
    ext = spread_rows(message_out, LAT).reshape(L, ext_rows + own_rows)

    joined, first, normed, inverse, new_edges, partial, own, node_up = run_edge_forward(
        scal, ext, edges, offsets, edge_shards, edge_gain_row, lat_size
    )
    node_shards = gather_far(node_part)
    spread = spread_rows(partial, LAT)
    second_out, d_direct, *node_saved = run_node_step(
        node_scal, spread, own, node_up, node_shards, node_gain_row
    )
    node_keep, node_send = run_node_grads(
        node_scal, node_saved, node_part, lax.axis_size("y")
    )
    second_in = spread_rows(second_out, LAT)
    new_nodes = second_in[:, L:].transpose(1, 0, 2).reshape(width, slab_rows).T
    node_far = reduce_far(node_keep, swap_cores(node_send))

    d_first, d_second, middle, lower, upper = run_edge_backward(
        scal, second_in, edge_cotangent, offsets, edge_gain_row,
        (normed, inverse, first, d_direct), edge_shards,
    )
    from_above = from_behind(lower, -1)
    from_below = from_behind(upper, 1)
    grad_edges, edge_keep, edge_send = run_edge_grads(
        scal, d_first, d_second, edge_cotangent, (first, joined), edge_shards
    )
    edge_arrived = swap_cores(edge_send)
    edge_far = reduce_far(edge_keep, edge_arrived)
    (columns,) = call(
        add_halo,
        [shape_of((lat_size, width, slab_rows), BF)],
        [((lat_size, L, BLK), F32)],
        8,
        "svvv",
        (halo, middle, from_above, from_below),
    )
    columns = spread_rows(columns, LAT)
    (grad_slab,) = call(finish, [shape_of((width, slab_rows), BF)], [], 4, "v", (columns,))

    shard = (32, L)
    shards = (4,) + shard
    kept, *sent = call(
        functools.partial(sum_far, pieces),
        [shape_of(shards, F32)] + [shape_of(shards, BF)] * 3,
        [((edge_rows, L), F32), ((node_rows, L), F32), ((4,) + shards, F32)],
        8,
        "s" + "v" * 8,
        (near_scal, *edge_far, *node_far),
    )
    moved = [shift(sent[k - 1], "z", k) for k in range(1, 4)]
    kept, *sent = call(
        sum_z,
        [shape_of(shard, F32)] + [shape_of(shard, BF)] * 3,
        [(shards, F32)],
        4,
        "s" + "v" * 4,
        (near_scal, kept, *moved),
    )
    moved = [shift(sent[k - 1], XS, k) for k in range(1, 4)]
    reduced = call(
        sum_x, [shape_of((count, L), F32) for count in pieces], [], 4, "v" * 4, (kept, *moved)
    )
    return (new_nodes, new_edges, grad_slab.T, grad_edges) + tuple(reduced)


def solution(mesh):
    fine = Mesh(mesh.devices.reshape(4, 2, 2, 2, 4), ("y", "xl", "c", "xh", "z"))
    every = SLAB + LAT
    by_rows = P(every, None)
    split = P(SLAB, LAT)
    placed = (
        split,
        by_rows,
        P(None, every),
        P(None, every),
        P(SLAB),
        P(SLAB, None, None),
        by_rows,
        by_rows,
        by_rows,
        by_rows,
        P(),
        P(),
        split,
        by_rows,
    )

    return jax.shard_map(
        per_device,
        mesh=fine,
        in_specs=placed,
        out_specs=(split, by_rows, split, by_rows, by_rows, by_rows, by_rows, by_rows),
        check_vma=False,
    )
```

```python
import functools

import jax
import jax.numpy as jnp
from jax import lax
from jax.experimental import pallas as pl
from jax.experimental.pallas import tpu as pltpu
from jax.sharding import Mesh, PartitionSpec as P


L = 512
BLK = 128
HB = 2
EPSILON = 1e-05

SLAB = ("y", "xl", "c")
LAT = ("xh", "z")
XS = ("xl", "xh")
BF = jnp.bfloat16
F32 = jnp.float32
EDGE_MIB = 16
NODE_MIB = 14
BACK_MIB = 28


def shape_of(shape, dtype):
    return jax.ShapeDtypeStruct(shape, dtype)


def from_behind(value, steps):
    count = lax.axis_size(SLAB)
    first, last = (max(0, -steps), min(count, count - steps))
    return lax.ppermute(value, SLAB, [(source, source + steps) for source in range(first, last)])


def dot(left, right):
    return jnp.dot(left, right, preferred_element_type=F32)


def dot_rows(left, right):
    return lax.dot_general(left, right, (((0,), (0,)), ((), ())), preferred_element_type=F32)


def dot_transpose(left, right):
    return lax.dot_general(left, right, (((1,), (1,)), ((), ())), preferred_element_type=F32)


def one_hot_columns(offsets):
    cells = lax.broadcasted_iota(jnp.int32, (BLK, BLK), 0)
    return (cells == offsets).astype(F32)


def norm_parts(values):
    average = jnp.mean(values, axis=-1, keepdims=True)
    centred = values - average
    variance = jnp.mean(centred * centred, axis=-1, keepdims=True)
    inverse = lax.rsqrt(variance + EPSILON)
    return centred * inverse, inverse


def norm_back(upstream, normed, inverse, gain_vector):
    scaled = upstream * gain_vector
    return inverse * (
        scaled
        - jnp.mean(scaled, axis=-1, keepdims=True)
        - normed * jnp.mean(scaled * normed, axis=-1, keepdims=True)
    )


def split_three(value):
    high = value.astype(BF)
    rest = value - high.astype(F32)
    middle = rest.astype(BF)
    return high, middle, (rest - middle.astype(F32)).astype(BF)


def block_at(number):
    return pl.ds(pl.multiple_of(number * BLK, BLK), BLK)


def copies(pairs, sems):
    made = [pltpu.make_async_copy(src, dst, sems.at[i]) for i, (src, dst) in enumerate(pairs)]
    for one in made:
        one.start()
    return made


def wait_all(made):
    for one in made:
        one.wait()


def weight_pairs(core, y_index, shards, outs, counts):
    total = sum(counts)
    y_count = len(shards) // 2
    pairs = []
    for number, source in enumerate(shards):
        step = number % y_count
        parity = core if number < y_count else 1 - core
        y = lax.rem(y_index - step + y_count, y_count)
        per = source.shape[0] // total
        for x in range(per):
            slab = (y * per + x) * 2 + parity
            at = x * total
            for out, count in zip(outs, counts):
                start = pl.multiple_of(slab * count, 32)
                pairs.append((source.at[pl.ds(at, count), :], out.at[pl.ds(start, count), :]))
                at += count
    return pairs


def unpack_weights(core, y_index, shards, outs, counts):
    for source, target in weight_pairs(core, y_index, shards, outs, counts):
        target[...] = source[...]


def pack_grads(core, y_index, grads, keep, send, counts):
    total = sum(counts)
    y_count = keep.shape[0]
    per = keep.shape[1] // total
    for target, parity in ((keep, core), (send, 1 - core)):
        for step in range(y_count):
            y = lax.rem(y_index + step, y_count)
            for x in range(per):
                at = x * total
                for grad, count in zip(grads, counts):
                    start = pl.multiple_of(((y * per + x) * 2 + parity) * count, 32)
                    target[step, pl.ds(at, count), :] = grad[pl.ds(start, count), :].astype(BF)
                    at += count


def prepare(halo, turned, *refs):
    weights, (up, down, packed), held, sems = refs[:4], refs[4:7], refs[7:-1], refs[-1]
    pairs = list(zip(weights, held))
    for j in range(HB):
        part = pl.ds(j * BLK, BLK)
        pairs.append((turned.at[:, block_at(halo[0, 0, j])], up.at[:, part]))
        pairs.append((turned.at[:, block_at(halo[0, 1, j])], down.at[:, part]))
    wait_all(copies(pairs, sems))
    parts = [ref[...].astype(F32) for ref in held]
    used = sum(part.shape[0] for part in parts)
    parts.append(jnp.zeros((packed.shape[0] - used, L), F32))
    packed[...] = jnp.concatenate(parts, axis=0).astype(BF)


def fill_message(lower, turned, upper, cot, out, table, held, in_sems, sems):
    rows, halo_rows = turned.shape[1], lower.shape[1]
    loads = copies([(turned, table.at[:, pl.ds(halo_rows, rows)]), (cot, held)], in_sems)
    table[:, pl.ds(0, halo_rows)] = lower[...]
    table[:, pl.ds(halo_rows + rows, halo_rows)] = upper[...]
    wait_all(loads)
    pairs = []
    for l in range(out.shape[0]):
        pairs.append((table, out.at[l, :, pl.ds(0, table.shape[1])]))
        part = out.at[l, :, pl.ds(table.shape[1], BLK)]
        pairs.append((held.at[:, pl.ds(l * BLK, BLK)], part))
    wait_all(copies(pairs, sems))


def assemble(pieces, scal, *refs):
    blocks, (edge_part, node_part, held, edge_rows, node_rows) = refs[:4], refs[4:]
    z_index, x_index = scal[0], scal[1]
    for k, block in enumerate(blocks):
        held[k] = block[...]
    outs = (edge_rows, edge_rows, node_rows, node_rows)
    bases = []
    for number, count in enumerate(pieces):
        bases.append(0 if number % 2 == 0 else bases[-1] + 8 * pieces[number - 1])
    sizes = (8 * (pieces[0] + pieces[1]), 8 * (pieces[2] + pieces[3]))
    for x in range(4):
        x_step = lax.rem(x_index - x + 4, 4)
        for z in range(4):
            z_step = lax.rem(z_index - z + 4, 4)
            shard = held[z_step, pl.ds(pl.multiple_of(x_step * 32, 32), 32), :].astype(F32)
            row, lat = 0, (x % 2) * 4 + z
            for number, count in enumerate(pieces):
                base = (x // 2) * sizes[number // 2] + bases[number] + lat * count
                outs[number][pl.ds(base, count), :] = shard[row : row + count]
                row += count
    edge_part[...] = edge_rows[...].astype(BF)
    node_part[...] = node_rows[...].astype(BF)


def sum_far(pieces, scal, edge_own, e1, e2, e3, node_own, n1, n2, n3, keep, s1, s2, s3, er, nr, sent):
    z_index = scal[0]
    er[...] = sum((ref[...].astype(F32) for ref in (e1, e2, e3)), edge_own[...].astype(F32))
    nr[...] = sum((ref[...].astype(F32) for ref in (n1, n2, n3)), node_own[...].astype(F32))
    ins = (er, er, nr, nr)
    bases = []
    for number, count in enumerate(pieces):
        bases.append(0 if number % 2 == 0 else bases[-1] + 8 * pieces[number - 1])
    sizes = (8 * (pieces[0] + pieces[1]), 8 * (pieces[2] + pieces[3]))
    spare = 32 - sum(pieces)
    for x in range(4):
        for z in range(4):
            lat = (x % 2) * 4 + z
            parts = []
            for number, count in enumerate(pieces):
                base = (x // 2) * sizes[number // 2] + bases[number] + lat * count
                parts.append(ins[number][pl.ds(base, count), :])
            parts.append(jnp.zeros((spare, L), F32))
            sent[z, x] = jnp.concatenate(parts, axis=0)
    keep[...] = sent[z_index]
    for step, out in ((1, s1), (2, s2), (3, s3)):
        out[...] = sent[lax.rem(z_index + step, 4)].astype(BF)


def sum_z(scal, own, r1, r2, r3, keep, s1, s2, s3, held):
    x_index = scal[1]
    held[...] = own[...] + (r1[...].astype(F32) + r2[...].astype(F32) + r3[...].astype(F32))
    keep[...] = held[x_index]
    for step, out in ((1, s1), (2, s2), (3, s3)):
        out[...] = held[lax.rem(x_index + step, 4)].astype(BF)


def sum_x(own, r1, r2, r3, *outs):
    total = own[...] + (r1[...].astype(F32) + r2[...].astype(F32) + r3[...].astype(F32))
    row = 0
    for out in outs:
        count = out.shape[0]
        out[...] = total[row : row + count]
        row += count


def edge_forward(scal, ext, edges, offsets, *refs):
    shards, refs = refs[:8], refs[8:]
    gain, joined_out, first_out, normed_out, inverse_out, new_edges_out, partial_out = refs[:7]
    own_out, up_out, refs = refs[7], refs[8], refs[9:]
    joined, first, normed, inverse, new_edges, partial, w_in, w_out, second, sems, out_sems = refs
    tiles = edges.shape[0] // BLK
    lat_index, core, y_index, count = (scal[2 * tiles + i] for i in range(4))
    slabs = w_in.shape[0] // 3 // 32
    counts = (3 * L // slabs, L // slabs)
    stores = []

    def store(source, target):
        copy = pltpu.make_async_copy(source, target, out_sems.at[len(stores)])
        copy.start()
        stores.append(copy)

    store(ext.at[:, block_at(HB + lat_index)], own_out)
    store(ext.at[:, pl.ds(ext.shape[1] - BLK, BLK)], up_out)
    loads = copies([(edges, joined.at[:, pl.ds(0, L)])], sems)
    for t in range(tiles):
        rows = pl.ds(t * BLK, BLK)
        to_src = one_hot_columns(offsets[1, pl.ds(t, 1), :]).T.astype(BF)
        to_dst = one_hot_columns(offsets[0, pl.ds(t, 1), :]).T.astype(BF)
        src, dst = block_at(scal[tiles + t]), block_at(scal[t] + HB)
        joined[rows, pl.ds(L, L)] = dot_transpose(to_src, ext[:, src]).astype(BF)
        joined[rows, pl.ds(2 * L, L)] = dot_transpose(to_dst, ext[:, dst]).astype(BF)
    wait_all(loads)
    store(joined, joined_out)
    unpack_weights(core, y_index, shards, (w_in, w_out), counts)
    for n in range(2):
        columns = pl.ds(n * 256, 256)
        first[:, columns] = jnp.maximum(dot(joined[...], w_in[:, columns]), 0.0).astype(BF)
    store(first, first_out)
    for n in range(2):
        columns = pl.ds(n * 256, 256)
        second[:, columns] = dot(first[...], w_out[:, columns])
    partial[...] = jnp.zeros_like(partial)
    for t in range(tiles):
        rows = pl.ds(t * BLK, BLK)
        live = (lat_index * tiles + t < count).astype(F32)
        values, inv = norm_parts(second[rows, :])
        normed[rows, :] = values
        inverse[rows, :] = jnp.broadcast_to(inv, (BLK, BLK))
        message = values * gain[...] * live
        new_edges[rows, :] = (joined[rows, pl.ds(0, L)].astype(F32) + message).astype(BF)
        second[rows, :] = message
    store(normed, normed_out)
    store(inverse, inverse_out)
    store(new_edges, new_edges_out)
    for t in range(tiles):
        rows = pl.ds(t * BLK, BLK)
        into = one_hot_columns(offsets[0, pl.ds(t, 1), :]).astype(BF)
        high, middle, low = split_three(second[rows, :])
        block = scal[t]
        partial[block] = partial[block] + (dot(into, low) + dot(into, middle) + dot(into, high))
    store(partial, partial_out)
    wait_all(stores)


def node_step(scal, spread, own_hbm, up_hbm, *refs):
    shards, refs = refs[:8], refs[8:]
    gain, out, rows_out, direct_out, joined_out, first_out, d_second_out, d_first_out = refs[:8]
    own_turned, up_turned, w_in, w_out, joined, first, d_second, d_first = refs[8:16]
    d_direct, new_rows, sems, out_sems = refs[16:]
    core, y_index = scal[1], scal[2]
    slabs = w_in.shape[0] // 2 // 32
    counts = (2 * L // slabs, L // slabs)
    pairs = weight_pairs(core, y_index, shards, (w_in, w_out), counts)
    loads = copies([(own_hbm, own_turned), (up_hbm, up_turned)] + pairs[:4], sems)
    for source, target in pairs[4:]:
        target[...] = source[...]
    wait_all(loads)
    own = own_turned[...].astype(F32).T
    upstream = up_turned[...].astype(F32).T
    joined[:, pl.ds(0, L)] = own.astype(BF)
    total = spread[0]
    for l in range(1, spread.shape[0]):
        total = total + spread[l]
    joined[:, pl.ds(L, L)] = total.astype(BF)
    first[...] = jnp.maximum(dot(joined[...], w_in[...]), 0.0).astype(BF)
    normed, inverse = norm_parts(dot(first[...], w_out[...]))
    d_second[...] = norm_back(upstream, normed, inverse, gain[...]).astype(BF)
    back = dot_transpose(d_second[...], w_out[...])
    d_first[...] = jnp.where(first[...].astype(F32) > 0, back, 0.0).astype(BF)
    d_agg = dot_transpose(w_in[pl.ds(L, L), :], d_first[...]).astype(BF)
    for l in range(out.shape[0]):
        out[l] = d_agg
    new_rows[...] = (own + normed * gain[...]).T.astype(BF)
    d_direct[...] = dot_transpose(w_in[pl.ds(0, L), :], d_first[...])
    held = (new_rows, d_direct, joined, first, d_second, d_first)
    outs = (rows_out, direct_out, joined_out, first_out, d_second_out, d_first_out)
    wait_all(copies(zip(held, outs), out_sems))


def node_grads(scal, *refs):
    saved, (keep, send), refs = refs[:4], refs[4:6], refs[6:]
    held, (g_in, g_out, sems) = refs[:4], refs[4:]
    wait_all(copies(zip(saved, held), sems))
    joined, first, d_second, d_first = held
    g_out[...] = dot_rows(first[...], d_second[...])
    g_in[...] = dot_rows(joined[...], d_first[...])
    slabs = g_in.shape[0] // 2 // 32
    pack_grads(scal[1], scal[2], (g_in, g_out), keep, send, (2 * L // slabs, L // slabs))


def edge_backward(scal, d_agg, cot, offsets, gain, *refs):
    saved, w_out_shards, refs = refs[:4], refs[4:12], refs[12:]
    d_first, keep, send = refs[:3]
    joined, first, normed, inverse, w_in, w_out, d_second, g_in, g_out, sems = refs[3:]
    tiles = cot.shape[0] // BLK
    lat_index, core, y_index, count = (scal[2 * tiles + i] for i in range(4))
    slabs = w_in.shape[0] // 3 // 32
    counts = (3 * L // slabs, L // slabs)
    normed_in, inverse_in, first_in, joined_in = saved
    pairs = [(normed_in, normed), (inverse_in, inverse)]
    pairs += weight_pairs(core, y_index, w_out_shards, (w_in, w_out), counts)[1::2]
    pairs += [(first_in, first), (joined_in, joined)]
    loads = copies(pairs, sems)
    wait_all(loads[:2])
    for t in range(tiles):
        rows = pl.ds(t * BLK, BLK)
        live = (lat_index * tiles + t < count).astype(F32)
        to_dst = one_hot_columns(offsets[0, pl.ds(t, 1), :]).T.astype(BF)
        picked = dot_transpose(to_dst, d_agg[scal[t]])
        d_message = (cot[rows, :].astype(F32) + picked) * live
        back = norm_back(d_message, normed[rows, :], inverse[rows, pl.ds(0, 1)], gain[...])
        d_second[rows, :] = back.astype(BF)
    wait_all(loads[2:])
    for n in range(2):
        part = pl.ds(n * 256, 256)
        back = dot_transpose(d_second[...], w_out[part, :])
        d_first[:, part] = jnp.where(first[:, part].astype(F32) > 0, back, 0.0).astype(BF)
    for n in range(2):
        part = pl.ds(n * 256, 256)
        g_out[part, :] = dot_rows(first[:, part], d_second[...])
    for n in range(6):
        part = pl.ds(n * 256, 256)
        g_in[part, :] = dot_rows(joined[:, part], d_first[...])
    pack_grads(core, y_index, (g_in, g_out), keep, send, counts)


def edge_inputs(scal, d_first, offsets, direct_in, *refs):
    shards, refs = refs[:8], refs[8:]
    middle_out, lower, upper, d_direct, w_in, w_out, d_ext, d_turned, sems = refs
    tiles = d_first.shape[0] // BLK
    lat_index, core, y_index = (scal[2 * tiles + i] for i in range(3))
    slabs = w_in.shape[0] // 3 // 32
    counts = (3 * L // slabs, L // slabs)
    pairs = weight_pairs(core, y_index, shards, (w_in, w_out), counts)[::2]
    pairs += [(direct_in, d_direct)]
    loads = copies(pairs, sems)
    d_ext[...] = jnp.zeros_like(d_ext)
    wait_all(loads)
    for n in range(4):
        d_turned[pl.ds(n * 256, 256), :] = dot_transpose(
            w_in[pl.ds(L + n * 256, 256), :], d_first[...]
        )
    for t in range(tiles):
        rows = pl.ds(t * BLK, BLK)
        for row, place, at in ((1, scal[tiles + t], 0), (0, scal[t] + HB, L)):
            into = one_hot_columns(offsets[row, pl.ds(t, 1), :]).T.astype(BF)
            value = d_turned[pl.ds(at, L), rows]
            high = value.astype(BF)
            low = (value - high.astype(F32)).astype(BF)
            d_ext[place] = d_ext[place] + (dot(low, into) + dot(high, into))
    d_ext[HB + lat_index] = d_ext[HB + lat_index] + d_direct[...]
    blocks = middle_out.shape[0]
    for j in range(HB):
        lower[:, pl.ds(j * BLK, BLK)] = d_ext[j].astype(BF)
        upper[:, pl.ds(j * BLK, BLK)] = d_ext[HB + blocks + j].astype(BF)
    middle_out[...] = d_ext[pl.ds(HB, blocks)]


def edge_grads(scal, d_first, cot_in, *refs):
    shards, (grad_out, grad_edges, cot, w_in, w_out, sems, out_sems) = refs[:8], refs[8:]
    tiles = cot.shape[0] // BLK
    core, y_index = scal[2 * tiles + 1], scal[2 * tiles + 2]
    slabs = w_in.shape[0] // 3 // 32
    counts = (3 * L // slabs, L // slabs)
    pairs = weight_pairs(core, y_index, shards, (w_in, w_out), counts)[::2]
    wait_all(copies(pairs + [(cot_in, cot)], sems))
    for n in range(2):
        part = pl.ds(n * 256, 256)
        back = dot_transpose(d_first[...], w_in[part, :])
        grad_edges[:, part] = (cot[:, part].astype(F32) + back).astype(BF)
    wait_all(copies([(grad_edges, grad_out)], out_sems))


def add_halo(halo, middle, above, below, new_rows, columns, held):
    held[...] = middle[...]
    for j in range(HB):
        for place, value in ((halo[0, 0, j], above), (halo[0, 1, j], below)):
            held[place] = held[place] + value[:, pl.ds(j * BLK, BLK)].astype(F32)
    width = columns.shape[1]
    for block in range(held.shape[0]):
        for l in range(columns.shape[0]):
            columns[l, :, pl.ds(block * BLK, BLK)] = held[
                block, pl.ds(l * width, width), :
            ].astype(BF)
    last = pl.ds(held.shape[0] * BLK, BLK)
    for l in range(columns.shape[0]):
        columns[l, :, last] = new_rows[pl.ds(l * width, width), :]


def finish(arrived, out, new_nodes):
    cells = pl.ds(0, out.shape[1])
    total = arrived[0, :, cells].astype(F32)
    for l in range(1, arrived.shape[0]):
        total = total + arrived[l, :, cells].astype(F32)
    out[...] = total.astype(BF)
    for l in range(arrived.shape[0]):
        new_nodes[:, pl.ds(l * BLK, BLK)] = arrived[l, :, pl.ds(out.shape[1], BLK)]


def call(kernel, out_shape, scratch, mib, spaces, operands, flops=0, out_spaces="", sems=()):
    moved = sum(x.size * x.dtype.itemsize for x in operands)
    moved += sum(x.size * x.dtype.itemsize for x in out_shape)
    named = {"s": pltpu.SMEM, "v": pltpu.VMEM, "h": pltpu.HBM}
    out_spaces = out_spaces or "v" * len(out_shape)
    operands = [
        pltpu.with_memory_space_constraint(x, pltpu.HBM) if space == "h" else x
        for x, space in zip(operands, spaces)
    ]
    placed = [
        pltpu.HBM(x.shape, x.dtype) if space == "h" else x
        for x, space in zip(out_shape, out_spaces)
    ]
    return pl.pallas_call(
        kernel,
        out_shape=placed,
        in_specs=[pl.BlockSpec(memory_space=named[space]) for space in spaces],
        out_specs=[pl.BlockSpec(memory_space=named[space]) for space in out_spaces],
        scratch_shapes=[pltpu.VMEM(shape, dtype) for shape, dtype in scratch]
        + [pltpu.SemaphoreType.DMA((count,)) for count in sems],
        cost_estimate=pl.CostEstimate(flops=flops, bytes_accessed=moved, transcendentals=0),
        compiler_params=pltpu.CompilerParams(vmem_limit_bytes=mib << 20),
    )(*operands)


def run_edge_forward(scal, ext, edges, offsets, shards, gain, lat_size):
    rows = edges.shape[0]
    outs = [
        shape_of((rows, 3 * L), BF),
        shape_of((rows, L), BF),
        shape_of((rows, L), F32),
        shape_of((rows, BLK), F32),
        shape_of((rows, L), BF),
        shape_of((lat_size, BLK, L), F32),
    ]
    held = [(out.shape, out.dtype) for out in outs]
    outs += [shape_of((L, BLK), BF)] * 2
    return call(
        edge_forward,
        outs,
        held + [((3 * L, L), BF), ((L, L), BF), ((rows, L), F32)],
        EDGE_MIB,
        "svhv" + "v" * len(shards) + "v",
        (scal, ext, edges, offsets, *shards, gain),
        flops=2 * rows * 4 * L * L,
        out_spaces="h" * len(outs),
        sems=(1, len(outs)),
    )


def run_node_step(scal, spread, own, up, shards, gain):
    lat_size = spread.shape[0]
    rows = [((BLK, 2 * L), BF), ((BLK, L), BF), ((BLK, L), BF), ((BLK, L), BF)]
    return call(
        node_step,
        [shape_of((lat_size, L, BLK), BF), shape_of((L, BLK), BF), shape_of((L, BLK), F32)]
        + [shape_of(*row) for row in rows],
        [((L, BLK), BF), ((L, BLK), BF), ((2 * L, L), BF), ((L, L), BF)]
        + rows
        + [((L, BLK), F32), ((L, BLK), BF)],
        NODE_MIB,
        "svhhh" + "v" * (len(shards) - 1) + "v",
        (scal, spread, own, up, *shards, gain),
        flops=2 * BLK * 6 * L * L,
        out_spaces="vhhhhhh",
        sems=(2 + 4, 6),
    )


def run_node_grads(scal, saved, shard, y_count):
    return call(
        node_grads,
        [shape_of((y_count,) + shard.shape, BF)] * 2,
        [(one.shape, BF) for one in saved] + [((2 * L, L), F32), ((L, L), F32)],
        NODE_MIB,
        "shhhh",
        (scal, *saved),
        flops=2 * BLK * 3 * L * L,
        sems=(4,),
    )


def run_edge_backward(scal, d_agg, cot, offsets, gain, saved, shards):
    rows = cot.shape[0]
    chunk = (len(shards) // 2,) + shards[0].shape
    normed, inverse, first, joined = saved
    return call(
        edge_backward,
        [shape_of((rows, L), BF), shape_of(chunk, BF), shape_of(chunk, BF)],
        [
            (joined.shape, BF),
            (first.shape, BF),
            (normed.shape, F32),
            (inverse.shape, F32),
            ((3 * L, L), BF),
            ((L, L), BF),
            ((rows, L), BF),
            ((3 * L, L), F32),
            ((L, L), F32),
        ],
        BACK_MIB,
        "svvvv" + "h" * (len(saved) + len(shards)),
        (scal, d_agg, cot, offsets, gain, *saved, *shards),
        flops=2 * rows * 5 * L * L,
        sems=(4 + 2 * len(shards),),
    )


def run_edge_inputs(scal, d_first, offsets, d_direct, shards, lat_size):
    rows = d_first.shape[0]
    return call(
        edge_inputs,
        [
            shape_of((lat_size, L, BLK), F32),
            shape_of((L, HB * BLK), BF),
            shape_of((L, HB * BLK), BF),
        ],
        [
            (d_direct.shape, F32),
            ((3 * L, L), BF),
            ((L, L), BF),
            ((lat_size + 2 * HB, L, BLK), F32),
            ((2 * L, rows), F32),
        ],
        EDGE_MIB,
        "svvh" + "h" * len(shards),
        (scal, d_first, offsets, d_direct, *shards),
        flops=2 * rows * 2 * L * L,
        sems=(1 + 2 * len(shards),),
    )


def run_edge_grads(scal, d_first, cot, shards):
    rows = cot.shape[0]
    return call(
        edge_grads,
        [shape_of((rows, L), BF)],
        [((rows, L), BF), ((rows, L), BF), ((3 * L, L), BF), ((L, L), BF)],
        EDGE_MIB,
        "svh" + "h" * len(shards),
        (scal, d_first, cot, *shards),
        flops=2 * rows * L * L,
        out_spaces="h",
        sems=(1 + 2 * len(shards), 1),
    )


def swap_cores(value):
    return lax.ppermute(value, "c", [(0, 1), (1, 0)])


def shift(value, axes, step):
    count = lax.axis_size(axes)
    return lax.ppermute(value, axes, [(i, (i + step) % count) for i in range(count)])


def shifts(value, axes):
    return [value] + [shift(value, axes, k) for k in range(1, lax.axis_size(axes))]


def spread_rows(value, axes):
    return lax.all_to_all(value, axes, 0, 0)


def gather_far(value):
    mine = shifts(value, "y")
    return mine + [swap_cores(one) for one in mine]


def reduce_far(keep, send):
    arrived = swap_cores(send)
    both = [(keep[k].astype(F32) + arrived[k].astype(F32)).astype(BF) for k in range(keep.shape[0])]
    return [both[0]] + [shift(both[k], "y", k) for k in range(1, keep.shape[0])]


def per_device(
    nodes,
    edges,
    edge_tiles,
    edge_offsets,
    tile_counts,
    halo_blocks,
    w_edge_in,
    w_edge_out,
    w_node_in,
    w_node_out,
    edge_gain,
    node_gain,
    node_cotangent,
    edge_cotangent,
):
    lat_size = lax.axis_size(LAT)
    place = [lax.axis_index(LAT), lax.axis_index("c"), lax.axis_index("y")]
    slab_rows, width = nodes.shape
    own_rows = slab_rows // lat_size
    halo_rows = HB * BLK
    ext_rows = slab_rows + 2 * halo_rows
    weights = (w_edge_in, w_edge_out, w_node_in, w_node_out)
    pieces = tuple(weight.shape[0] for weight in weights)
    edge_rows = 2 * lat_size * (pieces[0] + pieces[1])
    node_rows = 2 * lat_size * (pieces[2] + pieces[3])

    near_scal = jnp.stack([lax.axis_index("z"), lax.axis_index(XS)]).astype(jnp.int32)
    node_scal = jnp.stack(place).astype(jnp.int32)
    scal = jnp.concatenate([edge_tiles.reshape(-1), node_scal, tile_counts])
    halo = halo_blocks
    offsets = edge_offsets.reshape(2, -1, BLK)
    edge_gain_row = edge_gain.reshape(1, L)
    node_gain_row = node_gain.reshape(1, L)

    turned = nodes.T
    up, down, packed = call(
        prepare,
        [
            shape_of((width, halo_rows), BF),
            shape_of((width, halo_rows), BF),
            shape_of((32, L), BF),
        ],
        [(weight.shape, BF) for weight in weights],
        4,
        "shhhhh",
        (halo, turned, *weights),
        sems=(4 + 2 * HB,),
    )
    from_lower = from_behind(up, 1)
    from_upper = from_behind(down, -1)

    (message_out,) = call(
        fill_message,
        [shape_of((lat_size, width, ext_rows + own_rows), BF)],
        [((width, ext_rows), BF), ((width, slab_rows), BF)],
        4,
        "vhvh",
        (from_lower, turned, from_upper, node_cotangent.T),
        out_spaces="h",
        sems=(2, 2 * lat_size),
    )
    by_x = jnp.concatenate(shifts(packed, XS), axis=0)
    near = shifts(by_x, "z")
    edge_part, node_part = call(
        functools.partial(assemble, pieces),
        [shape_of((edge_rows, L), BF), shape_of((node_rows, L), BF)],
        [((4, 128, L), BF), ((edge_rows, L), F32), ((node_rows, L), F32)],
        6,
        "svvvv",
        (near_scal, *near),
    )

    edge_shards = gather_far(edge_part)
    ext = spread_rows(message_out, LAT).reshape(L, ext_rows + own_rows)

    joined, first, normed, inverse, new_edges, partial, own, node_up = run_edge_forward(
        scal, ext, edges, offsets, edge_shards, edge_gain_row, lat_size
    )
    node_shards = gather_far(node_part)
    spread = spread_rows(partial, LAT)
    second_out, new_rows, d_direct, *node_saved = run_node_step(
        node_scal, spread, own, node_up, node_shards, node_gain_row
    )
    node_keep, node_send = run_node_grads(
        node_scal, node_saved, node_part, lax.axis_size("y")
    )
    second_in = spread_rows(second_out, LAT)
    node_far = reduce_far(node_keep, node_send)

    d_first, edge_keep, edge_send = run_edge_backward(
        scal, second_in, edge_cotangent, offsets, edge_gain_row,
        (normed, inverse, first, joined), edge_shards,
    )
    middle, lower, upper = run_edge_inputs(
        scal, d_first, offsets, d_direct, edge_shards, lat_size
    )
    from_above = from_behind(lower, -1)
    from_below = from_behind(upper, 1)
    (grad_edges,) = run_edge_grads(scal, d_first, edge_cotangent, edge_shards)
    edge_far = reduce_far(edge_keep, edge_send)
    (columns,) = call(
        add_halo,
        [shape_of((lat_size, width, slab_rows + own_rows), BF)],
        [((lat_size, L, BLK), F32)],
        8,
        "svvvv",
        (halo, middle, from_above, from_below, new_rows),
    )
    columns = spread_rows(columns, LAT)
    grad_slab, new_nodes = call(
        finish, [shape_of((width, slab_rows), BF)] * 2, [], 6, "v", (columns,)
    )

    shard = (32, L)
    shards = (4,) + shard
    kept, *sent = call(
        functools.partial(sum_far, pieces),
        [shape_of(shards, F32)] + [shape_of(shards, BF)] * 3,
        [((edge_rows, L), F32), ((node_rows, L), F32), ((4,) + shards, F32)],
        8,
        "s" + "v" * 8,
        (near_scal, *edge_far, *node_far),
    )
    moved = [shift(sent[k - 1], "z", k) for k in range(1, 4)]
    kept, *sent = call(
        sum_z,
        [shape_of(shard, F32)] + [shape_of(shard, BF)] * 3,
        [(shards, F32)],
        4,
        "s" + "v" * 4,
        (near_scal, kept, *moved),
    )
    moved = [shift(sent[k - 1], XS, k) for k in range(1, 4)]
    reduced = call(
        sum_x, [shape_of((count, L), F32) for count in pieces], [], 4, "v" * 4, (kept, *moved)
    )
    return (new_nodes.T, new_edges, grad_slab.T, grad_edges) + tuple(reduced)


def solution(mesh):
    fine = Mesh(mesh.devices.reshape(4, 2, 2, 2, 4), ("y", "xl", "c", "xh", "z"))
    every = SLAB + LAT
    by_rows = P(every, None)
    split = P(SLAB, LAT)
    placed = (
        split,
        by_rows,
        P(None, every),
        P(None, every),
        P(SLAB),
        P(SLAB, None, None),
        by_rows,
        by_rows,
        by_rows,
        by_rows,
        P(),
        P(),
        split,
        by_rows,
    )

    return jax.shard_map(
        per_device,
        mesh=fine,
        in_specs=placed,
        out_specs=(split, by_rows, split, by_rows, by_rows, by_rows, by_rows, by_rows),
        check_vma=False,
    )
```

```python
import functools

import jax
import jax.numpy as jnp
from jax import lax
from jax.experimental import pallas as pl
from jax.experimental.pallas import tpu as pltpu
from jax.sharding import Mesh, PartitionSpec as P


L = 512
BLK = 128
HB = 2
EPSILON = 1e-05

SLAB = ("y", "xl", "c")
LAT = ("xh", "z")
XS = ("xl", "xh")
BF = jnp.bfloat16
F32 = jnp.float32
EDGE_MIB = 16
NODE_MIB = 14
BACK_MIB = 28


def shape_of(shape, dtype):
    return jax.ShapeDtypeStruct(shape, dtype)


def from_behind(value, steps):
    count = lax.axis_size(SLAB)
    first, last = (max(0, -steps), min(count, count - steps))
    return lax.ppermute(value, SLAB, [(source, source + steps) for source in range(first, last)])


def dot(left, right):
    return jnp.dot(left, right, preferred_element_type=F32)


def dot_rows(left, right):
    return lax.dot_general(left, right, (((0,), (0,)), ((), ())), preferred_element_type=F32)


def dot_transpose(left, right):
    return lax.dot_general(left, right, (((1,), (1,)), ((), ())), preferred_element_type=F32)


def one_hot_columns(offsets):
    cells = lax.broadcasted_iota(jnp.int32, (BLK, BLK), 0)
    return (cells == offsets).astype(F32)


def norm_parts(values):
    average = jnp.mean(values, axis=-1, keepdims=True)
    centred = values - average
    variance = jnp.mean(centred * centred, axis=-1, keepdims=True)
    inverse = lax.rsqrt(variance + EPSILON)
    return centred * inverse, inverse


def norm_back(upstream, normed, inverse, gain_vector):
    scaled = upstream * gain_vector
    return inverse * (
        scaled
        - jnp.mean(scaled, axis=-1, keepdims=True)
        - normed * jnp.mean(scaled * normed, axis=-1, keepdims=True)
    )


def split_three(value):
    high = value.astype(BF)
    rest = value - high.astype(F32)
    middle = rest.astype(BF)
    return high, middle, (rest - middle.astype(F32)).astype(BF)


def block_at(number):
    return pl.ds(pl.multiple_of(number * BLK, BLK), BLK)


def copies(pairs, sems):
    made = [pltpu.make_async_copy(src, dst, sems.at[i]) for i, (src, dst) in enumerate(pairs)]
    for one in made:
        one.start()
    return made


def wait_all(made):
    for one in made:
        one.wait()


def weight_pairs(core, y_index, shards, outs, counts):
    total = sum(counts)
    y_count = len(shards) // 2
    pairs = []
    for number, source in enumerate(shards):
        step = number % y_count
        parity = core if number < y_count else 1 - core
        y = lax.rem(y_index - step + y_count, y_count)
        per = source.shape[0] // total
        for x in range(per):
            slab = (y * per + x) * 2 + parity
            at = x * total
            for out, count in zip(outs, counts):
                start = pl.multiple_of(slab * count, 32)
                pairs.append((source.at[pl.ds(at, count), :], out.at[pl.ds(start, count), :]))
                at += count
    return pairs


def unpack_weights(core, y_index, shards, outs, counts):
    for source, target in weight_pairs(core, y_index, shards, outs, counts):
        target[...] = source[...]


def pack_grads(core, y_index, grads, keep, send, counts):
    total = sum(counts)
    y_count = keep.shape[0]
    per = keep.shape[1] // total
    for target, parity in ((keep, core), (send, 1 - core)):
        for step in range(y_count):
            y = lax.rem(y_index + step, y_count)
            for x in range(per):
                at = x * total
                for grad, count in zip(grads, counts):
                    start = pl.multiple_of(((y * per + x) * 2 + parity) * count, 32)
                    target[step, pl.ds(at, count), :] = grad[pl.ds(start, count), :].astype(BF)
                    at += count


def prepare(halo, turned, *refs):
    weights, (up, down, packed), held, sems = refs[:4], refs[4:7], refs[7:-1], refs[-1]
    pairs = list(zip(weights, held))
    for j in range(HB):
        part = pl.ds(j * BLK, BLK)
        pairs.append((turned.at[:, block_at(halo[0, 0, j])], up.at[:, part]))
        pairs.append((turned.at[:, block_at(halo[0, 1, j])], down.at[:, part]))
    wait_all(copies(pairs, sems))
    parts = [ref[...].astype(F32) for ref in held]
    used = sum(part.shape[0] for part in parts)
    parts.append(jnp.zeros((packed.shape[0] - used, L), F32))
    packed[...] = jnp.concatenate(parts, axis=0).astype(BF)


def fill_message(lower, turned, upper, cot, out, table, held, in_sems, sems):
    rows, halo_rows = turned.shape[1], lower.shape[1]
    loads = copies([(turned, table.at[:, pl.ds(halo_rows, rows)]), (cot, held)], in_sems)
    table[:, pl.ds(0, halo_rows)] = lower[...]
    table[:, pl.ds(halo_rows + rows, halo_rows)] = upper[...]
    wait_all(loads)
    pairs = []
    for l in range(out.shape[0]):
        pairs.append((table, out.at[l, :, pl.ds(0, table.shape[1])]))
        part = out.at[l, :, pl.ds(table.shape[1], BLK)]
        pairs.append((held.at[:, pl.ds(l * BLK, BLK)], part))
    wait_all(copies(pairs, sems))


def assemble(pieces, scal, *refs):
    blocks, (edge_part, node_part, held, edge_rows, node_rows) = refs[:4], refs[4:]
    z_index, x_index = scal[0], scal[1]
    for k, block in enumerate(blocks):
        held[k] = block[...]
    outs = (edge_rows, edge_rows, node_rows, node_rows)
    bases = []
    for number, count in enumerate(pieces):
        bases.append(0 if number % 2 == 0 else bases[-1] + 8 * pieces[number - 1])
    sizes = (8 * (pieces[0] + pieces[1]), 8 * (pieces[2] + pieces[3]))
    for x in range(4):
        x_step = lax.rem(x_index - x + 4, 4)
        for z in range(4):
            z_step = lax.rem(z_index - z + 4, 4)
            shard = held[z_step, pl.ds(pl.multiple_of(x_step * 32, 32), 32), :].astype(F32)
            row, lat = 0, (x % 2) * 4 + z
            for number, count in enumerate(pieces):
                base = (x // 2) * sizes[number // 2] + bases[number] + lat * count
                outs[number][pl.ds(base, count), :] = shard[row : row + count]
                row += count
    edge_part[...] = edge_rows[...].astype(BF)
    node_part[...] = node_rows[...].astype(BF)


def sum_far(pieces, scal, edge_own, e1, e2, e3, node_own, n1, n2, n3, keep, s1, s2, s3, er, nr, sent):
    z_index = scal[0]
    er[...] = sum((ref[...].astype(F32) for ref in (e1, e2, e3)), edge_own[...].astype(F32))
    nr[...] = sum((ref[...].astype(F32) for ref in (n1, n2, n3)), node_own[...].astype(F32))
    ins = (er, er, nr, nr)
    bases = []
    for number, count in enumerate(pieces):
        bases.append(0 if number % 2 == 0 else bases[-1] + 8 * pieces[number - 1])
    sizes = (8 * (pieces[0] + pieces[1]), 8 * (pieces[2] + pieces[3]))
    spare = 32 - sum(pieces)
    for x in range(4):
        for z in range(4):
            lat = (x % 2) * 4 + z
            parts = []
            for number, count in enumerate(pieces):
                base = (x // 2) * sizes[number // 2] + bases[number] + lat * count
                parts.append(ins[number][pl.ds(base, count), :])
            parts.append(jnp.zeros((spare, L), F32))
            sent[z, x] = jnp.concatenate(parts, axis=0)
    keep[...] = sent[z_index]
    for step, out in ((1, s1), (2, s2), (3, s3)):
        out[...] = sent[lax.rem(z_index + step, 4)].astype(BF)


def sum_z(scal, own, r1, r2, r3, keep, s1, s2, s3, held):
    x_index = scal[1]
    held[...] = own[...] + (r1[...].astype(F32) + r2[...].astype(F32) + r3[...].astype(F32))
    keep[...] = held[x_index]
    for step, out in ((1, s1), (2, s2), (3, s3)):
        out[...] = held[lax.rem(x_index + step, 4)].astype(BF)


def sum_x(own, r1, r2, r3, *outs):
    total = own[...] + (r1[...].astype(F32) + r2[...].astype(F32) + r3[...].astype(F32))
    row = 0
    for out in outs:
        count = out.shape[0]
        out[...] = total[row : row + count]
        row += count


def edge_forward(scal, ext, edges, offsets, *refs):
    shards, refs = refs[:8], refs[8:]
    gain, joined_out, first_out, normed_out, inverse_out, new_edges_out, partial_out = refs[:7]
    own_out, up_out, refs = refs[7], refs[8], refs[9:]
    joined, first, normed, inverse, new_edges, partial, w_in, w_out, second, sems, out_sems = refs
    tiles = edges.shape[0] // BLK
    lat_index, core, y_index, count = (scal[2 * tiles + i] for i in range(4))
    slabs = w_in.shape[0] // 3 // 32
    counts = (3 * L // slabs, L // slabs)
    stores = []

    def store(source, target):
        copy = pltpu.make_async_copy(source, target, out_sems.at[len(stores)])
        copy.start()
        stores.append(copy)

    store(ext.at[:, block_at(HB + lat_index)], own_out)
    store(ext.at[:, pl.ds(ext.shape[1] - BLK, BLK)], up_out)
    loads = copies([(edges, joined.at[:, pl.ds(0, L)])], sems)
    for t in range(tiles):
        rows = pl.ds(t * BLK, BLK)
        to_src = one_hot_columns(offsets[1, pl.ds(t, 1), :]).T.astype(BF)
        to_dst = one_hot_columns(offsets[0, pl.ds(t, 1), :]).T.astype(BF)
        src, dst = block_at(scal[tiles + t]), block_at(scal[t] + HB)
        joined[rows, pl.ds(L, L)] = dot_transpose(to_src, ext[:, src]).astype(BF)
        joined[rows, pl.ds(2 * L, L)] = dot_transpose(to_dst, ext[:, dst]).astype(BF)
    wait_all(loads)
    store(joined, joined_out)
    unpack_weights(core, y_index, shards, (w_in, w_out), counts)
    for n in range(2):
        columns = pl.ds(n * 256, 256)
        first[:, columns] = jnp.maximum(dot(joined[...], w_in[:, columns]), 0.0).astype(BF)
    store(first, first_out)
    for n in range(2):
        columns = pl.ds(n * 256, 256)
        second[:, columns] = dot(first[...], w_out[:, columns])
    partial[...] = jnp.zeros_like(partial)
    for t in range(tiles):
        rows = pl.ds(t * BLK, BLK)
        live = (lat_index * tiles + t < count).astype(F32)
        values, inv = norm_parts(second[rows, :])
        normed[rows, :] = values
        inverse[rows, :] = jnp.broadcast_to(inv, (BLK, BLK))
        message = values * gain[...] * live
        new_edges[rows, :] = (joined[rows, pl.ds(0, L)].astype(F32) + message).astype(BF)
        second[rows, :] = message
    store(normed, normed_out)
    store(inverse, inverse_out)
    store(new_edges, new_edges_out)
    for t in range(tiles):
        rows = pl.ds(t * BLK, BLK)
        into = one_hot_columns(offsets[0, pl.ds(t, 1), :]).astype(BF)
        high, middle, low = split_three(second[rows, :])
        block = scal[t]
        partial[block] = partial[block] + (dot(into, low) + dot(into, middle) + dot(into, high))
    store(partial, partial_out)
    wait_all(stores)


def node_step(scal, spread, own_hbm, up_hbm, *refs):
    shards, refs = refs[:8], refs[8:]
    gain, out, rows_out, direct_out, joined_out, first_out, d_second_out, d_first_out = refs[:8]
    own_turned, up_turned, w_in, w_out, joined, first, d_second, d_first = refs[8:16]
    d_direct, new_rows, sems, out_sems = refs[16:]
    core, y_index = scal[1], scal[2]
    slabs = w_in.shape[0] // 2 // 32
    counts = (2 * L // slabs, L // slabs)
    pairs = weight_pairs(core, y_index, shards, (w_in, w_out), counts)
    loads = copies([(own_hbm, own_turned), (up_hbm, up_turned)] + pairs[:4], sems)
    for source, target in pairs[4:]:
        target[...] = source[...]
    wait_all(loads)
    own = own_turned[...].astype(F32).T
    upstream = up_turned[...].astype(F32).T
    joined[:, pl.ds(0, L)] = own.astype(BF)
    total = spread[0]
    for l in range(1, spread.shape[0]):
        total = total + spread[l]
    joined[:, pl.ds(L, L)] = total.astype(BF)
    first[...] = jnp.maximum(dot(joined[...], w_in[...]), 0.0).astype(BF)
    normed, inverse = norm_parts(dot(first[...], w_out[...]))
    d_second[...] = norm_back(upstream, normed, inverse, gain[...]).astype(BF)
    back = dot_transpose(d_second[...], w_out[...])
    d_first[...] = jnp.where(first[...].astype(F32) > 0, back, 0.0).astype(BF)
    d_agg = dot_transpose(w_in[pl.ds(L, L), :], d_first[...]).astype(BF)
    for l in range(out.shape[0]):
        out[l] = d_agg
    new_rows[...] = (own + normed * gain[...]).T.astype(BF)
    d_direct[...] = dot_transpose(w_in[pl.ds(0, L), :], d_first[...])
    held = (new_rows, d_direct, joined, first, d_second, d_first)
    outs = (rows_out, direct_out, joined_out, first_out, d_second_out, d_first_out)
    wait_all(copies(zip(held, outs), out_sems))


def node_grads(scal, *refs):
    saved, (keep, send), refs = refs[:4], refs[4:6], refs[6:]
    held, (g_in, g_out, sems) = refs[:4], refs[4:]
    wait_all(copies(zip(saved, held), sems))
    joined, first, d_second, d_first = held
    g_out[...] = dot_rows(first[...], d_second[...])
    g_in[...] = dot_rows(joined[...], d_first[...])
    slabs = g_in.shape[0] // 2 // 32
    pack_grads(scal[1], scal[2], (g_in, g_out), keep, send, (2 * L // slabs, L // slabs))


def edge_backward(scal, d_agg, cot, offsets, gain, *refs):
    saved, w_out_shards, refs = refs[:4], refs[4:12], refs[12:]
    d_first, d_first_out, keep, send = refs[:4]
    joined, first, normed, inverse, w_in, w_out, d_second, g_in, g_out, sems, out_sems = refs[4:]
    tiles = cot.shape[0] // BLK
    lat_index, core, y_index, count = (scal[2 * tiles + i] for i in range(4))
    slabs = w_in.shape[0] // 3 // 32
    counts = (3 * L // slabs, L // slabs)
    normed_in, inverse_in, first_in, joined_in = saved
    pairs = [(normed_in, normed), (inverse_in, inverse)]
    pairs += weight_pairs(core, y_index, w_out_shards, (w_in, w_out), counts)[1::2]
    pairs += [(first_in, first), (joined_in, joined)]
    loads = copies(pairs, sems)
    wait_all(loads[:2])
    for t in range(tiles):
        rows = pl.ds(t * BLK, BLK)
        live = (lat_index * tiles + t < count).astype(F32)
        to_dst = one_hot_columns(offsets[0, pl.ds(t, 1), :]).T.astype(BF)
        picked = dot_transpose(to_dst, d_agg[scal[t]])
        d_message = (cot[rows, :].astype(F32) + picked) * live
        back = norm_back(d_message, normed[rows, :], inverse[rows, pl.ds(0, 1)], gain[...])
        d_second[rows, :] = back.astype(BF)
    wait_all(loads[2:])
    for n in range(2):
        part = pl.ds(n * 256, 256)
        back = dot_transpose(d_second[...], w_out[part, :])
        d_first[:, part] = jnp.where(first[:, part].astype(F32) > 0, back, 0.0).astype(BF)
    store = copies([(d_first, d_first_out)], out_sems)
    for n in range(2):
        part = pl.ds(n * 256, 256)
        g_out[part, :] = dot_rows(first[:, part], d_second[...])
    for n in range(6):
        part = pl.ds(n * 256, 256)
        g_in[part, :] = dot_rows(joined[:, part], d_first[...])
    pack_grads(core, y_index, (g_in, g_out), keep, send, counts)
    wait_all(store)


def edge_inputs(scal, d_first, offsets, direct_in, *refs):
    shards, refs = refs[:8], refs[8:]
    middle_out, lower, upper, d_direct, w_in, w_out, d_ext, d_turned, sems = refs
    tiles = d_first.shape[0] // BLK
    lat_index, core, y_index = (scal[2 * tiles + i] for i in range(3))
    slabs = w_in.shape[0] // 3 // 32
    counts = (3 * L // slabs, L // slabs)
    pairs = weight_pairs(core, y_index, shards, (w_in, w_out), counts)[::2]
    pairs += [(direct_in, d_direct)]
    loads = copies(pairs, sems)
    d_ext[...] = jnp.zeros_like(d_ext)
    wait_all(loads)
    for n in range(4):
        d_turned[pl.ds(n * 256, 256), :] = dot_transpose(
            w_in[pl.ds(L + n * 256, 256), :], d_first[...]
        )
    for t in range(tiles):
        rows = pl.ds(t * BLK, BLK)
        for row, place, at in ((1, scal[tiles + t], 0), (0, scal[t] + HB, L)):
            into = one_hot_columns(offsets[row, pl.ds(t, 1), :]).T.astype(BF)
            value = d_turned[pl.ds(at, L), rows]
            high = value.astype(BF)
            low = (value - high.astype(F32)).astype(BF)
            d_ext[place] = d_ext[place] + (dot(low, into) + dot(high, into))
    d_ext[HB + lat_index] = d_ext[HB + lat_index] + d_direct[...]
    blocks = middle_out.shape[0]
    for j in range(HB):
        lower[:, pl.ds(j * BLK, BLK)] = d_ext[j].astype(BF)
        upper[:, pl.ds(j * BLK, BLK)] = d_ext[HB + blocks + j].astype(BF)
    middle_out[...] = d_ext[pl.ds(HB, blocks)]


def edge_grads(scal, d_first_in, cot_in, *refs):
    shards, refs = refs[:8], refs[8:]
    grad_out, grad_edges, cot, d_first, w_in, w_out, sems, out_sems = refs
    tiles = cot.shape[0] // BLK
    core, y_index = scal[2 * tiles + 1], scal[2 * tiles + 2]
    slabs = w_in.shape[0] // 3 // 32
    counts = (3 * L // slabs, L // slabs)
    pairs = weight_pairs(core, y_index, shards, (w_in, w_out), counts)[::2]
    wait_all(copies(pairs + [(cot_in, cot), (d_first_in, d_first)], sems))
    for n in range(2):
        part = pl.ds(n * 256, 256)
        back = dot_transpose(d_first[...], w_in[part, :])
        grad_edges[:, part] = (cot[:, part].astype(F32) + back).astype(BF)
    wait_all(copies([(grad_edges, grad_out)], out_sems))


def add_halo(halo, middle, above, below, new_rows, columns, held):
    held[...] = middle[...]
    for j in range(HB):
        for place, value in ((halo[0, 0, j], above), (halo[0, 1, j], below)):
            held[place] = held[place] + value[:, pl.ds(j * BLK, BLK)].astype(F32)
    width = columns.shape[1]
    for block in range(held.shape[0]):
        for l in range(columns.shape[0]):
            columns[l, :, pl.ds(block * BLK, BLK)] = held[
                block, pl.ds(l * width, width), :
            ].astype(BF)
    last = pl.ds(held.shape[0] * BLK, BLK)
    for l in range(columns.shape[0]):
        columns[l, :, last] = new_rows[pl.ds(l * width, width), :]


def finish(arrived, out, new_nodes):
    cells = pl.ds(0, out.shape[1])
    total = arrived[0, :, cells].astype(F32)
    for l in range(1, arrived.shape[0]):
        total = total + arrived[l, :, cells].astype(F32)
    out[...] = total.astype(BF)
    for l in range(arrived.shape[0]):
        new_nodes[:, pl.ds(l * BLK, BLK)] = arrived[l, :, pl.ds(out.shape[1], BLK)]


def call(kernel, out_shape, scratch, mib, spaces, operands, flops=0, out_spaces="", sems=()):
    moved = sum(x.size * x.dtype.itemsize for x in operands)
    moved += sum(x.size * x.dtype.itemsize for x in out_shape)
    named = {"s": pltpu.SMEM, "v": pltpu.VMEM, "h": pltpu.HBM}
    out_spaces = out_spaces or "v" * len(out_shape)
    operands = [
        pltpu.with_memory_space_constraint(x, pltpu.HBM) if space == "h" else x
        for x, space in zip(operands, spaces)
    ]
    placed = [
        pltpu.HBM(x.shape, x.dtype) if space == "h" else x
        for x, space in zip(out_shape, out_spaces)
    ]
    return pl.pallas_call(
        kernel,
        out_shape=placed,
        in_specs=[pl.BlockSpec(memory_space=named[space]) for space in spaces],
        out_specs=[pl.BlockSpec(memory_space=named[space]) for space in out_spaces],
        scratch_shapes=[pltpu.VMEM(shape, dtype) for shape, dtype in scratch]
        + [pltpu.SemaphoreType.DMA((count,)) for count in sems],
        cost_estimate=pl.CostEstimate(flops=flops, bytes_accessed=moved, transcendentals=0),
        compiler_params=pltpu.CompilerParams(vmem_limit_bytes=mib << 20),
    )(*operands)


def run_edge_forward(scal, ext, edges, offsets, shards, gain, lat_size):
    rows = edges.shape[0]
    outs = [
        shape_of((rows, 3 * L), BF),
        shape_of((rows, L), BF),
        shape_of((rows, L), F32),
        shape_of((rows, BLK), F32),
        shape_of((rows, L), BF),
        shape_of((lat_size, BLK, L), F32),
    ]
    held = [(out.shape, out.dtype) for out in outs]
    outs += [shape_of((L, BLK), BF)] * 2
    return call(
        edge_forward,
        outs,
        held + [((3 * L, L), BF), ((L, L), BF), ((rows, L), F32)],
        EDGE_MIB,
        "svhv" + "v" * len(shards) + "v",
        (scal, ext, edges, offsets, *shards, gain),
        flops=2 * rows * 4 * L * L,
        out_spaces="h" * len(outs),
        sems=(1, len(outs)),
    )


def run_node_step(scal, spread, own, up, shards, gain):
    lat_size = spread.shape[0]
    rows = [((BLK, 2 * L), BF), ((BLK, L), BF), ((BLK, L), BF), ((BLK, L), BF)]
    return call(
        node_step,
        [shape_of((lat_size, L, BLK), BF), shape_of((L, BLK), BF), shape_of((L, BLK), F32)]
        + [shape_of(*row) for row in rows],
        [((L, BLK), BF), ((L, BLK), BF), ((2 * L, L), BF), ((L, L), BF)]
        + rows
        + [((L, BLK), F32), ((L, BLK), BF)],
        NODE_MIB,
        "svhhh" + "v" * (len(shards) - 1) + "v",
        (scal, spread, own, up, *shards, gain),
        flops=2 * BLK * 6 * L * L,
        out_spaces="vhhhhhh",
        sems=(2 + 4, 6),
    )


def run_node_grads(scal, saved, shard, y_count):
    return call(
        node_grads,
        [shape_of((y_count,) + shard.shape, BF)] * 2,
        [(one.shape, BF) for one in saved] + [((2 * L, L), F32), ((L, L), F32)],
        NODE_MIB,
        "shhhh",
        (scal, *saved),
        flops=2 * BLK * 3 * L * L,
        sems=(4,),
    )


def run_edge_backward(scal, d_agg, cot, offsets, gain, saved, shards):
    rows = cot.shape[0]
    chunk = (len(shards) // 2,) + shards[0].shape
    normed, inverse, first, joined = saved
    return call(
        edge_backward,
        [shape_of((rows, L), BF)] * 2 + [shape_of(chunk, BF)] * 2,
        [
            (joined.shape, BF),
            (first.shape, BF),
            (normed.shape, F32),
            (inverse.shape, F32),
            ((3 * L, L), BF),
            ((L, L), BF),
            ((rows, L), BF),
            ((3 * L, L), F32),
            ((L, L), F32),
        ],
        BACK_MIB,
        "svvvv" + "h" * (len(saved) + len(shards)),
        (scal, d_agg, cot, offsets, gain, *saved, *shards),
        flops=2 * rows * 5 * L * L,
        out_spaces="vhvv",
        sems=(4 + 2 * len(shards), 1),
    )


def run_edge_inputs(scal, d_first, offsets, d_direct, shards, lat_size):
    rows = d_first.shape[0]
    return call(
        edge_inputs,
        [
            shape_of((lat_size, L, BLK), F32),
            shape_of((L, HB * BLK), BF),
            shape_of((L, HB * BLK), BF),
        ],
        [
            (d_direct.shape, F32),
            ((3 * L, L), BF),
            ((L, L), BF),
            ((lat_size + 2 * HB, L, BLK), F32),
            ((2 * L, rows), F32),
        ],
        EDGE_MIB,
        "svvh" + "h" * len(shards),
        (scal, d_first, offsets, d_direct, *shards),
        flops=2 * rows * 2 * L * L,
        sems=(1 + 2 * len(shards),),
    )


def run_edge_grads(scal, d_first, cot, shards):
    rows = cot.shape[0]
    return call(
        edge_grads,
        [shape_of((rows, L), BF)],
        [((rows, L), BF)] * 3 + [((3 * L, L), BF), ((L, L), BF)],
        EDGE_MIB,
        "shh" + "h" * len(shards),
        (scal, d_first, cot, *shards),
        flops=2 * rows * L * L,
        out_spaces="h",
        sems=(2 + 2 * len(shards), 1),
    )


def swap_cores(value):
    return lax.ppermute(value, "c", [(0, 1), (1, 0)])


def shift(value, axes, step):
    count = lax.axis_size(axes)
    return lax.ppermute(value, axes, [(i, (i + step) % count) for i in range(count)])


def shifts(value, axes):
    return [value] + [shift(value, axes, k) for k in range(1, lax.axis_size(axes))]


def spread_rows(value, axes):
    return lax.all_to_all(value, axes, 0, 0)


def gather_far(value):
    mine = shifts(value, "y")
    return mine + [swap_cores(one) for one in mine]


def reduce_far(keep, send):
    arrived = swap_cores(send)
    both = [(keep[k].astype(F32) + arrived[k].astype(F32)).astype(BF) for k in range(keep.shape[0])]
    return [both[0]] + [shift(both[k], "y", k) for k in range(1, keep.shape[0])]


def per_device(
    nodes,
    edges,
    edge_tiles,
    edge_offsets,
    tile_counts,
    halo_blocks,
    w_edge_in,
    w_edge_out,
    w_node_in,
    w_node_out,
    edge_gain,
    node_gain,
    node_cotangent,
    edge_cotangent,
):
    lat_size = lax.axis_size(LAT)
    place = [lax.axis_index(LAT), lax.axis_index("c"), lax.axis_index("y")]
    slab_rows, width = nodes.shape
    own_rows = slab_rows // lat_size
    halo_rows = HB * BLK
    ext_rows = slab_rows + 2 * halo_rows
    weights = (w_edge_in, w_edge_out, w_node_in, w_node_out)
    pieces = tuple(weight.shape[0] for weight in weights)
    edge_rows = 2 * lat_size * (pieces[0] + pieces[1])
    node_rows = 2 * lat_size * (pieces[2] + pieces[3])

    near_scal = jnp.stack([lax.axis_index("z"), lax.axis_index(XS)]).astype(jnp.int32)
    node_scal = jnp.stack(place).astype(jnp.int32)
    scal = jnp.concatenate([edge_tiles.reshape(-1), node_scal, tile_counts])
    halo = halo_blocks
    offsets = edge_offsets.reshape(2, -1, BLK)
    edge_gain_row = edge_gain.reshape(1, L)
    node_gain_row = node_gain.reshape(1, L)

    turned = nodes.T
    up, down, packed = call(
        prepare,
        [
            shape_of((width, halo_rows), BF),
            shape_of((width, halo_rows), BF),
            shape_of((32, L), BF),
        ],
        [(weight.shape, BF) for weight in weights],
        4,
        "shhhhh",
        (halo, turned, *weights),
        sems=(4 + 2 * HB,),
    )
    from_lower = from_behind(up, 1)
    from_upper = from_behind(down, -1)

    (message_out,) = call(
        fill_message,
        [shape_of((lat_size, width, ext_rows + own_rows), BF)],
        [((width, ext_rows), BF), ((width, slab_rows), BF)],
        4,
        "vhvh",
        (from_lower, turned, from_upper, node_cotangent.T),
        out_spaces="h",
        sems=(2, 2 * lat_size),
    )
    by_x = jnp.concatenate(shifts(packed, XS), axis=0)
    near = shifts(by_x, "z")
    edge_part, node_part = call(
        functools.partial(assemble, pieces),
        [shape_of((edge_rows, L), BF), shape_of((node_rows, L), BF)],
        [((4, 128, L), BF), ((edge_rows, L), F32), ((node_rows, L), F32)],
        6,
        "svvvv",
        (near_scal, *near),
    )

    edge_shards = gather_far(edge_part)
    ext = spread_rows(message_out, LAT).reshape(L, ext_rows + own_rows)

    joined, first, normed, inverse, new_edges, partial, own, node_up = run_edge_forward(
        scal, ext, edges, offsets, edge_shards, edge_gain_row, lat_size
    )
    node_shards = gather_far(node_part)
    spread = spread_rows(partial, LAT)
    second_out, new_rows, d_direct, *node_saved = run_node_step(
        node_scal, spread, own, node_up, node_shards, node_gain_row
    )
    node_keep, node_send = run_node_grads(
        node_scal, node_saved, node_part, lax.axis_size("y")
    )
    second_in = spread_rows(second_out, LAT)
    node_far = reduce_far(node_keep, node_send)

    d_first, d_first_kept, edge_keep, edge_send = run_edge_backward(
        scal, second_in, edge_cotangent, offsets, edge_gain_row,
        (normed, inverse, first, joined), edge_shards,
    )
    middle, lower, upper = run_edge_inputs(
        scal, d_first, offsets, d_direct, edge_shards, lat_size
    )
    from_above = from_behind(lower, -1)
    from_below = from_behind(upper, 1)
    (grad_edges,) = run_edge_grads(scal, d_first_kept, edge_cotangent, edge_shards)
    edge_far = reduce_far(edge_keep, edge_send)
    (columns,) = call(
        add_halo,
        [shape_of((lat_size, width, slab_rows + own_rows), BF)],
        [((lat_size, L, BLK), F32)],
        8,
        "svvvv",
        (halo, middle, from_above, from_below, new_rows),
    )
    columns = spread_rows(columns, LAT)
    grad_slab, new_nodes = call(
        finish, [shape_of((width, slab_rows), BF)] * 2, [], 6, "v", (columns,)
    )

    shard = (32, L)
    shards = (4,) + shard
    kept, *sent = call(
        functools.partial(sum_far, pieces),
        [shape_of(shards, F32)] + [shape_of(shards, BF)] * 3,
        [((edge_rows, L), F32), ((node_rows, L), F32), ((4,) + shards, F32)],
        8,
        "s" + "v" * 8,
        (near_scal, *edge_far, *node_far),
    )
    moved = [shift(sent[k - 1], "z", k) for k in range(1, 4)]
    kept, *sent = call(
        sum_z,
        [shape_of(shard, F32)] + [shape_of(shard, BF)] * 3,
        [(shards, F32)],
        4,
        "s" + "v" * 4,
        (near_scal, kept, *moved),
    )
    moved = [shift(sent[k - 1], XS, k) for k in range(1, 4)]
    reduced = call(
        sum_x, [shape_of((count, L), F32) for count in pieces], [], 4, "v" * 4, (kept, *moved)
    )
    return (new_nodes.T, new_edges, grad_slab.T, grad_edges) + tuple(reduced)


def solution(mesh):
    fine = Mesh(mesh.devices.reshape(4, 2, 2, 2, 4), ("y", "xl", "c", "xh", "z"))
    every = SLAB + LAT
    by_rows = P(every, None)
    split = P(SLAB, LAT)
    placed = (
        split,
        by_rows,
        P(None, every),
        P(None, every),
        P(SLAB),
        P(SLAB, None, None),
        by_rows,
        by_rows,
        by_rows,
        by_rows,
        P(),
        P(),
        split,
        by_rows,
    )

    return jax.shard_map(
        per_device,
        mesh=fine,
        in_specs=placed,
        out_specs=(split, by_rows, split, by_rows, by_rows, by_rows, by_rows, by_rows),
        check_vma=False,
    )
```

```python
import functools

import jax
import jax.numpy as jnp
from jax import lax
from jax.experimental import pallas as pl
from jax.experimental.pallas import tpu as pltpu
from jax.sharding import Mesh, PartitionSpec as P


L = 512
BLK = 128
HB = 2
EPSILON = 1e-05

SLAB = ("y", "xl", "c")
LAT = ("xh", "z")
XS = ("xl", "xh")
BF = jnp.bfloat16
F32 = jnp.float32
EDGE_MIB = 16
NODE_MIB = 14
BACK_MIB = 28


def shape_of(shape, dtype):
    return jax.ShapeDtypeStruct(shape, dtype)


def from_behind(value, steps):
    count = lax.axis_size(SLAB)
    first, last = (max(0, -steps), min(count, count - steps))
    return lax.ppermute(value, SLAB, [(source, source + steps) for source in range(first, last)])


def dot(left, right):
    return jnp.dot(left, right, preferred_element_type=F32)


def dot_rows(left, right):
    return lax.dot_general(left, right, (((0,), (0,)), ((), ())), preferred_element_type=F32)


def dot_transpose(left, right):
    return lax.dot_general(left, right, (((1,), (1,)), ((), ())), preferred_element_type=F32)


def one_hot_columns(offsets):
    cells = lax.broadcasted_iota(jnp.int32, (BLK, BLK), 0)
    return (cells == offsets).astype(F32)


def norm_parts(values):
    average = jnp.mean(values, axis=-1, keepdims=True)
    centred = values - average
    variance = jnp.mean(centred * centred, axis=-1, keepdims=True)
    inverse = lax.rsqrt(variance + EPSILON)
    return centred * inverse, inverse


def norm_back(upstream, normed, inverse, gain_vector):
    scaled = upstream * gain_vector
    return inverse * (
        scaled
        - jnp.mean(scaled, axis=-1, keepdims=True)
        - normed * jnp.mean(scaled * normed, axis=-1, keepdims=True)
    )


def split_three(value):
    high = value.astype(BF)
    rest = value - high.astype(F32)
    middle = rest.astype(BF)
    return high, middle, (rest - middle.astype(F32)).astype(BF)


def block_at(number):
    return pl.ds(pl.multiple_of(number * BLK, BLK), BLK)


def copies(pairs, sems):
    made = [pltpu.make_async_copy(src, dst, sems.at[i]) for i, (src, dst) in enumerate(pairs)]
    for one in made:
        one.start()
    return made


def wait_all(made):
    for one in made:
        one.wait()


def weight_pairs(core, y_index, shards, outs, counts):
    total = sum(counts)
    y_count = len(shards) // 2
    pairs = []
    for number, source in enumerate(shards):
        step = number % y_count
        parity = core if number < y_count else 1 - core
        y = lax.rem(y_index - step + y_count, y_count)
        per = source.shape[0] // total
        for x in range(per):
            slab = (y * per + x) * 2 + parity
            at = x * total
            for out, count in zip(outs, counts):
                start = pl.multiple_of(slab * count, 32)
                pairs.append((source.at[pl.ds(at, count), :], out.at[pl.ds(start, count), :]))
                at += count
    return pairs


def unpack_weights(core, y_index, shards, outs, counts):
    for source, target in weight_pairs(core, y_index, shards, outs, counts):
        target[...] = source[...]


def pack_grads(core, y_index, grads, keep, send, counts):
    total = sum(counts)
    y_count = keep.shape[0]
    per = keep.shape[1] // total
    for target, parity in ((keep, core), (send, 1 - core)):
        for step in range(y_count):
            y = lax.rem(y_index + step, y_count)
            for x in range(per):
                at = x * total
                for grad, count in zip(grads, counts):
                    start = pl.multiple_of(((y * per + x) * 2 + parity) * count, 32)
                    target[step, pl.ds(at, count), :] = grad[pl.ds(start, count), :].astype(BF)
                    at += count


def prepare(halo, turned, *refs):
    weights, (up, down, packed), held, sems = refs[:4], refs[4:7], refs[7:-1], refs[-1]
    pairs = list(zip(weights, held))
    for j in range(HB):
        part = pl.ds(j * BLK, BLK)
        pairs.append((turned.at[:, block_at(halo[0, 0, j])], up.at[:, part]))
        pairs.append((turned.at[:, block_at(halo[0, 1, j])], down.at[:, part]))
    wait_all(copies(pairs, sems))
    parts = [ref[...].astype(F32) for ref in held]
    used = sum(part.shape[0] for part in parts)
    parts.append(jnp.zeros((packed.shape[0] - used, L), F32))
    packed[...] = jnp.concatenate(parts, axis=0).astype(BF)


def fill_message(lower, turned, upper, cot, out, table, held, in_sems, sems):
    rows, halo_rows = turned.shape[1], lower.shape[1]
    loads = copies([(turned, table.at[:, pl.ds(halo_rows, rows)]), (cot, held)], in_sems)
    table[:, pl.ds(0, halo_rows)] = lower[...]
    table[:, pl.ds(halo_rows + rows, halo_rows)] = upper[...]
    wait_all(loads)
    pairs = []
    for l in range(out.shape[0]):
        pairs.append((table, out.at[l, :, pl.ds(0, table.shape[1])]))
        part = out.at[l, :, pl.ds(table.shape[1], BLK)]
        pairs.append((held.at[:, pl.ds(l * BLK, BLK)], part))
    wait_all(copies(pairs, sems))


def assemble(pieces, scal, *refs):
    blocks, (edge_part, node_part, held, edge_rows, node_rows) = refs[:4], refs[4:]
    z_index, x_index = scal[0], scal[1]
    for k, block in enumerate(blocks):
        held[k] = block[...]
    outs = (edge_rows, edge_rows, node_rows, node_rows)
    bases = []
    for number, count in enumerate(pieces):
        bases.append(0 if number % 2 == 0 else bases[-1] + 8 * pieces[number - 1])
    sizes = (8 * (pieces[0] + pieces[1]), 8 * (pieces[2] + pieces[3]))
    for x in range(4):
        x_step = lax.rem(x_index - x + 4, 4)
        for z in range(4):
            z_step = lax.rem(z_index - z + 4, 4)
            shard = held[z_step, pl.ds(pl.multiple_of(x_step * 32, 32), 32), :].astype(F32)
            row, lat = 0, (x % 2) * 4 + z
            for number, count in enumerate(pieces):
                base = (x // 2) * sizes[number // 2] + bases[number] + lat * count
                outs[number][pl.ds(base, count), :] = shard[row : row + count]
                row += count
    edge_part[...] = edge_rows[...].astype(BF)
    node_part[...] = node_rows[...].astype(BF)


def sum_far(pieces, scal, edge_own, e1, e2, e3, node_own, n1, n2, n3, keep, s1, s2, s3, er, nr, sent):
    z_index = scal[0]
    er[...] = sum((ref[...].astype(F32) for ref in (e1, e2, e3)), edge_own[...].astype(F32))
    nr[...] = sum((ref[...].astype(F32) for ref in (n1, n2, n3)), node_own[...].astype(F32))
    ins = (er, er, nr, nr)
    bases = []
    for number, count in enumerate(pieces):
        bases.append(0 if number % 2 == 0 else bases[-1] + 8 * pieces[number - 1])
    sizes = (8 * (pieces[0] + pieces[1]), 8 * (pieces[2] + pieces[3]))
    spare = 32 - sum(pieces)
    for x in range(4):
        for z in range(4):
            lat = (x % 2) * 4 + z
            parts = []
            for number, count in enumerate(pieces):
                base = (x // 2) * sizes[number // 2] + bases[number] + lat * count
                parts.append(ins[number][pl.ds(base, count), :])
            parts.append(jnp.zeros((spare, L), F32))
            sent[z, x] = jnp.concatenate(parts, axis=0)
    keep[...] = sent[z_index]
    for step, out in ((1, s1), (2, s2), (3, s3)):
        out[...] = sent[lax.rem(z_index + step, 4)].astype(BF)


def sum_z(scal, own, r1, r2, r3, keep, s1, s2, s3, held):
    x_index = scal[1]
    held[...] = own[...] + (r1[...].astype(F32) + r2[...].astype(F32) + r3[...].astype(F32))
    keep[...] = held[x_index]
    for step, out in ((1, s1), (2, s2), (3, s3)):
        out[...] = held[lax.rem(x_index + step, 4)].astype(BF)


def sum_x(own, r1, r2, r3, *outs):
    total = own[...] + (r1[...].astype(F32) + r2[...].astype(F32) + r3[...].astype(F32))
    row = 0
    for out in outs:
        count = out.shape[0]
        out[...] = total[row : row + count]
        row += count


def edge_forward(scal, ext, edges, offsets, *refs):
    shards, refs = refs[:8], refs[8:]
    gain, joined_out, first_out, normed_out, inverse_out, new_edges_out, partial_out = refs[:7]
    own_out, up_out, refs = refs[7], refs[8], refs[9:]
    joined, first, normed, inverse, new_edges, partial, w_in, w_out, second, sems, out_sems = refs
    tiles = edges.shape[0] // BLK
    lat_index, core, y_index, count = (scal[2 * tiles + i] for i in range(4))
    slabs = w_in.shape[0] // 3 // 32
    counts = (3 * L // slabs, L // slabs)
    stores = []

    def store(source, target):
        copy = pltpu.make_async_copy(source, target, out_sems.at[len(stores)])
        copy.start()
        stores.append(copy)

    store(ext.at[:, block_at(HB + lat_index)], own_out)
    store(ext.at[:, pl.ds(ext.shape[1] - BLK, BLK)], up_out)
    loads = copies([(edges, joined.at[:, pl.ds(0, L)])], sems)
    for t in range(tiles):
        rows = pl.ds(t * BLK, BLK)
        to_src = one_hot_columns(offsets[1, pl.ds(t, 1), :]).T.astype(BF)
        to_dst = one_hot_columns(offsets[0, pl.ds(t, 1), :]).T.astype(BF)
        src, dst = block_at(scal[tiles + t]), block_at(scal[t] + HB)
        joined[rows, pl.ds(L, L)] = dot_transpose(to_src, ext[:, src]).astype(BF)
        joined[rows, pl.ds(2 * L, L)] = dot_transpose(to_dst, ext[:, dst]).astype(BF)
    wait_all(loads)
    store(joined, joined_out)
    unpack_weights(core, y_index, shards, (w_in, w_out), counts)
    for n in range(2):
        columns = pl.ds(n * 256, 256)
        first[:, columns] = jnp.maximum(dot(joined[...], w_in[:, columns]), 0.0).astype(BF)
    store(first, first_out)
    for n in range(2):
        columns = pl.ds(n * 256, 256)
        second[:, columns] = dot(first[...], w_out[:, columns])
    partial[...] = jnp.zeros_like(partial)
    for t in range(tiles):
        rows = pl.ds(t * BLK, BLK)
        live = (lat_index * tiles + t < count).astype(F32)
        values, inv = norm_parts(second[rows, :])
        normed[rows, :] = values
        inverse[rows, :] = jnp.broadcast_to(inv, (BLK, BLK))
        message = values * gain[...] * live
        new_edges[rows, :] = (joined[rows, pl.ds(0, L)].astype(F32) + message).astype(BF)
        second[rows, :] = message
    store(normed, normed_out)
    store(inverse, inverse_out)
    store(new_edges, new_edges_out)
    for t in range(tiles):
        rows = pl.ds(t * BLK, BLK)
        into = one_hot_columns(offsets[0, pl.ds(t, 1), :]).astype(BF)
        high, middle, low = split_three(second[rows, :])
        block = scal[t]
        partial[block] = partial[block] + (dot(into, low) + dot(into, middle) + dot(into, high))
    store(partial, partial_out)
    wait_all(stores)


def node_step(scal, spread, own_hbm, up_hbm, *refs):
    shards, refs = refs[:8], refs[8:]
    gain, out, rows_out, direct_out, joined_out, first_out, d_second_out, d_first_out = refs[:8]
    own_turned, up_turned, w_in, w_out, joined, first, d_second, d_first = refs[8:16]
    d_direct, new_rows, sems, out_sems = refs[16:]
    core, y_index = scal[1], scal[2]
    slabs = w_in.shape[0] // 2 // 32
    counts = (2 * L // slabs, L // slabs)
    pairs = weight_pairs(core, y_index, shards, (w_in, w_out), counts)
    loads = copies([(own_hbm, own_turned), (up_hbm, up_turned)] + pairs[-4:], sems)
    for source, target in pairs[:-4]:
        target[...] = source[...]
    wait_all(loads)
    own = own_turned[...].astype(F32).T
    upstream = up_turned[...].astype(F32).T
    joined[:, pl.ds(0, L)] = own.astype(BF)
    total = spread[0]
    for l in range(1, spread.shape[0]):
        total = total + spread[l]
    joined[:, pl.ds(L, L)] = total.astype(BF)
    first[...] = jnp.maximum(dot(joined[...], w_in[...]), 0.0).astype(BF)
    normed, inverse = norm_parts(dot(first[...], w_out[...]))
    d_second[...] = norm_back(upstream, normed, inverse, gain[...]).astype(BF)
    back = dot_transpose(d_second[...], w_out[...])
    d_first[...] = jnp.where(first[...].astype(F32) > 0, back, 0.0).astype(BF)
    d_agg = dot_transpose(w_in[pl.ds(L, L), :], d_first[...]).astype(BF)
    for l in range(out.shape[0]):
        out[l] = d_agg
    new_rows[...] = (own + normed * gain[...]).T.astype(BF)
    d_direct[...] = dot_transpose(w_in[pl.ds(0, L), :], d_first[...])
    held = (new_rows, d_direct, joined, first, d_second, d_first)
    outs = (rows_out, direct_out, joined_out, first_out, d_second_out, d_first_out)
    wait_all(copies(zip(held, outs), out_sems))


def node_grads(scal, *refs):
    saved, (keep, send), refs = refs[:4], refs[4:6], refs[6:]
    held, (g_in, g_out, sems) = refs[:4], refs[4:]
    wait_all(copies(zip(saved, held), sems))
    joined, first, d_second, d_first = held
    g_out[...] = dot_rows(first[...], d_second[...])
    g_in[...] = dot_rows(joined[...], d_first[...])
    slabs = g_in.shape[0] // 2 // 32
    pack_grads(scal[1], scal[2], (g_in, g_out), keep, send, (2 * L // slabs, L // slabs))


def edge_backward(scal, d_agg, cot, offsets, gain, *refs):
    saved, w_out_shards, refs = refs[:4], refs[4:12], refs[12:]
    d_first, d_first_out, keep, send = refs[:4]
    joined, first, normed, inverse, w_in, w_out, d_second, g_in, g_out, sems, out_sems = refs[4:]
    tiles = cot.shape[0] // BLK
    lat_index, core, y_index, count = (scal[2 * tiles + i] for i in range(4))
    slabs = w_in.shape[0] // 3 // 32
    counts = (3 * L // slabs, L // slabs)
    normed_in, inverse_in, first_in, joined_in = saved
    pairs = [(normed_in, normed), (inverse_in, inverse)]
    pairs += weight_pairs(core, y_index, w_out_shards, (w_in, w_out), counts)[1::2]
    pairs += [(first_in, first), (joined_in, joined)]
    loads = copies(pairs, sems)
    wait_all(loads[:2])
    for t in range(tiles):
        rows = pl.ds(t * BLK, BLK)
        live = (lat_index * tiles + t < count).astype(F32)
        to_dst = one_hot_columns(offsets[0, pl.ds(t, 1), :]).T.astype(BF)
        picked = dot_transpose(to_dst, d_agg[scal[t]])
        d_message = (cot[rows, :].astype(F32) + picked) * live
        back = norm_back(d_message, normed[rows, :], inverse[rows, pl.ds(0, 1)], gain[...])
        d_second[rows, :] = back.astype(BF)
    wait_all(loads[2:])
    for n in range(2):
        part = pl.ds(n * 256, 256)
        back = dot_transpose(d_second[...], w_out[part, :])
        d_first[:, part] = jnp.where(first[:, part].astype(F32) > 0, back, 0.0).astype(BF)
    store = copies([(d_first, d_first_out)], out_sems)
    for n in range(2):
        part = pl.ds(n * 256, 256)
        g_out[part, :] = dot_rows(first[:, part], d_second[...])
    for n in range(6):
        part = pl.ds(n * 256, 256)
        g_in[part, :] = dot_rows(joined[:, part], d_first[...])
    pack_grads(core, y_index, (g_in, g_out), keep, send, counts)
    wait_all(store)


def edge_inputs(scal, d_first, offsets, direct_in, *refs):
    shards, refs = refs[:8], refs[8:]
    middle_out, lower, upper, d_direct, w_in, w_out, d_ext, d_turned, sems = refs
    tiles = d_first.shape[0] // BLK
    lat_index, core, y_index = (scal[2 * tiles + i] for i in range(3))
    slabs = w_in.shape[0] // 3 // 32
    counts = (3 * L // slabs, L // slabs)
    pairs = weight_pairs(core, y_index, shards, (w_in, w_out), counts)[::2]
    pairs += [(direct_in, d_direct)]
    loads = copies(pairs, sems)
    d_ext[...] = jnp.zeros_like(d_ext)
    wait_all(loads)
    for n in range(4):
        d_turned[pl.ds(n * 256, 256), :] = dot_transpose(
            w_in[pl.ds(L + n * 256, 256), :], d_first[...]
        )
    for t in range(tiles):
        rows = pl.ds(t * BLK, BLK)
        for row, place, at in ((1, scal[tiles + t], 0), (0, scal[t] + HB, L)):
            into = one_hot_columns(offsets[row, pl.ds(t, 1), :]).T.astype(BF)
            value = d_turned[pl.ds(at, L), rows]
            high = value.astype(BF)
            low = (value - high.astype(F32)).astype(BF)
            d_ext[place] = d_ext[place] + (dot(low, into) + dot(high, into))
    d_ext[HB + lat_index] = d_ext[HB + lat_index] + d_direct[...]
    blocks = middle_out.shape[0]
    for j in range(HB):
        lower[:, pl.ds(j * BLK, BLK)] = d_ext[j].astype(BF)
        upper[:, pl.ds(j * BLK, BLK)] = d_ext[HB + blocks + j].astype(BF)
    middle_out[...] = d_ext[pl.ds(HB, blocks)]


def edge_grads(scal, d_first_in, cot_in, *refs):
    shards, refs = refs[:8], refs[8:]
    grad_out, grad_edges, cot, d_first, w_in, w_out, sems, out_sems = refs
    tiles = cot.shape[0] // BLK
    core, y_index = scal[2 * tiles + 1], scal[2 * tiles + 2]
    slabs = w_in.shape[0] // 3 // 32
    counts = (3 * L // slabs, L // slabs)
    pairs = weight_pairs(core, y_index, shards, (w_in, w_out), counts)[::2]
    wait_all(copies(pairs + [(cot_in, cot), (d_first_in, d_first)], sems))
    for n in range(2):
        part = pl.ds(n * 256, 256)
        back = dot_transpose(d_first[...], w_in[part, :])
        grad_edges[:, part] = (cot[:, part].astype(F32) + back).astype(BF)
    wait_all(copies([(grad_edges, grad_out)], out_sems))


def add_halo(halo, middle, above, below, new_rows, columns, held):
    held[...] = middle[...]
    for j in range(HB):
        for place, value in ((halo[0, 0, j], above), (halo[0, 1, j], below)):
            held[place] = held[place] + value[:, pl.ds(j * BLK, BLK)].astype(F32)
    width = columns.shape[1]
    for block in range(held.shape[0]):
        for l in range(columns.shape[0]):
            columns[l, :, pl.ds(block * BLK, BLK)] = held[
                block, pl.ds(l * width, width), :
            ].astype(BF)
    last = pl.ds(held.shape[0] * BLK, BLK)
    for l in range(columns.shape[0]):
        columns[l, :, last] = new_rows[pl.ds(l * width, width), :]


def finish(arrived, out, new_nodes):
    cells = pl.ds(0, out.shape[1])
    total = arrived[0, :, cells].astype(F32)
    for l in range(1, arrived.shape[0]):
        total = total + arrived[l, :, cells].astype(F32)
    out[...] = total.astype(BF)
    for l in range(arrived.shape[0]):
        new_nodes[:, pl.ds(l * BLK, BLK)] = arrived[l, :, pl.ds(out.shape[1], BLK)]


def call(kernel, out_shape, scratch, mib, spaces, operands, flops=0, out_spaces="", sems=()):
    moved = sum(x.size * x.dtype.itemsize for x in operands)
    moved += sum(x.size * x.dtype.itemsize for x in out_shape)
    named = {"s": pltpu.SMEM, "v": pltpu.VMEM, "h": pltpu.HBM}
    out_spaces = out_spaces or "v" * len(out_shape)
    operands = [
        pltpu.with_memory_space_constraint(x, pltpu.HBM) if space == "h" else x
        for x, space in zip(operands, spaces)
    ]
    placed = [
        pltpu.HBM(x.shape, x.dtype) if space == "h" else x
        for x, space in zip(out_shape, out_spaces)
    ]
    return pl.pallas_call(
        kernel,
        out_shape=placed,
        in_specs=[pl.BlockSpec(memory_space=named[space]) for space in spaces],
        out_specs=[pl.BlockSpec(memory_space=named[space]) for space in out_spaces],
        scratch_shapes=[pltpu.VMEM(shape, dtype) for shape, dtype in scratch]
        + [pltpu.SemaphoreType.DMA((count,)) for count in sems],
        cost_estimate=pl.CostEstimate(flops=flops, bytes_accessed=moved, transcendentals=0),
        compiler_params=pltpu.CompilerParams(vmem_limit_bytes=mib << 20),
    )(*operands)


def run_edge_forward(scal, ext, edges, offsets, shards, gain, lat_size):
    rows = edges.shape[0]
    outs = [
        shape_of((rows, 3 * L), BF),
        shape_of((rows, L), BF),
        shape_of((rows, L), F32),
        shape_of((rows, BLK), F32),
        shape_of((rows, L), BF),
        shape_of((lat_size, BLK, L), F32),
    ]
    held = [(out.shape, out.dtype) for out in outs]
    outs += [shape_of((L, BLK), BF)] * 2
    return call(
        edge_forward,
        outs,
        held + [((3 * L, L), BF), ((L, L), BF), ((rows, L), F32)],
        EDGE_MIB,
        "svhv" + "v" * len(shards) + "v",
        (scal, ext, edges, offsets, *shards, gain),
        flops=2 * rows * 4 * L * L,
        out_spaces="h" * len(outs),
        sems=(1, len(outs)),
    )


def run_node_step(scal, spread, own, up, shards, gain):
    lat_size = spread.shape[0]
    rows = [((BLK, 2 * L), BF), ((BLK, L), BF), ((BLK, L), BF), ((BLK, L), BF)]
    return call(
        node_step,
        [shape_of((lat_size, L, BLK), BF), shape_of((L, BLK), BF), shape_of((L, BLK), F32)]
        + [shape_of(*row) for row in rows],
        [((L, BLK), BF), ((L, BLK), BF), ((2 * L, L), BF), ((L, L), BF)]
        + rows
        + [((L, BLK), F32), ((L, BLK), BF)],
        NODE_MIB,
        "svhh" + "v" * (len(shards) - 1) + "hv",
        (scal, spread, own, up, *shards, gain),
        flops=2 * BLK * 6 * L * L,
        out_spaces="vhhhhhh",
        sems=(2 + 4, 6),
    )


def run_node_grads(scal, saved, shard, y_count):
    return call(
        node_grads,
        [shape_of((y_count,) + shard.shape, BF)] * 2,
        [(one.shape, BF) for one in saved] + [((2 * L, L), F32), ((L, L), F32)],
        NODE_MIB,
        "shhhh",
        (scal, *saved),
        flops=2 * BLK * 3 * L * L,
        sems=(4,),
    )


def run_edge_backward(scal, d_agg, cot, offsets, gain, saved, shards):
    rows = cot.shape[0]
    chunk = (len(shards) // 2,) + shards[0].shape
    normed, inverse, first, joined = saved
    return call(
        edge_backward,
        [shape_of((rows, L), BF)] * 2 + [shape_of(chunk, BF)] * 2,
        [
            (joined.shape, BF),
            (first.shape, BF),
            (normed.shape, F32),
            (inverse.shape, F32),
            ((3 * L, L), BF),
            ((L, L), BF),
            ((rows, L), BF),
            ((3 * L, L), F32),
            ((L, L), F32),
        ],
        BACK_MIB,
        "svvvv" + "h" * (len(saved) + len(shards)),
        (scal, d_agg, cot, offsets, gain, *saved, *shards),
        flops=2 * rows * 5 * L * L,
        out_spaces="vhvv",
        sems=(4 + 2 * len(shards), 1),
    )


def run_edge_inputs(scal, d_first, offsets, d_direct, shards, lat_size):
    rows = d_first.shape[0]
    return call(
        edge_inputs,
        [
            shape_of((lat_size, L, BLK), F32),
            shape_of((L, HB * BLK), BF),
            shape_of((L, HB * BLK), BF),
        ],
        [
            (d_direct.shape, F32),
            ((3 * L, L), BF),
            ((L, L), BF),
            ((lat_size + 2 * HB, L, BLK), F32),
            ((2 * L, rows), F32),
        ],
        EDGE_MIB,
        "svvh" + "h" * len(shards),
        (scal, d_first, offsets, d_direct, *shards),
        flops=2 * rows * 2 * L * L,
        sems=(1 + 2 * len(shards),),
    )


def run_edge_grads(scal, d_first, cot, shards):
    rows = cot.shape[0]
    return call(
        edge_grads,
        [shape_of((rows, L), BF)],
        [((rows, L), BF)] * 3 + [((3 * L, L), BF), ((L, L), BF)],
        EDGE_MIB,
        "shh" + "h" * len(shards),
        (scal, d_first, cot, *shards),
        flops=2 * rows * L * L,
        out_spaces="h",
        sems=(2 + 2 * len(shards), 1),
    )


def swap_cores(value):
    return lax.ppermute(value, "c", [(0, 1), (1, 0)])


def shift(value, axes, step):
    count = lax.axis_size(axes)
    return lax.ppermute(value, axes, [(i, (i + step) % count) for i in range(count)])


def shifts(value, axes):
    return [value] + [shift(value, axes, k) for k in range(1, lax.axis_size(axes))]


def spread_rows(value, axes):
    return lax.all_to_all(value, axes, 0, 0)


def gather_far(value):
    mine = shifts(value, "y")
    return mine + [swap_cores(one) for one in mine]


def reduce_far(keep, arrived):
    both = [(keep[k].astype(F32) + arrived[k].astype(F32)).astype(BF) for k in range(keep.shape[0])]
    return [both[0]] + [shift(both[k], "y", k) for k in range(1, keep.shape[0])]


def per_device(
    nodes,
    edges,
    edge_tiles,
    edge_offsets,
    tile_counts,
    halo_blocks,
    w_edge_in,
    w_edge_out,
    w_node_in,
    w_node_out,
    edge_gain,
    node_gain,
    node_cotangent,
    edge_cotangent,
):
    lat_size = lax.axis_size(LAT)
    place = [lax.axis_index(LAT), lax.axis_index("c"), lax.axis_index("y")]
    slab_rows, width = nodes.shape
    own_rows = slab_rows // lat_size
    halo_rows = HB * BLK
    ext_rows = slab_rows + 2 * halo_rows
    weights = (w_edge_in, w_edge_out, w_node_in, w_node_out)
    pieces = tuple(weight.shape[0] for weight in weights)
    edge_rows = 2 * lat_size * (pieces[0] + pieces[1])
    node_rows = 2 * lat_size * (pieces[2] + pieces[3])

    near_scal = jnp.stack([lax.axis_index("z"), lax.axis_index(XS)]).astype(jnp.int32)
    node_scal = jnp.stack(place).astype(jnp.int32)
    scal = jnp.concatenate([edge_tiles.reshape(-1), node_scal, tile_counts])
    halo = halo_blocks
    offsets = edge_offsets.reshape(2, -1, BLK)
    edge_gain_row = edge_gain.reshape(1, L)
    node_gain_row = node_gain.reshape(1, L)

    turned = nodes.T
    up, down, packed = call(
        prepare,
        [
            shape_of((width, halo_rows), BF),
            shape_of((width, halo_rows), BF),
            shape_of((32, L), BF),
        ],
        [(weight.shape, BF) for weight in weights],
        4,
        "shhhhh",
        (halo, turned, *weights),
        sems=(4 + 2 * HB,),
    )
    from_lower = from_behind(up, 1)
    from_upper = from_behind(down, -1)

    (message_out,) = call(
        fill_message,
        [shape_of((lat_size, width, ext_rows + own_rows), BF)],
        [((width, ext_rows), BF), ((width, slab_rows), BF)],
        4,
        "vhvh",
        (from_lower, turned, from_upper, node_cotangent.T),
        out_spaces="h",
        sems=(2, 2 * lat_size),
    )
    by_x = jnp.concatenate(shifts(packed, XS), axis=0)
    near = shifts(by_x, "z")
    edge_part, node_part = call(
        functools.partial(assemble, pieces),
        [shape_of((edge_rows, L), BF), shape_of((node_rows, L), BF)],
        [((4, 128, L), BF), ((edge_rows, L), F32), ((node_rows, L), F32)],
        6,
        "svvvv",
        (near_scal, *near),
    )

    edge_shards = gather_far(edge_part)
    ext = spread_rows(message_out, LAT).reshape(L, ext_rows + own_rows)

    joined, first, normed, inverse, new_edges, partial, own, node_up = run_edge_forward(
        scal, ext, edges, offsets, edge_shards, edge_gain_row, lat_size
    )
    node_shards = gather_far(node_part)
    spread = spread_rows(partial, LAT)
    second_out, new_rows, d_direct, *node_saved = run_node_step(
        node_scal, spread, own, node_up, node_shards, node_gain_row
    )
    node_keep, node_send = run_node_grads(
        node_scal, node_saved, node_part, lax.axis_size("y")
    )
    second_in = spread_rows(second_out, LAT)
    node_far = reduce_far(node_keep, swap_cores(node_send))

    d_first, d_first_kept, edge_keep, edge_send = run_edge_backward(
        scal, second_in, edge_cotangent, offsets, edge_gain_row,
        (normed, inverse, first, joined), edge_shards,
    )
    middle, lower, upper = run_edge_inputs(scal, d_first, offsets, d_direct, edge_shards, lat_size)
    from_above = from_behind(lower, -1)
    from_below = from_behind(upper, 1)
    (grad_edges,) = run_edge_grads(scal, d_first_kept, edge_cotangent, edge_shards)
    edge_arrived = swap_cores(edge_send)
    edge_far = reduce_far(edge_keep, edge_arrived)
    (columns,) = call(
        add_halo,
        [shape_of((lat_size, width, slab_rows + own_rows), BF)],
        [((lat_size, L, BLK), F32)],
        8,
        "svvvv",
        (halo, middle, from_above, from_below, new_rows),
    )
    columns = spread_rows(columns, LAT)
    grad_slab, new_nodes = call(
        finish, [shape_of((width, slab_rows), BF)] * 2, [], 6, "v", (columns,)
    )

    shard = (32, L)
    shards = (4,) + shard
    kept, *sent = call(
        functools.partial(sum_far, pieces),
        [shape_of(shards, F32)] + [shape_of(shards, BF)] * 3,
        [((edge_rows, L), F32), ((node_rows, L), F32), ((4,) + shards, F32)],
        8,
        "s" + "v" * 8,
        (near_scal, *edge_far, *node_far),
    )
    moved = [shift(sent[k - 1], "z", k) for k in range(1, 4)]
    kept, *sent = call(
        sum_z,
        [shape_of(shard, F32)] + [shape_of(shard, BF)] * 3,
        [(shards, F32)],
        4,
        "s" + "v" * 4,
        (near_scal, kept, *moved),
    )
    moved = [shift(sent[k - 1], XS, k) for k in range(1, 4)]
    reduced = call(
        sum_x, [shape_of((count, L), F32) for count in pieces], [], 4, "v" * 4, (kept, *moved)
    )
    return (new_nodes.T, new_edges, grad_slab.T, grad_edges) + tuple(reduced)


def solution(mesh):
    fine = Mesh(mesh.devices.reshape(4, 2, 2, 2, 4), ("y", "xl", "c", "xh", "z"))
    every = SLAB + LAT
    by_rows = P(every, None)
    split = P(SLAB, LAT)
    placed = (
        split,
        by_rows,
        P(None, every),
        P(None, every),
        P(SLAB),
        P(SLAB, None, None),
        by_rows,
        by_rows,
        by_rows,
        by_rows,
        P(),
        P(),
        split,
        by_rows,
    )

    return jax.shard_map(
        per_device,
        mesh=fine,
        in_specs=placed,
        out_specs=(split, by_rows, split, by_rows, by_rows, by_rows, by_rows, by_rows),
        check_vma=False,
    )
```

```python
import functools

import jax
import jax.numpy as jnp
from jax import lax
from jax.experimental import pallas as pl
from jax.experimental.pallas import tpu as pltpu
from jax.sharding import Mesh, PartitionSpec as P


L = 512
BLK = 128
HB = 2
EPSILON = 1e-05

SLAB = ("y", "xl", "c")
LAT = ("xh", "z")
XS = ("xl", "xh")
BF = jnp.bfloat16
F32 = jnp.float32
EDGE_MIB = 16
NODE_MIB = 14
BACK_MIB = 28


def shape_of(shape, dtype):
    return jax.ShapeDtypeStruct(shape, dtype)


def from_behind(value, steps):
    count = lax.axis_size(SLAB)
    first, last = (max(0, -steps), min(count, count - steps))
    return lax.ppermute(value, SLAB, [(source, source + steps) for source in range(first, last)])


def dot(left, right):
    return jnp.dot(left, right, preferred_element_type=F32)


def dot_rows(left, right):
    return lax.dot_general(left, right, (((0,), (0,)), ((), ())), preferred_element_type=F32)


def dot_transpose(left, right):
    return lax.dot_general(left, right, (((1,), (1,)), ((), ())), preferred_element_type=F32)


def one_hot_columns(offsets):
    cells = lax.broadcasted_iota(jnp.int32, (BLK, BLK), 0)
    return (cells == offsets).astype(F32)


def norm_parts(values):
    average = jnp.mean(values, axis=-1, keepdims=True)
    centred = values - average
    variance = jnp.mean(centred * centred, axis=-1, keepdims=True)
    inverse = lax.rsqrt(variance + EPSILON)
    return centred * inverse, inverse


def norm_back(upstream, normed, inverse, gain_vector):
    scaled = upstream * gain_vector
    return inverse * (
        scaled
        - jnp.mean(scaled, axis=-1, keepdims=True)
        - normed * jnp.mean(scaled * normed, axis=-1, keepdims=True)
    )


def split_three(value):
    high = value.astype(BF)
    rest = value - high.astype(F32)
    middle = rest.astype(BF)
    return high, middle, (rest - middle.astype(F32)).astype(BF)


def block_at(number):
    return pl.ds(pl.multiple_of(number * BLK, BLK), BLK)


def copies(pairs, sems):
    made = [pltpu.make_async_copy(src, dst, sems.at[i]) for i, (src, dst) in enumerate(pairs)]
    for one in made:
        one.start()
    return made


def wait_all(made):
    for one in made:
        one.wait()


def weight_pairs(core, y_index, shards, outs, counts):
    total = sum(counts)
    y_count = len(shards) // 2
    pairs = []
    for number, source in enumerate(shards):
        step = number % y_count
        parity = core if number < y_count else 1 - core
        y = lax.rem(y_index - step + y_count, y_count)
        per = source.shape[0] // total
        for x in range(per):
            slab = (y * per + x) * 2 + parity
            at = x * total
            for out, count in zip(outs, counts):
                start = pl.multiple_of(slab * count, 32)
                pairs.append((source.at[pl.ds(at, count), :], out.at[pl.ds(start, count), :]))
                at += count
    return pairs


def unpack_weights(core, y_index, shards, outs, counts):
    for source, target in weight_pairs(core, y_index, shards, outs, counts):
        target[...] = source[...]


def pack_grads(core, y_index, grads, keep, send, counts):
    total = sum(counts)
    y_count = keep.shape[0]
    per = keep.shape[1] // total
    for target, parity in ((keep, core), (send, 1 - core)):
        for step in range(y_count):
            y = lax.rem(y_index + step, y_count)
            for x in range(per):
                at = x * total
                for grad, count in zip(grads, counts):
                    start = pl.multiple_of(((y * per + x) * 2 + parity) * count, 32)
                    target[step, pl.ds(at, count), :] = grad[pl.ds(start, count), :].astype(BF)
                    at += count


def prepare(halo, turned, *refs):
    weights, (up, down, packed), held, sems = refs[:4], refs[4:7], refs[7:-1], refs[-1]
    pairs = list(zip(weights, held))
    for j in range(HB):
        part = pl.ds(j * BLK, BLK)
        pairs.append((turned.at[:, block_at(halo[0, 0, j])], up.at[:, part]))
        pairs.append((turned.at[:, block_at(halo[0, 1, j])], down.at[:, part]))
    wait_all(copies(pairs, sems))
    parts = [ref[...].astype(F32) for ref in held]
    used = sum(part.shape[0] for part in parts)
    parts.append(jnp.zeros((packed.shape[0] - used, L), F32))
    packed[...] = jnp.concatenate(parts, axis=0).astype(BF)


def fill_message(lower, turned, upper, cot, out, table, held, in_sems, sems):
    rows, halo_rows = turned.shape[1], lower.shape[1]
    loads = copies([(turned, table.at[:, pl.ds(halo_rows, rows)]), (cot, held)], in_sems)
    table[:, pl.ds(0, halo_rows)] = lower[...]
    table[:, pl.ds(halo_rows + rows, halo_rows)] = upper[...]
    wait_all(loads)
    pairs = []
    for l in range(out.shape[0]):
        pairs.append((table, out.at[l, :, pl.ds(0, table.shape[1])]))
        part = out.at[l, :, pl.ds(table.shape[1], BLK)]
        pairs.append((held.at[:, pl.ds(l * BLK, BLK)], part))
    wait_all(copies(pairs, sems))


def assemble(pieces, scal, *refs):
    blocks, (edge_part, node_part, held, edge_rows, node_rows) = refs[:4], refs[4:]
    z_index, x_index = scal[0], scal[1]
    for k, block in enumerate(blocks):
        held[k] = block[...]
    outs = (edge_rows, edge_rows, node_rows, node_rows)
    bases = []
    for number, count in enumerate(pieces):
        bases.append(0 if number % 2 == 0 else bases[-1] + 8 * pieces[number - 1])
    sizes = (8 * (pieces[0] + pieces[1]), 8 * (pieces[2] + pieces[3]))
    for x in range(4):
        x_step = lax.rem(x_index - x + 4, 4)
        for z in range(4):
            z_step = lax.rem(z_index - z + 4, 4)
            shard = held[z_step, pl.ds(pl.multiple_of(x_step * 32, 32), 32), :].astype(F32)
            row, lat = 0, (x % 2) * 4 + z
            for number, count in enumerate(pieces):
                base = (x // 2) * sizes[number // 2] + bases[number] + lat * count
                outs[number][pl.ds(base, count), :] = shard[row : row + count]
                row += count
    edge_part[...] = edge_rows[...].astype(BF)
    node_part[...] = node_rows[...].astype(BF)


def sum_far(pieces, scal, edge_own, e1, e2, e3, node_own, n1, n2, n3, keep, s1, s2, s3, er, nr, sent):
    z_index = scal[0]
    er[...] = sum((ref[...].astype(F32) for ref in (e1, e2, e3)), edge_own[...].astype(F32))
    nr[...] = sum((ref[...].astype(F32) for ref in (n1, n2, n3)), node_own[...].astype(F32))
    ins = (er, er, nr, nr)
    bases = []
    for number, count in enumerate(pieces):
        bases.append(0 if number % 2 == 0 else bases[-1] + 8 * pieces[number - 1])
    sizes = (8 * (pieces[0] + pieces[1]), 8 * (pieces[2] + pieces[3]))
    spare = 32 - sum(pieces)
    for x in range(4):
        for z in range(4):
            lat = (x % 2) * 4 + z
            parts = []
            for number, count in enumerate(pieces):
                base = (x // 2) * sizes[number // 2] + bases[number] + lat * count
                parts.append(ins[number][pl.ds(base, count), :])
            parts.append(jnp.zeros((spare, L), F32))
            sent[z, x] = jnp.concatenate(parts, axis=0)
    keep[...] = sent[z_index]
    for step, out in ((1, s1), (2, s2), (3, s3)):
        out[...] = sent[lax.rem(z_index + step, 4)].astype(BF)


def sum_z(scal, own, r1, r2, r3, keep, s1, s2, s3, held):
    x_index = scal[1]
    held[...] = own[...] + (r1[...].astype(F32) + r2[...].astype(F32) + r3[...].astype(F32))
    keep[...] = held[x_index]
    for step, out in ((1, s1), (2, s2), (3, s3)):
        out[...] = held[lax.rem(x_index + step, 4)].astype(BF)


def sum_x(own, r1, r2, r3, *outs):
    total = own[...] + (r1[...].astype(F32) + r2[...].astype(F32) + r3[...].astype(F32))
    row = 0
    for out in outs:
        count = out.shape[0]
        out[...] = total[row : row + count]
        row += count


def edge_forward(scal, ext, edges, offsets, *refs):
    shards, refs = refs[:8], refs[8:]
    gain, joined_out, first_out, normed_out, inverse_out, new_edges_out, partial_out = refs[:7]
    own_out, up_out, refs = refs[7], refs[8], refs[9:]
    joined, first, normed, inverse, new_edges, partial, w_in, w_out, second, sems, out_sems = refs
    tiles = edges.shape[0] // BLK
    lat_index, core, y_index, count = (scal[2 * tiles + i] for i in range(4))
    slabs = w_in.shape[0] // 3 // 32
    counts = (3 * L // slabs, L // slabs)
    stores = []

    def store(source, target):
        copy = pltpu.make_async_copy(source, target, out_sems.at[len(stores)])
        copy.start()
        stores.append(copy)

    store(ext.at[:, block_at(HB + lat_index)], own_out)
    store(ext.at[:, pl.ds(ext.shape[1] - BLK, BLK)], up_out)
    loads = copies([(edges, joined.at[:, pl.ds(0, L)])], sems)
    for t in range(tiles):
        rows = pl.ds(t * BLK, BLK)
        to_src = one_hot_columns(offsets[1, pl.ds(t, 1), :]).T.astype(BF)
        to_dst = one_hot_columns(offsets[0, pl.ds(t, 1), :]).T.astype(BF)
        src, dst = block_at(scal[tiles + t]), block_at(scal[t] + HB)
        joined[rows, pl.ds(L, L)] = dot_transpose(to_src, ext[:, src]).astype(BF)
        joined[rows, pl.ds(2 * L, L)] = dot_transpose(to_dst, ext[:, dst]).astype(BF)
    wait_all(loads)
    store(joined, joined_out)
    unpack_weights(core, y_index, shards, (w_in, w_out), counts)
    for n in range(2):
        columns = pl.ds(n * 256, 256)
        first[:, columns] = jnp.maximum(dot(joined[...], w_in[:, columns]), 0.0).astype(BF)
    store(first, first_out)
    for n in range(2):
        columns = pl.ds(n * 256, 256)
        second[:, columns] = dot(first[...], w_out[:, columns])
    partial[...] = jnp.zeros_like(partial)
    for t in range(tiles):
        rows = pl.ds(t * BLK, BLK)
        live = (lat_index * tiles + t < count).astype(F32)
        values, inv = norm_parts(second[rows, :])
        normed[rows, :] = values
        inverse[rows, :] = jnp.broadcast_to(inv, (BLK, BLK))
        message = values * gain[...] * live
        new_edges[rows, :] = (joined[rows, pl.ds(0, L)].astype(F32) + message).astype(BF)
        second[rows, :] = message
    store(normed, normed_out)
    store(inverse, inverse_out)
    store(new_edges, new_edges_out)
    for t in range(tiles):
        rows = pl.ds(t * BLK, BLK)
        into = one_hot_columns(offsets[0, pl.ds(t, 1), :]).astype(BF)
        high, middle, low = split_three(second[rows, :])
        block = scal[t]
        partial[block] = partial[block] + (dot(into, low) + dot(into, middle) + dot(into, high))
    store(partial, partial_out)
    wait_all(stores)


def node_step(scal, spread, own_hbm, up_hbm, *refs):
    shards, refs = refs[:8], refs[8:]
    gain, out, rows_out, direct_out, joined_out, first_out, d_second_out, d_first_out = refs[:8]
    own_turned, up_turned, w_in, w_out, joined, first, d_second, d_first = refs[8:16]
    d_direct, new_rows, sems, out_sems = refs[16:]
    core, y_index = scal[1], scal[2]
    slabs = w_in.shape[0] // 2 // 32
    counts = (2 * L // slabs, L // slabs)
    pairs = weight_pairs(core, y_index, shards, (w_in, w_out), counts)
    loads = copies([(own_hbm, own_turned), (up_hbm, up_turned)] + pairs[-4:], sems)
    for source, target in pairs[:-4]:
        target[...] = source[...]
    wait_all(loads)
    own = own_turned[...].astype(F32).T
    upstream = up_turned[...].astype(F32).T
    joined[:, pl.ds(0, L)] = own.astype(BF)
    total = spread[0]
    for l in range(1, spread.shape[0]):
        total = total + spread[l]
    joined[:, pl.ds(L, L)] = total.astype(BF)
    first[...] = jnp.maximum(dot(joined[...], w_in[...]), 0.0).astype(BF)
    normed, inverse = norm_parts(dot(first[...], w_out[...]))
    d_second[...] = norm_back(upstream, normed, inverse, gain[...]).astype(BF)
    back = dot_transpose(d_second[...], w_out[...])
    d_first[...] = jnp.where(first[...].astype(F32) > 0, back, 0.0).astype(BF)
    d_agg = dot_transpose(w_in[pl.ds(L, L), :], d_first[...]).astype(BF)
    for l in range(out.shape[0]):
        out[l] = d_agg
    new_rows[...] = (own + normed * gain[...]).T.astype(BF)
    d_direct[...] = dot_transpose(w_in[pl.ds(0, L), :], d_first[...])
    held = (new_rows, d_direct, joined, first, d_second, d_first)
    outs = (rows_out, direct_out, joined_out, first_out, d_second_out, d_first_out)
    wait_all(copies(zip(held, outs), out_sems))


def node_grads(scal, *refs):
    saved, (keep, send), refs = refs[:4], refs[4:6], refs[6:]
    held, (g_in, g_out, sems) = refs[:4], refs[4:]
    wait_all(copies(zip(saved, held), sems))
    joined, first, d_second, d_first = held
    g_out[...] = dot_rows(first[...], d_second[...])
    g_in[...] = dot_rows(joined[...], d_first[...])
    slabs = g_in.shape[0] // 2 // 32
    pack_grads(scal[1], scal[2], (g_in, g_out), keep, send, (2 * L // slabs, L // slabs))


def edge_backward(scal, d_agg, cot, offsets, gain, *refs):
    saved, w_out_shards, refs = refs[:4], refs[4:12], refs[12:]
    d_first, d_first_out, keep, send = refs[:4]
    joined, first, normed, inverse, w_in, w_out, d_second, g_in, g_out, sems, out_sems = refs[4:]
    tiles = cot.shape[0] // BLK
    lat_index, core, y_index, count = (scal[2 * tiles + i] for i in range(4))
    slabs = w_in.shape[0] // 3 // 32
    counts = (3 * L // slabs, L // slabs)
    normed_in, inverse_in, first_in, joined_in = saved
    pairs = [(normed_in, normed), (inverse_in, inverse)]
    pairs += weight_pairs(core, y_index, w_out_shards, (w_in, w_out), counts)[1::2]
    pairs += [(first_in, first), (joined_in, joined)]
    loads = copies(pairs, sems)
    wait_all(loads[:2])
    for t in range(tiles):
        rows = pl.ds(t * BLK, BLK)
        live = (lat_index * tiles + t < count).astype(F32)
        to_dst = one_hot_columns(offsets[0, pl.ds(t, 1), :]).T.astype(BF)
        picked = dot_transpose(to_dst, d_agg[scal[t]])
        d_message = (cot[rows, :].astype(F32) + picked) * live
        back = norm_back(d_message, normed[rows, :], inverse[rows, pl.ds(0, 1)], gain[...])
        d_second[rows, :] = back.astype(BF)
    wait_all(loads[2:])
    for n in range(2):
        part = pl.ds(n * 256, 256)
        back = dot_transpose(d_second[...], w_out[part, :])
        d_first[:, part] = jnp.where(first[:, part].astype(F32) > 0, back, 0.0).astype(BF)
    store = copies([(d_first, d_first_out)], out_sems)
    for n in range(2):
        part = pl.ds(n * 256, 256)
        g_out[part, :] = dot_rows(first[:, part], d_second[...])
    for n in range(6):
        part = pl.ds(n * 256, 256)
        g_in[part, :] = dot_rows(joined[:, part], d_first[...])
    pack_grads(core, y_index, (g_in, g_out), keep, send, counts)
    wait_all(store)


def edge_inputs(scal, d_first, offsets, direct_in, *refs):
    shards, refs = refs[:8], refs[8:]
    middle_out, lower, upper, d_direct, w_in, w_out, d_ext, d_turned, sems = refs
    tiles = d_first.shape[0] // BLK
    lat_index, core, y_index = (scal[2 * tiles + i] for i in range(3))
    slabs = w_in.shape[0] // 3 // 32
    counts = (3 * L // slabs, L // slabs)
    pairs = weight_pairs(core, y_index, shards, (w_in, w_out), counts)[::2]
    pairs += [(direct_in, d_direct)]
    loads = copies(pairs, sems)
    d_ext[...] = jnp.zeros_like(d_ext)
    wait_all(loads)
    for n in range(4):
        d_turned[pl.ds(n * 256, 256), :] = dot_transpose(
            w_in[pl.ds(L + n * 256, 256), :], d_first[...]
        )
    for t in range(tiles):
        rows = pl.ds(t * BLK, BLK)
        for row, place, at in ((1, scal[tiles + t], 0), (0, scal[t] + HB, L)):
            into = one_hot_columns(offsets[row, pl.ds(t, 1), :]).T.astype(BF)
            value = d_turned[pl.ds(at, L), rows]
            high = value.astype(BF)
            low = (value - high.astype(F32)).astype(BF)
            d_ext[place] = d_ext[place] + (dot(low, into) + dot(high, into))
    d_ext[HB + lat_index] = d_ext[HB + lat_index] + d_direct[...]
    blocks = middle_out.shape[0]
    for j in range(HB):
        lower[:, pl.ds(j * BLK, BLK)] = d_ext[j].astype(BF)
        upper[:, pl.ds(j * BLK, BLK)] = d_ext[HB + blocks + j].astype(BF)
    middle_out[...] = d_ext[pl.ds(HB, blocks)]


def edge_grads(scal, d_first_in, cot_in, *refs):
    shards, refs = refs[:8], refs[8:]
    grad_out, grad_edges, cot, d_first, w_in, w_out, sems, out_sems = refs
    tiles = cot.shape[0] // BLK
    core, y_index = scal[2 * tiles + 1], scal[2 * tiles + 2]
    slabs = w_in.shape[0] // 3 // 32
    counts = (3 * L // slabs, L // slabs)
    pairs = weight_pairs(core, y_index, shards, (w_in, w_out), counts)[::2]
    wait_all(copies(pairs + [(cot_in, cot), (d_first_in, d_first)], sems))
    for n in range(2):
        part = pl.ds(n * 256, 256)
        back = dot_transpose(d_first[...], w_in[part, :])
        grad_edges[:, part] = (cot[:, part].astype(F32) + back).astype(BF)
    wait_all(copies([(grad_edges, grad_out)], out_sems))


def add_halo(halo, middle, above, below, new_rows, columns, held):
    held[...] = middle[...]
    for j in range(HB):
        for place, value in ((halo[0, 0, j], above), (halo[0, 1, j], below)):
            held[place] = held[place] + value[:, pl.ds(j * BLK, BLK)].astype(F32)
    width = columns.shape[1]
    for block in range(held.shape[0]):
        for l in range(columns.shape[0]):
            columns[l, :, pl.ds(block * BLK, BLK)] = held[
                block, pl.ds(l * width, width), :
            ].astype(BF)
    last = pl.ds(held.shape[0] * BLK, BLK)
    for l in range(columns.shape[0]):
        columns[l, :, last] = new_rows[pl.ds(l * width, width), :]


def finish(arrived, out, new_nodes):
    cells = pl.ds(0, out.shape[1])
    total = arrived[0, :, cells].astype(F32)
    for l in range(1, arrived.shape[0]):
        total = total + arrived[l, :, cells].astype(F32)
    out[...] = total.astype(BF)
    for l in range(arrived.shape[0]):
        new_nodes[:, pl.ds(l * BLK, BLK)] = arrived[l, :, pl.ds(out.shape[1], BLK)]


def call(kernel, out_shape, scratch, mib, spaces, operands, flops=0, out_spaces="", sems=()):
    moved = sum(x.size * x.dtype.itemsize for x in operands)
    moved += sum(x.size * x.dtype.itemsize for x in out_shape)
    named = {"s": pltpu.SMEM, "v": pltpu.VMEM, "h": pltpu.HBM}
    out_spaces = out_spaces or "v" * len(out_shape)
    operands = [
        pltpu.with_memory_space_constraint(x, pltpu.HBM) if space == "h" else x
        for x, space in zip(operands, spaces)
    ]
    placed = [
        pltpu.HBM(x.shape, x.dtype) if space == "h" else x
        for x, space in zip(out_shape, out_spaces)
    ]
    return pl.pallas_call(
        kernel,
        out_shape=placed,
        in_specs=[pl.BlockSpec(memory_space=named[space]) for space in spaces],
        out_specs=[pl.BlockSpec(memory_space=named[space]) for space in out_spaces],
        scratch_shapes=[pltpu.VMEM(shape, dtype) for shape, dtype in scratch]
        + [pltpu.SemaphoreType.DMA((count,)) for count in sems],
        cost_estimate=pl.CostEstimate(flops=flops, bytes_accessed=moved, transcendentals=0),
        compiler_params=pltpu.CompilerParams(vmem_limit_bytes=mib << 20),
    )(*operands)


def run_edge_forward(scal, ext, edges, offsets, shards, gain, lat_size):
    rows = edges.shape[0]
    outs = [
        shape_of((rows, 3 * L), BF),
        shape_of((rows, L), BF),
        shape_of((rows, L), F32),
        shape_of((rows, BLK), F32),
        shape_of((rows, L), BF),
        shape_of((lat_size, BLK, L), F32),
    ]
    held = [(out.shape, out.dtype) for out in outs]
    outs += [shape_of((L, BLK), BF)] * 2
    return call(
        edge_forward,
        outs,
        held + [((3 * L, L), BF), ((L, L), BF), ((rows, L), F32)],
        EDGE_MIB,
        "svhv" + "v" * len(shards) + "v",
        (scal, ext, edges, offsets, *shards, gain),
        flops=2 * rows * 4 * L * L,
        out_spaces="h" * len(outs),
        sems=(1, len(outs)),
    )


def run_node_step(scal, spread, own, up, shards, gain):
    lat_size = spread.shape[0]
    rows = [((BLK, 2 * L), BF), ((BLK, L), BF), ((BLK, L), BF), ((BLK, L), BF)]
    return call(
        node_step,
        [shape_of((lat_size, L, BLK), BF), shape_of((L, BLK), BF), shape_of((L, BLK), F32)]
        + [shape_of(*row) for row in rows],
        [((L, BLK), BF), ((L, BLK), BF), ((2 * L, L), BF), ((L, L), BF)]
        + rows
        + [((L, BLK), F32), ((L, BLK), BF)],
        NODE_MIB,
        "svhh" + "v" * (len(shards) - 1) + "hv",
        (scal, spread, own, up, *shards, gain),
        flops=2 * BLK * 6 * L * L,
        out_spaces="vhhhhhh",
        sems=(2 + 4, 6),
    )


def run_node_grads(scal, saved, shard, y_count):
    return call(
        node_grads,
        [shape_of((y_count,) + shard.shape, BF)] * 2,
        [(one.shape, BF) for one in saved] + [((2 * L, L), F32), ((L, L), F32)],
        NODE_MIB,
        "shhhh",
        (scal, *saved),
        flops=2 * BLK * 3 * L * L,
        sems=(4,),
    )


def run_edge_backward(scal, d_agg, cot, offsets, gain, saved, shards):
    rows = cot.shape[0]
    chunk = (len(shards) // 2,) + shards[0].shape
    normed, inverse, first, joined = saved
    return call(
        edge_backward,
        [shape_of((rows, L), BF)] * 2 + [shape_of(chunk, BF)] * 2,
        [
            (joined.shape, BF),
            (first.shape, BF),
            (normed.shape, F32),
            (inverse.shape, F32),
            ((3 * L, L), BF),
            ((L, L), BF),
            ((rows, L), BF),
            ((3 * L, L), F32),
            ((L, L), F32),
        ],
        BACK_MIB,
        "svvvv" + "h" * (len(saved) + len(shards)),
        (scal, d_agg, cot, offsets, gain, *saved, *shards),
        flops=2 * rows * 5 * L * L,
        out_spaces="vhvv",
        sems=(4 + 2 * len(shards), 1),
    )


def run_edge_inputs(scal, d_first, offsets, d_direct, shards, lat_size):
    rows = d_first.shape[0]
    return call(
        edge_inputs,
        [
            shape_of((lat_size, L, BLK), F32),
            shape_of((L, HB * BLK), BF),
            shape_of((L, HB * BLK), BF),
        ],
        [
            (d_direct.shape, F32),
            ((3 * L, L), BF),
            ((L, L), BF),
            ((lat_size + 2 * HB, L, BLK), F32),
            ((2 * L, rows), F32),
        ],
        EDGE_MIB,
        "svvh" + "h" * len(shards),
        (scal, d_first, offsets, d_direct, *shards),
        flops=2 * rows * 2 * L * L,
        sems=(1 + 2 * len(shards),),
    )


def run_edge_grads(scal, d_first, cot, shards):
    rows = cot.shape[0]
    return call(
        edge_grads,
        [shape_of((rows, L), BF)],
        [((rows, L), BF)] * 3 + [((3 * L, L), BF), ((L, L), BF)],
        EDGE_MIB,
        "shh" + "h" * len(shards),
        (scal, d_first, cot, *shards),
        flops=2 * rows * L * L,
        out_spaces="h",
        sems=(2 + 2 * len(shards), 1),
    )


def swap_cores(value):
    return lax.ppermute(value, "c", [(0, 1), (1, 0)])


def shift(value, axes, step):
    count = lax.axis_size(axes)
    return lax.ppermute(value, axes, [(i, (i + step) % count) for i in range(count)])


def shifts(value, axes):
    return [value] + [shift(value, axes, k) for k in range(1, lax.axis_size(axes))]


def spread_rows(value, axes):
    return lax.all_to_all(value, axes, 0, 0)


def gather_far(value):
    mine = shifts(value, "y")
    return mine + [swap_cores(one) for one in mine]


def reduce_far(keep, send):
    arrived = swap_cores(send)
    both = [(keep[k].astype(F32) + arrived[k].astype(F32)).astype(BF) for k in range(keep.shape[0])]
    return [both[0]] + [shift(both[k], "y", k) for k in range(1, keep.shape[0])]


def per_device(
    nodes,
    edges,
    edge_tiles,
    edge_offsets,
    tile_counts,
    halo_blocks,
    w_edge_in,
    w_edge_out,
    w_node_in,
    w_node_out,
    edge_gain,
    node_gain,
    node_cotangent,
    edge_cotangent,
):
    lat_size = lax.axis_size(LAT)
    place = [lax.axis_index(LAT), lax.axis_index("c"), lax.axis_index("y")]
    slab_rows, width = nodes.shape
    own_rows = slab_rows // lat_size
    halo_rows = HB * BLK
    ext_rows = slab_rows + 2 * halo_rows
    weights = (w_edge_in, w_edge_out, w_node_in, w_node_out)
    pieces = tuple(weight.shape[0] for weight in weights)
    edge_rows = 2 * lat_size * (pieces[0] + pieces[1])
    node_rows = 2 * lat_size * (pieces[2] + pieces[3])

    near_scal = jnp.stack([lax.axis_index("z"), lax.axis_index(XS)]).astype(jnp.int32)
    node_scal = jnp.stack(place).astype(jnp.int32)
    scal = jnp.concatenate([edge_tiles.reshape(-1), node_scal, tile_counts])
    halo = halo_blocks
    offsets = edge_offsets.reshape(2, -1, BLK)
    edge_gain_row = edge_gain.reshape(1, L)
    node_gain_row = node_gain.reshape(1, L)

    turned = nodes.T
    up, down, packed = call(
        prepare,
        [
            shape_of((width, halo_rows), BF),
            shape_of((width, halo_rows), BF),
            shape_of((32, L), BF),
        ],
        [(weight.shape, BF) for weight in weights],
        4,
        "shhhhh",
        (halo, turned, *weights),
        sems=(4 + 2 * HB,),
    )
    from_lower = from_behind(up, 1)
    from_upper = from_behind(down, -1)

    (message_out,) = call(
        fill_message,
        [shape_of((lat_size, width, ext_rows + own_rows), BF)],
        [((width, ext_rows), BF), ((width, slab_rows), BF)],
        4,
        "vhvh",
        (from_lower, turned, from_upper, node_cotangent.T),
        out_spaces="h",
        sems=(2, 2 * lat_size),
    )
    by_x = jnp.concatenate(shifts(packed, XS), axis=0)
    near = shifts(by_x, "z")
    edge_part, node_part = call(
        functools.partial(assemble, pieces),
        [shape_of((edge_rows, L), BF), shape_of((node_rows, L), BF)],
        [((4, 128, L), BF), ((edge_rows, L), F32), ((node_rows, L), F32)],
        6,
        "svvvv",
        (near_scal, *near),
    )

    edge_shards = gather_far(edge_part)
    ext = spread_rows(message_out, LAT).reshape(L, ext_rows + own_rows)

    joined, first, normed, inverse, new_edges, partial, own, node_up = run_edge_forward(
        scal, ext, edges, offsets, edge_shards, edge_gain_row, lat_size
    )
    node_shards = gather_far(node_part)
    spread = spread_rows(partial, LAT)
    second_out, new_rows, d_direct, *node_saved = run_node_step(
        node_scal, spread, own, node_up, node_shards, node_gain_row
    )
    node_keep, node_send = run_node_grads(
        node_scal, node_saved, node_part, lax.axis_size("y")
    )
    second_in = spread_rows(second_out, LAT)
    node_far = reduce_far(node_keep, node_send)

    d_first, d_first_kept, edge_keep, edge_send = run_edge_backward(
        scal, second_in, edge_cotangent, offsets, edge_gain_row,
        (normed, inverse, first, joined), edge_shards,
    )
    middle, lower, upper = run_edge_inputs(
        scal, d_first, offsets, d_direct, edge_shards, lat_size
    )
    from_above = from_behind(lower, -1)
    from_below = from_behind(upper, 1)
    (grad_edges,) = run_edge_grads(scal, d_first_kept, edge_cotangent, edge_shards)
    edge_far = reduce_far(edge_keep, edge_send)
    (columns,) = call(
        add_halo,
        [shape_of((lat_size, width, slab_rows + own_rows), BF)],
        [((lat_size, L, BLK), F32)],
        8,
        "svvvv",
        (halo, middle, from_above, from_below, new_rows),
    )
    columns = spread_rows(columns, LAT)
    grad_slab, new_nodes = call(
        finish, [shape_of((width, slab_rows), BF)] * 2, [], 6, "v", (columns,)
    )

    shard = (32, L)
    shards = (4,) + shard
    kept, *sent = call(
        functools.partial(sum_far, pieces),
        [shape_of(shards, F32)] + [shape_of(shards, BF)] * 3,
        [((edge_rows, L), F32), ((node_rows, L), F32), ((4,) + shards, F32)],
        8,
        "s" + "v" * 8,
        (near_scal, *edge_far, *node_far),
    )
    moved = [shift(sent[k - 1], "z", k) for k in range(1, 4)]
    kept, *sent = call(
        sum_z,
        [shape_of(shard, F32)] + [shape_of(shard, BF)] * 3,
        [(shards, F32)],
        4,
        "s" + "v" * 4,
        (near_scal, kept, *moved),
    )
    moved = [shift(sent[k - 1], XS, k) for k in range(1, 4)]
    reduced = call(
        sum_x, [shape_of((count, L), F32) for count in pieces], [], 4, "v" * 4, (kept, *moved)
    )
    return (new_nodes.T, new_edges, grad_slab.T, grad_edges) + tuple(reduced)


def solution(mesh):
    fine = Mesh(mesh.devices.reshape(4, 2, 2, 2, 4), ("y", "xl", "c", "xh", "z"))
    every = SLAB + LAT
    by_rows = P(every, None)
    split = P(SLAB, LAT)
    placed = (
        split,
        by_rows,
        P(None, every),
        P(None, every),
        P(SLAB),
        P(SLAB, None, None),
        by_rows,
        by_rows,
        by_rows,
        by_rows,
        P(),
        P(),
        split,
        by_rows,
    )

    return jax.shard_map(
        per_device,
        mesh=fine,
        in_specs=placed,
        out_specs=(split, by_rows, split, by_rows, by_rows, by_rows, by_rows, by_rows),
        check_vma=False,
    )
```

```python
import functools

import jax
import jax.numpy as jnp
from jax import lax
from jax.experimental import pallas as pl
from jax.experimental.pallas import tpu as pltpu
from jax.sharding import Mesh, PartitionSpec as P


L = 512
BLK = 128
HB = 2
EPSILON = 1e-05

SLAB = ("y", "xl", "c")
LAT = ("xh", "z")
XS = ("xl", "xh")
BF = jnp.bfloat16
F32 = jnp.float32
EDGE_MIB = 16
NODE_MIB = 14
BACK_MIB = 28


def shape_of(shape, dtype):
    return jax.ShapeDtypeStruct(shape, dtype)


def from_behind(value, steps):
    count = lax.axis_size(SLAB)
    first, last = (max(0, -steps), min(count, count - steps))
    return lax.ppermute(value, SLAB, [(source, source + steps) for source in range(first, last)])


def dot(left, right):
    return jnp.dot(left, right, preferred_element_type=F32)


def dot_rows(left, right):
    return lax.dot_general(left, right, (((0,), (0,)), ((), ())), preferred_element_type=F32)


def dot_transpose(left, right):
    return lax.dot_general(left, right, (((1,), (1,)), ((), ())), preferred_element_type=F32)


def one_hot_columns(offsets):
    cells = lax.broadcasted_iota(jnp.int32, (BLK, BLK), 0)
    return (cells == offsets).astype(F32)


def norm_parts(values):
    average = jnp.mean(values, axis=-1, keepdims=True)
    centred = values - average
    variance = jnp.mean(centred * centred, axis=-1, keepdims=True)
    inverse = lax.rsqrt(variance + EPSILON)
    return centred * inverse, inverse


def norm_back(upstream, normed, inverse, gain_vector):
    scaled = upstream * gain_vector
    return inverse * (
        scaled
        - jnp.mean(scaled, axis=-1, keepdims=True)
        - normed * jnp.mean(scaled * normed, axis=-1, keepdims=True)
    )


def split_three(value):
    high = value.astype(BF)
    rest = value - high.astype(F32)
    middle = rest.astype(BF)
    return high, middle, (rest - middle.astype(F32)).astype(BF)


def block_at(number):
    return pl.ds(pl.multiple_of(number * BLK, BLK), BLK)


def copies(pairs, sems):
    made = [pltpu.make_async_copy(src, dst, sems.at[i]) for i, (src, dst) in enumerate(pairs)]
    for one in made:
        one.start()
    return made


def wait_all(made):
    for one in made:
        one.wait()


def weight_pairs(core, y_index, shards, outs, counts):
    total = sum(counts)
    y_count = len(shards) // 2
    pairs = []
    for number, source in enumerate(shards):
        step = number % y_count
        parity = core if number < y_count else 1 - core
        y = lax.rem(y_index - step + y_count, y_count)
        per = source.shape[0] // total
        for x in range(per):
            slab = (y * per + x) * 2 + parity
            at = x * total
            for out, count in zip(outs, counts):
                start = pl.multiple_of(slab * count, 32)
                pairs.append((source.at[pl.ds(at, count), :], out.at[pl.ds(start, count), :]))
                at += count
    return pairs


def unpack_weights(core, y_index, shards, outs, counts):
    for source, target in weight_pairs(core, y_index, shards, outs, counts):
        target[...] = source[...]


def pack_grads(core, y_index, grads, keep, send, counts):
    total = sum(counts)
    y_count = keep.shape[0]
    per = keep.shape[1] // total
    for target, parity in ((keep, core), (send, 1 - core)):
        for step in range(y_count):
            y = lax.rem(y_index + step, y_count)
            for x in range(per):
                at = x * total
                for grad, count in zip(grads, counts):
                    start = pl.multiple_of(((y * per + x) * 2 + parity) * count, 32)
                    target[step, pl.ds(at, count), :] = grad[pl.ds(start, count), :].astype(BF)
                    at += count


def prepare(halo, turned, *refs):
    weights, (up, down, packed), held, sems = refs[:4], refs[4:7], refs[7:-1], refs[-1]
    pairs = list(zip(weights, held))
    for j in range(HB):
        part = pl.ds(j * BLK, BLK)
        pairs.append((turned.at[:, block_at(halo[0, 0, j])], up.at[:, part]))
        pairs.append((turned.at[:, block_at(halo[0, 1, j])], down.at[:, part]))
    wait_all(copies(pairs, sems))
    parts = [ref[...].astype(F32) for ref in held]
    used = sum(part.shape[0] for part in parts)
    parts.append(jnp.zeros((packed.shape[0] - used, L), F32))
    packed[...] = jnp.concatenate(parts, axis=0).astype(BF)


def fill_message(lower, turned, upper, cot, out, table, held, in_sems, sems):
    rows, halo_rows = turned.shape[1], lower.shape[1]
    loads = copies([(turned, table.at[:, pl.ds(halo_rows, rows)]), (cot, held)], in_sems)
    table[:, pl.ds(0, halo_rows)] = lower[...]
    table[:, pl.ds(halo_rows + rows, halo_rows)] = upper[...]
    wait_all(loads)
    pairs = []
    for l in range(out.shape[0]):
        pairs.append((table, out.at[l, :, pl.ds(0, table.shape[1])]))
        part = out.at[l, :, pl.ds(table.shape[1], BLK)]
        pairs.append((held.at[:, pl.ds(l * BLK, BLK)], part))
    wait_all(copies(pairs, sems))


def assemble(pieces, scal, *refs):
    blocks, (edge_part, node_part, held, edge_rows, node_rows) = refs[:4], refs[4:]
    z_index, x_index = scal[0], scal[1]
    for k, block in enumerate(blocks):
        held[k] = block[...]
    outs = (edge_rows, edge_rows, node_rows, node_rows)
    bases = []
    for number, count in enumerate(pieces):
        bases.append(0 if number % 2 == 0 else bases[-1] + 8 * pieces[number - 1])
    sizes = (8 * (pieces[0] + pieces[1]), 8 * (pieces[2] + pieces[3]))
    for x in range(4):
        x_step = lax.rem(x_index - x + 4, 4)
        for z in range(4):
            z_step = lax.rem(z_index - z + 4, 4)
            shard = held[z_step, pl.ds(pl.multiple_of(x_step * 32, 32), 32), :].astype(F32)
            row, lat = 0, (x % 2) * 4 + z
            for number, count in enumerate(pieces):
                base = (x // 2) * sizes[number // 2] + bases[number] + lat * count
                outs[number][pl.ds(base, count), :] = shard[row : row + count]
                row += count
    edge_part[...] = edge_rows[...].astype(BF)
    node_part[...] = node_rows[...].astype(BF)


def sum_far(pieces, scal, edge_own, e1, e2, e3, node_own, n1, n2, n3, keep, s1, s2, s3, er, nr, sent):
    z_index = scal[0]
    er[...] = sum((ref[...].astype(F32) for ref in (e1, e2, e3)), edge_own[...].astype(F32))
    nr[...] = sum((ref[...].astype(F32) for ref in (n1, n2, n3)), node_own[...].astype(F32))
    ins = (er, er, nr, nr)
    bases = []
    for number, count in enumerate(pieces):
        bases.append(0 if number % 2 == 0 else bases[-1] + 8 * pieces[number - 1])
    sizes = (8 * (pieces[0] + pieces[1]), 8 * (pieces[2] + pieces[3]))
    spare = 32 - sum(pieces)
    for x in range(4):
        for z in range(4):
            lat = (x % 2) * 4 + z
            parts = []
            for number, count in enumerate(pieces):
                base = (x // 2) * sizes[number // 2] + bases[number] + lat * count
                parts.append(ins[number][pl.ds(base, count), :])
            parts.append(jnp.zeros((spare, L), F32))
            sent[z, x] = jnp.concatenate(parts, axis=0)
    keep[...] = sent[z_index]
    for step, out in ((1, s1), (2, s2), (3, s3)):
        out[...] = sent[lax.rem(z_index + step, 4)].astype(BF)


def sum_z(scal, own, r1, r2, r3, keep, s1, s2, s3, held):
    x_index = scal[1]
    held[...] = own[...] + (r1[...].astype(F32) + r2[...].astype(F32) + r3[...].astype(F32))
    keep[...] = held[x_index]
    for step, out in ((1, s1), (2, s2), (3, s3)):
        out[...] = held[lax.rem(x_index + step, 4)].astype(BF)


def sum_x(own, r1, r2, r3, *outs):
    total = own[...] + (r1[...].astype(F32) + r2[...].astype(F32) + r3[...].astype(F32))
    row = 0
    for out in outs:
        count = out.shape[0]
        out[...] = total[row : row + count]
        row += count


def edge_forward(scal, ext, edges, offsets, *refs):
    shards, refs = refs[:8], refs[8:]
    gain, joined_out, first_out, normed_out, inverse_out, new_edges_out, partial_out = refs[:7]
    own_out, up_out, refs = refs[7], refs[8], refs[9:]
    joined, first, normed, inverse, new_edges, partial, w_in, w_out, second, sems, out_sems = refs
    tiles = edges.shape[0] // BLK
    lat_index, core, y_index, count = (scal[2 * tiles + i] for i in range(4))
    slabs = w_in.shape[0] // 3 // 32
    counts = (3 * L // slabs, L // slabs)
    stores = []

    def store(source, target):
        copy = pltpu.make_async_copy(source, target, out_sems.at[len(stores)])
        copy.start()
        stores.append(copy)

    store(ext.at[:, block_at(HB + lat_index)], own_out)
    store(ext.at[:, pl.ds(ext.shape[1] - BLK, BLK)], up_out)
    loads = copies([(edges, joined.at[:, pl.ds(0, L)])], sems)
    for t in range(tiles):
        rows = pl.ds(t * BLK, BLK)
        to_src = one_hot_columns(offsets[1, pl.ds(t, 1), :]).T.astype(BF)
        to_dst = one_hot_columns(offsets[0, pl.ds(t, 1), :]).T.astype(BF)
        src, dst = block_at(scal[tiles + t]), block_at(scal[t] + HB)
        joined[rows, pl.ds(L, L)] = dot_transpose(to_src, ext[:, src]).astype(BF)
        joined[rows, pl.ds(2 * L, L)] = dot_transpose(to_dst, ext[:, dst]).astype(BF)
    wait_all(loads)
    store(joined, joined_out)
    unpack_weights(core, y_index, shards, (w_in, w_out), counts)
    for n in range(2):
        columns = pl.ds(n * 256, 256)
        first[:, columns] = jnp.maximum(dot(joined[...], w_in[:, columns]), 0.0).astype(BF)
    store(first, first_out)
    for n in range(2):
        columns = pl.ds(n * 256, 256)
        second[:, columns] = dot(first[...], w_out[:, columns])
    partial[...] = jnp.zeros_like(partial)
    for t in range(tiles):
        rows = pl.ds(t * BLK, BLK)
        live = (lat_index * tiles + t < count).astype(F32)
        values, inv = norm_parts(second[rows, :])
        normed[rows, :] = values
        inverse[rows, :] = jnp.broadcast_to(inv, (BLK, BLK))
        message = values * gain[...] * live
        new_edges[rows, :] = (joined[rows, pl.ds(0, L)].astype(F32) + message).astype(BF)
        second[rows, :] = message
    store(normed, normed_out)
    store(inverse, inverse_out)
    store(new_edges, new_edges_out)
    for t in range(tiles):
        rows = pl.ds(t * BLK, BLK)
        into = one_hot_columns(offsets[0, pl.ds(t, 1), :]).astype(BF)
        high, middle, low = split_three(second[rows, :])
        block = scal[t]
        partial[block] = partial[block] + (dot(into, low) + dot(into, middle) + dot(into, high))
    store(partial, partial_out)
    wait_all(stores)


def node_step(scal, spread, own_hbm, up_hbm, *refs):
    shards, refs = refs[:8], refs[8:]
    gain, out, rows_out, direct_out, joined_out, first_out, d_second_out, d_first_out = refs[:8]
    own_turned, up_turned, w_in, w_out, joined, first, d_second, d_first = refs[8:16]
    d_direct, new_rows, sems, out_sems = refs[16:]
    core, y_index = scal[1], scal[2]
    slabs = w_in.shape[0] // 2 // 32
    counts = (2 * L // slabs, L // slabs)
    pairs = weight_pairs(core, y_index, shards, (w_in, w_out), counts)
    loads = copies([(own_hbm, own_turned), (up_hbm, up_turned)] + pairs[-4:], sems)
    for source, target in pairs[:-4]:
        target[...] = source[...]
    wait_all(loads)
    own = own_turned[...].astype(F32).T
    upstream = up_turned[...].astype(F32).T
    joined[:, pl.ds(0, L)] = own.astype(BF)
    total = spread[0]
    for l in range(1, spread.shape[0]):
        total = total + spread[l]
    joined[:, pl.ds(L, L)] = total.astype(BF)
    stores = copies([(joined, joined_out)], out_sems)
    first[...] = jnp.maximum(dot(joined[...], w_in[...]), 0.0).astype(BF)
    stores += copies([(first, first_out)], out_sems.at[pl.ds(1, 1)])
    normed, inverse = norm_parts(dot(first[...], w_out[...]))
    d_second[...] = norm_back(upstream, normed, inverse, gain[...]).astype(BF)
    back = dot_transpose(d_second[...], w_out[...])
    d_first[...] = jnp.where(first[...].astype(F32) > 0, back, 0.0).astype(BF)
    pairs = [(d_second, d_second_out), (d_first, d_first_out)]
    stores += copies(pairs, out_sems.at[pl.ds(2, 2)])
    d_direct[...] = dot_transpose(w_in[pl.ds(0, L), :], d_first[...])
    new_rows[...] = (own + normed * gain[...]).T.astype(BF)
    pairs = [(d_direct, direct_out), (new_rows, rows_out)]
    stores += copies(pairs, out_sems.at[pl.ds(4, 2)])
    d_agg = dot_transpose(w_in[pl.ds(L, L), :], d_first[...]).astype(BF)
    for l in range(out.shape[0]):
        out[l] = d_agg
    wait_all(stores)


def node_grads(scal, *refs):
    saved, (keep, send), refs = refs[:4], refs[4:6], refs[6:]
    held, (g_in, g_out, sems) = refs[:4], refs[4:]
    wait_all(copies(zip(saved, held), sems))
    joined, first, d_second, d_first = held
    g_out[...] = dot_rows(first[...], d_second[...])
    g_in[...] = dot_rows(joined[...], d_first[...])
    slabs = g_in.shape[0] // 2 // 32
    pack_grads(scal[1], scal[2], (g_in, g_out), keep, send, (2 * L // slabs, L // slabs))


def edge_backward(scal, d_agg, cot, offsets, gain, *refs):
    saved, w_out_shards, refs = refs[:4], refs[4:12], refs[12:]
    d_first, d_first_out, keep, send = refs[:4]
    joined, first, normed, inverse, w_in, w_out, d_second, g_in, g_out, sems, out_sems = refs[4:]
    tiles = cot.shape[0] // BLK
    lat_index, core, y_index, count = (scal[2 * tiles + i] for i in range(4))
    slabs = w_in.shape[0] // 3 // 32
    counts = (3 * L // slabs, L // slabs)
    normed_in, inverse_in, first_in, joined_in = saved
    pairs = [(normed_in, normed), (inverse_in, inverse)]
    pairs += weight_pairs(core, y_index, w_out_shards, (w_in, w_out), counts)[1::2]
    pairs += [(first_in, first), (joined_in, joined)]
    loads = copies(pairs, sems)
    wait_all(loads[:2])
    for t in range(tiles):
        rows = pl.ds(t * BLK, BLK)
        live = (lat_index * tiles + t < count).astype(F32)
        to_dst = one_hot_columns(offsets[0, pl.ds(t, 1), :]).T.astype(BF)
        picked = dot_transpose(to_dst, d_agg[scal[t]])
        d_message = (cot[rows, :].astype(F32) + picked) * live
        back = norm_back(d_message, normed[rows, :], inverse[rows, pl.ds(0, 1)], gain[...])
        d_second[rows, :] = back.astype(BF)
    wait_all(loads[2:])
    for n in range(2):
        part = pl.ds(n * 256, 256)
        back = dot_transpose(d_second[...], w_out[part, :])
        d_first[:, part] = jnp.where(first[:, part].astype(F32) > 0, back, 0.0).astype(BF)
    store = copies([(d_first, d_first_out)], out_sems)
    for n in range(2):
        part = pl.ds(n * 256, 256)
        g_out[part, :] = dot_rows(first[:, part], d_second[...])
    for n in range(6):
        part = pl.ds(n * 256, 256)
        g_in[part, :] = dot_rows(joined[:, part], d_first[...])
    pack_grads(core, y_index, (g_in, g_out), keep, send, counts)
    wait_all(store)


def edge_inputs(scal, d_first, offsets, direct_in, *refs):
    shards, refs = refs[:8], refs[8:]
    middle_out, lower, upper, d_direct, w_in, w_out, d_ext, d_turned, sems = refs
    tiles = d_first.shape[0] // BLK
    lat_index, core, y_index = (scal[2 * tiles + i] for i in range(3))
    slabs = w_in.shape[0] // 3 // 32
    counts = (3 * L // slabs, L // slabs)
    pairs = weight_pairs(core, y_index, shards, (w_in, w_out), counts)[::2]
    pairs += [(direct_in, d_direct)]
    loads = copies(pairs, sems)
    d_ext[...] = jnp.zeros_like(d_ext)
    wait_all(loads)
    for n in range(4):
        d_turned[pl.ds(n * 256, 256), :] = dot_transpose(
            w_in[pl.ds(L + n * 256, 256), :], d_first[...]
        )
    for t in range(tiles):
        rows = pl.ds(t * BLK, BLK)
        for row, place, at in ((1, scal[tiles + t], 0), (0, scal[t] + HB, L)):
            into = one_hot_columns(offsets[row, pl.ds(t, 1), :]).T.astype(BF)
            value = d_turned[pl.ds(at, L), rows]
            high = value.astype(BF)
            low = (value - high.astype(F32)).astype(BF)
            d_ext[place] = d_ext[place] + (dot(low, into) + dot(high, into))
    d_ext[HB + lat_index] = d_ext[HB + lat_index] + d_direct[...]
    blocks = middle_out.shape[0]
    for j in range(HB):
        lower[:, pl.ds(j * BLK, BLK)] = d_ext[j].astype(BF)
        upper[:, pl.ds(j * BLK, BLK)] = d_ext[HB + blocks + j].astype(BF)
    middle_out[...] = d_ext[pl.ds(HB, blocks)]


def edge_grads(scal, d_first_in, cot_in, *refs):
    shards, refs = refs[:8], refs[8:]
    grad_out, grad_edges, cot, d_first, w_in, w_out, sems, out_sems = refs
    tiles = cot.shape[0] // BLK
    core, y_index = scal[2 * tiles + 1], scal[2 * tiles + 2]
    slabs = w_in.shape[0] // 3 // 32
    counts = (3 * L // slabs, L // slabs)
    pairs = weight_pairs(core, y_index, shards, (w_in, w_out), counts)[::2]
    wait_all(copies(pairs + [(cot_in, cot), (d_first_in, d_first)], sems))
    for n in range(2):
        part = pl.ds(n * 256, 256)
        back = dot_transpose(d_first[...], w_in[part, :])
        grad_edges[:, part] = (cot[:, part].astype(F32) + back).astype(BF)
    wait_all(copies([(grad_edges, grad_out)], out_sems))


def add_halo(halo, middle, above, below, new_rows, columns, held):
    held[...] = middle[...]
    for j in range(HB):
        for place, value in ((halo[0, 0, j], above), (halo[0, 1, j], below)):
            held[place] = held[place] + value[:, pl.ds(j * BLK, BLK)].astype(F32)
    width = columns.shape[1]
    for block in range(held.shape[0]):
        for l in range(columns.shape[0]):
            columns[l, :, pl.ds(block * BLK, BLK)] = held[
                block, pl.ds(l * width, width), :
            ].astype(BF)
    last = pl.ds(held.shape[0] * BLK, BLK)
    for l in range(columns.shape[0]):
        columns[l, :, last] = new_rows[pl.ds(l * width, width), :]


def finish(arrived, out, new_nodes):
    cells = pl.ds(0, out.shape[1])
    total = arrived[0, :, cells].astype(F32)
    for l in range(1, arrived.shape[0]):
        total = total + arrived[l, :, cells].astype(F32)
    out[...] = total.astype(BF)
    for l in range(arrived.shape[0]):
        new_nodes[:, pl.ds(l * BLK, BLK)] = arrived[l, :, pl.ds(out.shape[1], BLK)]


def call(kernel, out_shape, scratch, mib, spaces, operands, flops=0, out_spaces="", sems=()):
    moved = sum(x.size * x.dtype.itemsize for x in operands)
    moved += sum(x.size * x.dtype.itemsize for x in out_shape)
    named = {"s": pltpu.SMEM, "v": pltpu.VMEM, "h": pltpu.HBM}
    out_spaces = out_spaces or "v" * len(out_shape)
    operands = [
        pltpu.with_memory_space_constraint(x, pltpu.HBM) if space == "h" else x
        for x, space in zip(operands, spaces)
    ]
    placed = [
        pltpu.HBM(x.shape, x.dtype) if space == "h" else x
        for x, space in zip(out_shape, out_spaces)
    ]
    return pl.pallas_call(
        kernel,
        out_shape=placed,
        in_specs=[pl.BlockSpec(memory_space=named[space]) for space in spaces],
        out_specs=[pl.BlockSpec(memory_space=named[space]) for space in out_spaces],
        scratch_shapes=[pltpu.VMEM(shape, dtype) for shape, dtype in scratch]
        + [pltpu.SemaphoreType.DMA((count,)) for count in sems],
        cost_estimate=pl.CostEstimate(flops=flops, bytes_accessed=moved, transcendentals=0),
        compiler_params=pltpu.CompilerParams(vmem_limit_bytes=mib << 20),
    )(*operands)


def run_edge_forward(scal, ext, edges, offsets, shards, gain, lat_size):
    rows = edges.shape[0]
    outs = [
        shape_of((rows, 3 * L), BF),
        shape_of((rows, L), BF),
        shape_of((rows, L), F32),
        shape_of((rows, BLK), F32),
        shape_of((rows, L), BF),
        shape_of((lat_size, BLK, L), F32),
    ]
    held = [(out.shape, out.dtype) for out in outs]
    outs += [shape_of((L, BLK), BF)] * 2
    return call(
        edge_forward,
        outs,
        held + [((3 * L, L), BF), ((L, L), BF), ((rows, L), F32)],
        EDGE_MIB,
        "svhv" + "v" * len(shards) + "v",
        (scal, ext, edges, offsets, *shards, gain),
        flops=2 * rows * 4 * L * L,
        out_spaces="h" * len(outs),
        sems=(1, len(outs)),
    )


def run_node_step(scal, spread, own, up, shards, gain):
    lat_size = spread.shape[0]
    rows = [((BLK, 2 * L), BF), ((BLK, L), BF), ((BLK, L), BF), ((BLK, L), BF)]
    return call(
        node_step,
        [shape_of((lat_size, L, BLK), BF), shape_of((L, BLK), BF), shape_of((L, BLK), F32)]
        + [shape_of(*row) for row in rows],
        [((L, BLK), BF), ((L, BLK), BF), ((2 * L, L), BF), ((L, L), BF)]
        + rows
        + [((L, BLK), F32), ((L, BLK), BF)],
        NODE_MIB,
        "svhh" + "v" * (len(shards) - 1) + "hv",
        (scal, spread, own, up, *shards, gain),
        flops=2 * BLK * 6 * L * L,
        out_spaces="vhhhhhh",
        sems=(2 + 4, 6),
    )


def run_node_grads(scal, saved, shard, y_count):
    return call(
        node_grads,
        [shape_of((y_count,) + shard.shape, BF)] * 2,
        [(one.shape, BF) for one in saved] + [((2 * L, L), F32), ((L, L), F32)],
        NODE_MIB,
        "shhhh",
        (scal, *saved),
        flops=2 * BLK * 3 * L * L,
        sems=(4,),
    )


def run_edge_backward(scal, d_agg, cot, offsets, gain, saved, shards):
    rows = cot.shape[0]
    chunk = (len(shards) // 2,) + shards[0].shape
    normed, inverse, first, joined = saved
    return call(
        edge_backward,
        [shape_of((rows, L), BF)] * 2 + [shape_of(chunk, BF)] * 2,
        [
            (joined.shape, BF),
            (first.shape, BF),
            (normed.shape, F32),
            (inverse.shape, F32),
            ((3 * L, L), BF),
            ((L, L), BF),
            ((rows, L), BF),
            ((3 * L, L), F32),
            ((L, L), F32),
        ],
        BACK_MIB,
        "svvvv" + "h" * (len(saved) + len(shards)),
        (scal, d_agg, cot, offsets, gain, *saved, *shards),
        flops=2 * rows * 5 * L * L,
        out_spaces="vhvv",
        sems=(4 + 2 * len(shards), 1),
    )


def run_edge_inputs(scal, d_first, offsets, d_direct, shards, lat_size):
    rows = d_first.shape[0]
    return call(
        edge_inputs,
        [
            shape_of((lat_size, L, BLK), F32),
            shape_of((L, HB * BLK), BF),
            shape_of((L, HB * BLK), BF),
        ],
        [
            (d_direct.shape, F32),
            ((3 * L, L), BF),
            ((L, L), BF),
            ((lat_size + 2 * HB, L, BLK), F32),
            ((2 * L, rows), F32),
        ],
        EDGE_MIB,
        "svvh" + "h" * len(shards),
        (scal, d_first, offsets, d_direct, *shards),
        flops=2 * rows * 2 * L * L,
        sems=(1 + 2 * len(shards),),
    )


def run_edge_grads(scal, d_first, cot, shards):
    rows = cot.shape[0]
    return call(
        edge_grads,
        [shape_of((rows, L), BF)],
        [((rows, L), BF)] * 3 + [((3 * L, L), BF), ((L, L), BF)],
        EDGE_MIB,
        "shh" + "h" * len(shards),
        (scal, d_first, cot, *shards),
        flops=2 * rows * L * L,
        out_spaces="h",
        sems=(2 + 2 * len(shards), 1),
    )


def swap_cores(value):
    return lax.ppermute(value, "c", [(0, 1), (1, 0)])


def shift(value, axes, step):
    count = lax.axis_size(axes)
    return lax.ppermute(value, axes, [(i, (i + step) % count) for i in range(count)])


def shifts(value, axes):
    return [value] + [shift(value, axes, k) for k in range(1, lax.axis_size(axes))]


def spread_rows(value, axes):
    return lax.all_to_all(value, axes, 0, 0)


def gather_far(value):
    mine = shifts(value, "y")
    return mine + [swap_cores(one) for one in mine]


def reduce_far(keep, send):
    arrived = swap_cores(send)
    both = [(keep[k].astype(F32) + arrived[k].astype(F32)).astype(BF) for k in range(keep.shape[0])]
    return [both[0]] + [shift(both[k], "y", k) for k in range(1, keep.shape[0])]


def per_device(
    nodes,
    edges,
    edge_tiles,
    edge_offsets,
    tile_counts,
    halo_blocks,
    w_edge_in,
    w_edge_out,
    w_node_in,
    w_node_out,
    edge_gain,
    node_gain,
    node_cotangent,
    edge_cotangent,
):
    lat_size = lax.axis_size(LAT)
    place = [lax.axis_index(LAT), lax.axis_index("c"), lax.axis_index("y")]
    slab_rows, width = nodes.shape
    own_rows = slab_rows // lat_size
    halo_rows = HB * BLK
    ext_rows = slab_rows + 2 * halo_rows
    weights = (w_edge_in, w_edge_out, w_node_in, w_node_out)
    pieces = tuple(weight.shape[0] for weight in weights)
    edge_rows = 2 * lat_size * (pieces[0] + pieces[1])
    node_rows = 2 * lat_size * (pieces[2] + pieces[3])

    near_scal = jnp.stack([lax.axis_index("z"), lax.axis_index(XS)]).astype(jnp.int32)
    node_scal = jnp.stack(place).astype(jnp.int32)
    scal = jnp.concatenate([edge_tiles.reshape(-1), node_scal, tile_counts])
    halo = halo_blocks
    offsets = edge_offsets.reshape(2, -1, BLK)
    edge_gain_row = edge_gain.reshape(1, L)
    node_gain_row = node_gain.reshape(1, L)

    turned = nodes.T
    up, down, packed = call(
        prepare,
        [
            shape_of((width, halo_rows), BF),
            shape_of((width, halo_rows), BF),
            shape_of((32, L), BF),
        ],
        [(weight.shape, BF) for weight in weights],
        4,
        "shhhhh",
        (halo, turned, *weights),
        sems=(4 + 2 * HB,),
    )
    from_lower = from_behind(up, 1)
    from_upper = from_behind(down, -1)

    (message_out,) = call(
        fill_message,
        [shape_of((lat_size, width, ext_rows + own_rows), BF)],
        [((width, ext_rows), BF), ((width, slab_rows), BF)],
        4,
        "vhvh",
        (from_lower, turned, from_upper, node_cotangent.T),
        out_spaces="h",
        sems=(2, 2 * lat_size),
    )
    by_x = jnp.concatenate(shifts(packed, XS), axis=0)
    near = shifts(by_x, "z")
    edge_part, node_part = call(
        functools.partial(assemble, pieces),
        [shape_of((edge_rows, L), BF), shape_of((node_rows, L), BF)],
        [((4, 128, L), BF), ((edge_rows, L), F32), ((node_rows, L), F32)],
        6,
        "svvvv",
        (near_scal, *near),
    )

    edge_shards = gather_far(edge_part)
    ext = spread_rows(message_out, LAT).reshape(L, ext_rows + own_rows)

    joined, first, normed, inverse, new_edges, partial, own, node_up = run_edge_forward(
        scal, ext, edges, offsets, edge_shards, edge_gain_row, lat_size
    )
    node_shards = gather_far(node_part)
    spread = spread_rows(partial, LAT)
    second_out, new_rows, d_direct, *node_saved = run_node_step(
        node_scal, spread, own, node_up, node_shards, node_gain_row
    )
    node_keep, node_send = run_node_grads(
        node_scal, node_saved, node_part, lax.axis_size("y")
    )
    second_in = spread_rows(second_out, LAT)
    node_far = reduce_far(node_keep, node_send)

    d_first, d_first_kept, edge_keep, edge_send = run_edge_backward(
        scal, second_in, edge_cotangent, offsets, edge_gain_row,
        (normed, inverse, first, joined), edge_shards,
    )
    middle, lower, upper = run_edge_inputs(
        scal, d_first, offsets, d_direct, edge_shards, lat_size
    )
    from_above = from_behind(lower, -1)
    from_below = from_behind(upper, 1)
    (grad_edges,) = run_edge_grads(scal, d_first_kept, edge_cotangent, edge_shards)
    edge_far = reduce_far(edge_keep, edge_send)
    (columns,) = call(
        add_halo,
        [shape_of((lat_size, width, slab_rows + own_rows), BF)],
        [((lat_size, L, BLK), F32)],
        8,
        "svvvv",
        (halo, middle, from_above, from_below, new_rows),
    )
    columns = spread_rows(columns, LAT)
    grad_slab, new_nodes = call(
        finish, [shape_of((width, slab_rows), BF)] * 2, [], 6, "v", (columns,)
    )

    shard = (32, L)
    shards = (4,) + shard
    kept, *sent = call(
        functools.partial(sum_far, pieces),
        [shape_of(shards, F32)] + [shape_of(shards, BF)] * 3,
        [((edge_rows, L), F32), ((node_rows, L), F32), ((4,) + shards, F32)],
        8,
        "s" + "v" * 8,
        (near_scal, *edge_far, *node_far),
    )
    moved = [shift(sent[k - 1], "z", k) for k in range(1, 4)]
    kept, *sent = call(
        sum_z,
        [shape_of(shard, F32)] + [shape_of(shard, BF)] * 3,
        [(shards, F32)],
        4,
        "s" + "v" * 4,
        (near_scal, kept, *moved),
    )
    moved = [shift(sent[k - 1], XS, k) for k in range(1, 4)]
    reduced = call(
        sum_x, [shape_of((count, L), F32) for count in pieces], [], 4, "v" * 4, (kept, *moved)
    )
    return (new_nodes.T, new_edges, grad_slab.T, grad_edges) + tuple(reduced)


def solution(mesh):
    fine = Mesh(mesh.devices.reshape(4, 2, 2, 2, 4), ("y", "xl", "c", "xh", "z"))
    every = SLAB + LAT
    by_rows = P(every, None)
    split = P(SLAB, LAT)
    placed = (
        split,
        by_rows,
        P(None, every),
        P(None, every),
        P(SLAB),
        P(SLAB, None, None),
        by_rows,
        by_rows,
        by_rows,
        by_rows,
        P(),
        P(),
        split,
        by_rows,
    )

    return jax.shard_map(
        per_device,
        mesh=fine,
        in_specs=placed,
        out_specs=(split, by_rows, split, by_rows, by_rows, by_rows, by_rows, by_rows),
        check_vma=False,
    )
```
